256 devices in a mesh: gx: 8 (over x, core), gy: 32 (over y, z).
Axes of the slice: x: 4, y: 4, z: 8, core: 2. Of those that a mesh axis runs over, the one named last changes fastest.
Arguments:
- rock_type: int32 [128, 1024, 256], P('gx', 'gy'), may hold values from 0 to 7
- perm_table: float32 [8], replicated, may hold values from 0.1 to 10
- poro_table: float32 [8], replicated, may hold values from 0.1 to 0.3
- saturation: float32 [128, 1024, 256], P('gx', 'gy'), may hold values from 0 to 1
- pressure_old: float32 [128, 1024, 256], P('gx', 'gy'), may hold values from -10 to 10
- factor_inverse: float32 [8, 64, 256, 256], P('gx', 'gy'), may hold values from -2 to 2, as said below
- inject_cells: int32 [4, 128, 2], replicated, may hold values from 0 to 131071, as said below
- inject_index: float32 [4, 128], replicated, may hold values from 1 to 8
- inject_rate: float32 [4], replicated, may hold values from 200 to 1000
- produce_cells: int32 [8, 128, 2], replicated, may hold values from 0 to 131071, as said below
- produce_index: float32 [8, 128], replicated, may hold values from 1 to 8
- produce_pressure: float32 [8], replicated, may hold values from -3 to -1
Outputs:
- saturation_new: float32 [128, 1024, 256], P('gx', 'gy')
- pressure: float32 [128, 1024, 256], P('gx', 'gy')
The draws below stay inside these ranges and needn't reach their ends.
Inputs may be any that keep to these rules, and one draw needn't show every extreme that they name: `inject_cells`: the 128 perforations of a well lie in one layer and one row of columns: perforation k at second index (start + k) modulo 1024 for a start per well. `produce_cells`: laid out as for injectors. `factor_inverse`: each block's matrix is lower triangular with a positive diagonal.
All inputs are finite; a program needn't handle non-finite values.
Results may differ from the reference program's by a relative error of at most 0.0003.
Values sent between devices are 32-bit elements; how exact they have to be, the bound alone decides.
A program may use at most 64 MiB of HBM per device.

```python
import math
import jax
import jax.numpy as jnp
from jax import lax

CY = 32
NZ = 256
BLOCK = 16
ROCKS = 8
INJECTORS = 4
PRODUCERS = 8
PERFS = 128
ITERS = 3
NX = 128
NY = 1024


def draw_saturation(key, part):
    grid_shape = (NX, NY, NZ)
    half_cols = CY // 2
    layer_group = 8
    level_shape = (NX, NY // half_cols, NZ // layer_group)
    level_key = jax.random.fold_in(key, 31)
    base_key = jax.random.fold_in(key, 37)
    levels = jax.random.uniform(level_key, level_shape, jnp.float32, -2.0, 2.0)
    base = jax.random.uniform(base_key, grid_shape, jnp.float32, 0.0, 1.0)
    exponent = jnp.exp(levels * math.log(2.0))
    exponent = jnp.repeat(jnp.repeat(exponent, half_cols, axis=1), layer_group, axis=2)
    return jnp.clip(jnp.power(base, exponent), 0.0, 1.0)


def draw_pressure_old(key, part):
    grid_shape = (NX, NY, NZ)
    row_share = lax.broadcasted_iota(jnp.float32, grid_shape, 0) / NX
    col_share = lax.broadcasted_iota(jnp.float32, grid_shape, 1) / NY
    amplitude = (1.0 + 2.0 * row_share) * (1.0 + col_share) / 3.0
    noise = jnp.clip(jax.random.normal(key, grid_shape, jnp.float32), -5.0, 5.0)
    return noise * amplitude


def draw_factor_inverse(key, part):
    grid_shape = (NX // BLOCK, NY // BLOCK, NZ, NZ)
    row_pos = lax.broadcasted_iota(jnp.int32, grid_shape, 2)
    col_pos = lax.broadcasted_iota(jnp.int32, grid_shape, 3)
    below = jnp.where(col_pos < row_pos, 1.0, 0.0)
    on_diagonal = jnp.where(col_pos == row_pos, 1.0, 0.0)
    first_key = jax.random.fold_in(key, 5)
    second_key = jax.random.fold_in(key, 7)
    spread_scale = 0.7 / math.sqrt(NZ)
    off_part = jnp.clip(jax.random.normal(first_key, grid_shape, jnp.float32), -4.0, 4.0) * spread_scale
    diag_part = jnp.exp(jax.random.uniform(second_key, grid_shape, jnp.float32, 0.0, math.log(2.0)))
    return below * off_part + on_diagonal * diag_part


def well_path(key, well_count):
    row_start = jax.random.randint(jax.random.fold_in(key, 1), (well_count, 1), 0, NX)
    col_start = jax.random.randint(jax.random.fold_in(key, 2), (well_count, 1), 0, NY)
    layer_pick = jax.random.randint(jax.random.fold_in(key, 3), (well_count, 1), 0, NZ)
    well_pos = lax.broadcasted_iota(jnp.int32, (well_count, 1), 0)
    row_start = jnp.where(well_pos == 0, NX - 1, jnp.where(well_pos == 1, 0, row_start))
    col_start = jnp.where(well_pos == 0, NY - PERFS, jnp.where(well_pos == 1, 0, col_start))
    offsets = lax.broadcasted_iota(jnp.int32, (well_count, PERFS), 1)
    column = row_start * NY + (col_start + offsets) % NY
    layer_all = jnp.broadcast_to(layer_pick, (well_count, PERFS))
    return jnp.stack([column, layer_all], -1).astype(jnp.int32)


def draw_inject_cells(key, part):
    return well_path(jax.random.fold_in(key, 11), INJECTORS)


def draw_produce_cells(key, part):
    return well_path(jax.random.fold_in(key, 23), PRODUCERS)


def set_ends(entries, key, low, largest):
    longest = entries.shape.index(max(entries.shape))
    spots = []
    for shift in (0, 1):
        where = [jax.random.randint(jax.random.fold_in(key, axis), (), 0, length) for axis, length in enumerate(entries.shape)]
        where[longest] = (where[longest] + shift) % entries.shape[longest]
        spots.append(tuple(where))
    return entries.at[spots[0]].set(low).at[spots[1]].set(largest)


def setup_inputs(seed: int = 0) -> dict:
    key_list = jax.random.split(jax.random.key(seed), 13)
    return {
        "rock_type": set_ends(jax.random.randint(key_list[0], (NX, NY, NZ), 0, ROCKS), jax.random.fold_in(key_list[0], 1), 0, ROCKS - 1).astype(jnp.int32),
        "perm_table": jnp.clip(jnp.exp(jax.random.uniform(key_list[1], (ROCKS,), jnp.float32, math.log(0.1), math.log(10.0))), 0.1, 10.0),
        "poro_table": jnp.clip(jnp.exp(jax.random.uniform(key_list[2], (ROCKS,), jnp.float32, math.log(0.1), math.log(0.3))), 0.1, 0.3),
        "saturation": draw_saturation(jax.random.fold_in(key_list[12], 71), 0),
        "pressure_old": draw_pressure_old(jax.random.fold_in(key_list[12], 71), 0),
        "factor_inverse": draw_factor_inverse(jax.random.fold_in(key_list[12], 71), 0),
        "inject_cells": draw_inject_cells(jax.random.fold_in(key_list[12], 71), 0),
        "inject_index": jnp.clip(jnp.exp(jax.random.uniform(key_list[7], (INJECTORS, PERFS), jnp.float32, math.log(1.0), math.log(8.0))), 1.0, 8.0),
        "inject_rate": jnp.clip(jnp.exp(jax.random.uniform(key_list[8], (INJECTORS,), jnp.float32, math.log(200.0), math.log(1000.0))), 200.0, 1000.0),
        "produce_cells": draw_produce_cells(jax.random.fold_in(key_list[12], 71), 0),
        "produce_index": jnp.clip(jnp.exp(jax.random.uniform(key_list[10], (PRODUCERS, PERFS), jnp.float32, math.log(1.0), math.log(8.0))), 1.0, 8.0),
        "produce_pressure": jnp.clip(jax.random.uniform(key_list[11], (PRODUCERS,), jnp.float32, -3.0, -1.0), -3.0, -1.0),
    }


water_viscosity = 0.5
oil_viscosity = 1.0
time_step = 0.002
compress = 1.0
vertical_ratio = 0.1


def total_mobility(saturation):
    return saturation * saturation / water_viscosity + (1.0 - saturation) * (1.0 - saturation) / oil_viscosity


def mobilities(saturation):
    water_part = saturation * saturation / water_viscosity
    total_part = water_part + (1.0 - saturation) * (1.0 - saturation) / oil_viscosity
    return total_part, water_part / total_part


def harmonic(former, latter):
    summed = former + latter
    safe_sum = jnp.where(summed > 0.0, summed, 1.0)
    return 2.0 * former * latter / safe_sum


def cell_index(cells):
    return (cells[..., 0] * NZ + cells[..., 1]).astype(jnp.int32)


def spread_all(slot_index, values, grid_shape):
    flat_field = jnp.zeros((grid_shape[0] * grid_shape[1] * grid_shape[2],), jnp.float32)
    flat_field = flat_field.at[slot_index.reshape(-1)].add(values.reshape(-1))
    return flat_field.reshape(grid_shape)


def layer_difference(flux_values):
    zero_layer = jnp.zeros_like(flux_values[:, :, :1])
    return jnp.concatenate([flux_values, zero_layer], 2) - jnp.concatenate([zero_layer, flux_values], 2)


def apply_padded(padded, vector, coefficients):
    coef_x, coef_y, coef_z, diagonal = coefficients
    across_x = coef_x * (padded[:-1, 1:-1] - padded[1:, 1:-1])
    across_y = coef_y * (padded[1:-1, :-1] - padded[1:-1, 1:])
    across_z = coef_z * (vector[:, :, :-1] - vector[:, :, 1:])
    return diagonal * vector + across_x[1:] - across_x[:-1] + across_y[:, 1:] - across_y[:, :-1] + layer_difference(across_z)


def operate(vector, coefficients):
    padded = jnp.pad(vector, ((1, 1), (1, 1), (0, 0)))
    return apply_padded(padded, vector, coefficients)


def precondition(vector, factor_inverse):
    row_count, col_count, layer_count = vector.shape
    blocks = vector.reshape(row_count // BLOCK, BLOCK, col_count // BLOCK, BLOCK, layer_count)
    lowered = jnp.einsum("aibjk,abmk->aibjm", blocks, factor_inverse, precision=lax.Precision.HIGHEST)
    result = jnp.einsum("aibjm,abmk->aibjk", lowered, factor_inverse, precision=lax.Precision.HIGHEST)
    return result.reshape(vector.shape)


def reference(rock_type, perm_table, poro_table, saturation, pressure_old, factor_inverse, inject_cells, inject_index, inject_rate, produce_cells, produce_index, produce_pressure):
    permeability = perm_table[rock_type]
    porosity = poro_table[rock_type]
    widths = ((1, 1), (1, 1), (0, 0))
    saturation_pad = jnp.pad(saturation, widths)
    pressure_pad = jnp.pad(pressure_old, widths)
    permeability_pad = jnp.pad(permeability, widths)
    total_pad, fraction_pad = mobilities(saturation_pad)
    total_here = total_pad[1:-1, 1:-1]
    fraction_here = fraction_pad[1:-1, 1:-1]
    grid_shape = saturation.shape

    inject_slot = cell_index(inject_cells)
    inject_weight = inject_index * total_here.reshape(-1)[inject_slot]
    inject_share = inject_rate[:, None] * inject_weight / jnp.sum(inject_weight, axis=1)[:, None]
    inject_source = spread_all(inject_slot, inject_share, grid_shape)
    produce_slot = cell_index(produce_cells)
    produce_flow = produce_index * total_here.reshape(-1)[produce_slot] * (pressure_old.reshape(-1)[produce_slot] - produce_pressure[:, None])
    produce_water = spread_all(produce_slot, produce_flow * fraction_here.reshape(-1)[produce_slot], grid_shape)

    vertical = vertical_ratio * permeability
    face_x = harmonic(permeability_pad[:-1, 1:-1], permeability_pad[1:, 1:-1])
    face_y = harmonic(permeability_pad[1:-1, :-1], permeability_pad[1:-1, 1:])
    face_z = harmonic(vertical[:, :, :-1], vertical[:, :, 1:])
    flow_x = face_x * (pressure_pad[:-1, 1:-1] - pressure_pad[1:, 1:-1])
    water_x = flow_x * jnp.where(flow_x > 0.0, fraction_pad[:-1, 1:-1], fraction_pad[1:, 1:-1])
    flow_y = face_y * (pressure_pad[1:-1, :-1] - pressure_pad[1:-1, 1:])
    water_y = flow_y * jnp.where(flow_y > 0.0, fraction_pad[1:-1, :-1], fraction_pad[1:-1, 1:])
    flow_z = face_z * (pressure_old[:, :, :-1] - pressure_old[:, :, 1:])
    water_z = flow_z * jnp.where(flow_z > 0.0, fraction_here[:, :, :-1], fraction_here[:, :, 1:])
    divergence = water_x[1:] - water_x[:-1] + water_y[:, 1:] - water_y[:, :-1] + layer_difference(water_z)
    saturation_new = saturation - time_step / porosity * (divergence + produce_water - inject_source)

    total_new = total_mobility(saturation_new)
    total_new_pad = jnp.pad(total_new, widths)
    coef_x = face_x * (0.5 * (total_new_pad[:-1, 1:-1] + total_new_pad[1:, 1:-1]))
    coef_y = face_y * (0.5 * (total_new_pad[1:-1, :-1] + total_new_pad[1:-1, 1:]))
    coef_z = face_z * (0.5 * (total_new[:, :, :-1] + total_new[:, :, 1:]))
    produce_coef = produce_index * total_new.reshape(-1)[produce_slot]
    diagonal = compress * porosity + spread_all(produce_slot, produce_coef, grid_shape)
    right_side = compress * porosity * pressure_old + inject_source + spread_all(produce_slot, produce_coef * produce_pressure[:, None], grid_shape)
    coefficients = (coef_x, coef_y, coef_z, diagonal)

    solution = pressure_old
    residual = right_side - apply_padded(pressure_pad, pressure_old, coefficients)
    precond = precondition(residual, factor_inverse)
    product = jnp.sum(residual * precond)
    direction = precond
    for sweep in range(ITERS):
        image_field = operate(direction, coefficients)
        step_size = product / jnp.sum(direction * image_field)
        solution = solution + step_size * direction
        if sweep + 1 < ITERS:
            residual = residual - step_size * image_field
            precond = precondition(residual, factor_inverse)
            product_next = jnp.sum(residual * precond)
            direction = precond + (product_next / product) * direction
            product = product_next
    return saturation_new, solution
```

```python
import functools

import jax
import jax.numpy as jnp
from jax import lax
from jax.experimental import pallas as pl
from jax.experimental.pallas import tpu as pltpu
from jax.sharding import PartitionSpec as P

MESH = pl.DeviceIdType.MESH
HIGHEST = lax.Precision.HIGHEST
BLOCK = 16
BASIS = 3
RING = 8
TIME_STEP = 0.002
SHIFT = 1.0 / 16.0

SAT, PRS, PERM, TOTAL, BASE = 0, 1, 2, 3, 4
EXCHANGES = BASE + BASIS
LO_X, HI_X, LO_Y, HI_Y = 0, 1, 2, 3


def harmonic(former, latter):
    return 2.0 * former * latter / (former + latter)


def upwind(face, p_a, p_b, f_a, f_b):
    flow = face * (p_a - p_b)
    return flow * jnp.where(flow > 0.0, f_a, f_b)


def kernel(
    sizes,
    inj_cell,
    inj_rate,
    pro_cell,
    pro_pressure,
    perm_table,
    poro_table,
    inj_index,
    pro_index,
    rock_hbm,
    sat_hbm,
    prs_hbm,
    fac_hbm,
    satn_hbm,
    out_hbm,
    sat,
    prs,
    rock,
    fac,
    prod_hi,
    prod_lo,
    perm,
    dtp,
    poro,
    frac,
    mob,
    select,
    spots,
    face_x,
    face_y,
    face_z,
    low_x,
    side_y,
    div,
    well_d,
    well_e,
    satn,
    total,
    diag,
    resid,
    base,
    image,
    halo_x,
    halo_y,
    pack_y,
    own_z,
    slot_z,
    own_y,
    slot_y,
    own_a,
    slot_a,
    own_b,
    slot_b,
    load_sem,
    store_sem,
    face_send,
    face_recv,
    wz_send,
    wz_recv,
    wy_send,
    wy_recv,
    a_send,
    a_recv,
    b_send,
    b_recv,
):
    rows, cols, layers, n_gx, n_gy = sizes
    cells = rows * cols
    full_cols = cols * n_gy
    n_y = n_gy // RING
    plane = n_gx * n_y
    injectors = inj_index.shape[0]
    producers = pro_index.shape[0]
    perfs = inj_index.shape[1]

    gx = lax.axis_index("gx")
    gy = lax.axis_index("gy")
    yy = gy // RING
    zz = gy % RING
    spot_a = gx * n_y + yy

    def row(x):
        return pl.ds(pl.multiple_of(x * cols, cols), cols)

    def take(ref, c):
        parts = [ref[pl.ds(x * cols + c, 1), :] for x in range(rows)]
        return jnp.concatenate(parts, axis=0)

    def add_to(ref, c, value):
        for x in range(rows):
            ref[pl.ds(x * cols + c, 1), :] += value[x : x + 1]

    neighbours = (
        (lax.rem(gx + n_gx - 1, n_gx), gy),
        (lax.rem(gx + 1, n_gx), gy),
        (gx, lax.rem(gy + n_gy - 1, n_gy)),
        (gx, lax.rem(gy + 1, n_gy)),
    )

    def z_peer(p):
        return (gx, yy * RING + lax.rem(zz + p, RING))

    def plane_peer(p):
        spot = lax.rem(spot_a + p, plane)
        return (spot // n_y, lax.rem(spot, n_y) * RING + zz)

    def y_peer(p):
        return (gx, lax.rem(yy + p, n_y) * RING + zz)

    loads = [
        pltpu.make_async_copy(src, dst, load_sem.at[i])
        for i, (src, dst) in enumerate(
            ((sat_hbm, sat), (rock_hbm, rock), (prs_hbm, prs), (fac_hbm, fac))
        )
    ]
    for load in loads:
        load.start()

    barrier = pltpu.get_barrier_semaphore()
    for peer in neighbours:
        pl.semaphore_signal(barrier, inc=1, device_id=peer, device_id_type=MESH)

    @pl.loop(1, RING)
    def _(p):
        pl.semaphore_signal(barrier, inc=1, device_id=z_peer(p), device_id_type=MESH)

    @pl.loop(1, plane)
    def _(p):
        pl.semaphore_signal(barrier, inc=1, device_id=plane_peer(p), device_id_type=MESH)

    lane = lax.broadcasted_iota(jnp.int32, (1, 128), 1)
    well_row = jnp.full((1, 128), -1, jnp.int32)
    well_layer = jnp.full((1, 128), -1, jnp.int32)
    pressure_row = jnp.zeros((1, 128), jnp.float32)
    rate_row = jnp.zeros((1, 128), jnp.float32)
    spread = lax.broadcasted_iota(jnp.int32, (cols, perfs), 0) - lax.broadcasted_iota(
        jnp.int32, (cols, perfs), 1
    )
    lane_wide = lax.broadcasted_iota(jnp.int32, (cols, 128), 1)
    column = jnp.zeros((cols, 128), jnp.float32)
    for w in range(producers + injectors):
        produces = w < producers
        cell_ref = pro_cell if produces else inj_cell
        index_ref = pro_index if produces else inj_index
        i = w if produces else w - producers
        cell = cell_ref[i, 0, 0]
        well_row = jnp.where(lane == w, cell // full_cols - gx * rows, well_row)
        well_layer = jnp.where(lane == w, cell_ref[i, 1, 0], well_layer)
        start = cell % full_cols
        offset = spread + (gy * cols - start)
        hit = jnp.where(
            (offset == 0) | (offset == full_cols) | (offset == -full_cols),
            index_ref[i : i + 1, :],
            0.0,
        )
        column = jnp.where(lane_wide == w, jnp.sum(hit, axis=1, keepdims=True), column)
        if produces:
            pressure_row = jnp.where(lane == w, pro_pressure[i], pressure_row)
        else:
            rate_row = jnp.where(lane == w, inj_rate[i], rate_row)
    is_producer = jnp.where(lane < producers, 1.0, 0.0)
    layer_pos = lax.broadcasted_iota(jnp.int32, (layers, 128), 0)
    spots[...] = jnp.where(layer_pos == well_layer, 1.0, 0.0)

    @pl.loop(0, rows)
    def _(x):
        select[row(x), :] = jnp.where(well_row == x, column, 0.0)

    loads[0].wait()

    @pl.loop(0, rows)
    def _(x):
        s = sat[row(x), :]
        water = 2.0 * s * s
        rest = 1.0 - s
        t = water + rest * rest
        mob[row(x), :] = t
        frac[row(x), :] = water / t

    picked = jnp.dot(
        mob[...], spots[...], precision=HIGHEST, preferred_element_type=jnp.float32
    )
    own_z[0] = jnp.sum(picked * select[...], axis=0, keepdims=True)

    loads[1].wait()

    @pl.loop(0, rows)
    def _(x):
        kind = rock[row(x), :]
        bit0 = (kind & 1) == 1
        bit1 = (kind & 2) == 2
        bit2 = kind >= 4

        def lookup(table):
            pairs = [jnp.where(bit0, table[2 * i + 1], table[2 * i]) for i in range(4)]
            return jnp.where(
                bit2, jnp.where(bit1, pairs[3], pairs[2]), jnp.where(bit1, pairs[1], pairs[0])
            )

        perm[row(x), :] = lookup(perm_table)
        porosity = lookup(poro_table)
        poro[row(x), :] = porosity
        dtp[row(x), :] = TIME_STEP / porosity

    loads[2].wait()
    for e, field in ((SAT, sat), (PRS, prs), (PERM, perm)):
        pack_y[e, 0] = take(field, 0)
        pack_y[e, 1] = take(field, cols - 1)

    def face_copy(e, d):
        field = (sat, prs, perm, total)[e] if e < BASE else base.at[e - BASE]
        if d == LO_X:
            src, dst = field.at[pl.ds(0, cols), :], halo_x.at[e, 1]
        elif d == HI_X:
            src, dst = field.at[pl.ds(cells - cols, cols), :], halo_x.at[e, 0]
        elif d == LO_Y:
            src, dst = pack_y.at[e, 0], halo_y.at[e, 1]
        else:
            src, dst = pack_y.at[e, 1], halo_y.at[e, 0]
        return pltpu.make_async_remote_copy(
            src_ref=src,
            dst_ref=dst,
            send_sem=face_send.at[e, d],
            recv_sem=face_recv.at[e, d],
            device_id=neighbours[d],
            device_id_type=MESH,
        )

    def send_faces(e):
        for d in range(4):
            face_copy(e, d).start()

    def take_faces(e):
        for d in range(4):
            face_copy(e, d).wait_recv()

    def z_copy(p, own, slots, send, recv):
        return pltpu.make_async_remote_copy(
            src_ref=own.at[0],
            dst_ref=slots.at[p],
            send_sem=send.at[p],
            recv_sem=recv.at[p],
            device_id=z_peer(p),
            device_id_type=MESH,
        )

    def plane_copy(p):
        return pltpu.make_async_remote_copy(
            src_ref=own_a.at[0],
            dst_ref=slot_a.at[p],
            send_sem=a_send.at[p],
            recv_sem=a_recv.at[p],
            device_id=plane_peer(p),
            device_id_type=MESH,
        )

    def y_copy(i):
        return pltpu.make_async_remote_copy(
            src_ref=own_y.at[0],
            dst_ref=slot_y.at[i],
            send_sem=wy_send.at[i],
            recv_sem=wy_recv.at[i],
            device_id=y_peer(1 if i == 0 else n_y - 1),
            device_id_type=MESH,
        )

    pl.semaphore_wait(barrier, 4 + (RING - 1) + (plane - 1))

    @pl.loop(1, RING)
    def _(p):
        z_copy(p, own_z, slot_z, wz_send, wz_recv).start()

    for e in (SAT, PRS, PERM):
        send_faces(e)

    lane_z = lax.broadcasted_iota(jnp.int32, (cols, layers), 1)
    col_y = lax.broadcasted_iota(jnp.int32, (cols, layers), 0)
    inner_z = lane_z < layers - 1
    inner_y = col_y < cols - 1

    def next_y(v):
        return pltpu.roll(v, cols - 1, 0)

    def last_y(v):
        return pltpu.roll(v, 1, 0)

    def next_z(v):
        return pltpu.roll(v, layers - 1, 1)

    def last_z(v):
        return pltpu.roll(v, 1, 1)

    well_d[...] = lax.dot_general(
        select[...],
        spots[...] * is_producer,
        (((1,), (1,)), ((), ())),
        precision=HIGHEST,
        preferred_element_type=jnp.float32,
    )
    well_e[...] = lax.dot_general(
        select[...],
        spots[...] * pressure_row,
        (((1,), (1,)), ((), ())),
        precision=HIGHEST,
        preferred_element_type=jnp.float32,
    )

    zero_row = jnp.zeros((cols, layers), jnp.float32)

    def flux_row(x, flux_last):
        here, there = row(x), row(jnp.minimum(x + 1, rows - 1))
        k, p, f = perm[here, :], prs[here, :], frac[here, :]
        kx, px, fx = perm[there, :], prs[there, :], frac[there, :]
        tx = harmonic(k, kx)
        ty = jnp.where(inner_y, harmonic(k, next_y(k)), 0.0)
        tz = jnp.where(inner_z, 0.1 * harmonic(k, next_z(k)), 0.0)
        face_x[here, :] = tx
        face_y[here, :] = ty
        face_z[here, :] = tz
        wx = upwind(tx, p, px, f, fx)
        wy = upwind(ty, p, next_y(p), f, next_y(f))
        wz = upwind(tz, p, next_z(p), f, next_z(f))
        s = sat[here, :]
        made = 2.0 * s * s * (p * well_d[here, :] - well_e[here, :])
        div[here, :] = (
            made + (wx - flux_last) + (wy - last_y(wy)) + (wz - last_z(wz))
        )
        return wx

    lax.fori_loop(0, rows, flux_row, zero_row)

    loads[3].wait()
    for b in range(cols // BLOCK):
        lower = fac[b]
        gram = lax.dot_general(
            lower,
            lower,
            (((0,), (0,)), ((), ())),
            precision=HIGHEST,
            preferred_element_type=jnp.float32,
        )
        high = gram.astype(jnp.bfloat16)
        prod_hi[b] = high
        prod_lo[b] = (gram - high.astype(jnp.float32)).astype(jnp.bfloat16)

    @pl.loop(1, RING)
    def _(p):
        z_copy(p, own_z, slot_z, wz_send, wz_recv).wait_recv()

    slot_z[0] = own_z[0]
    own_y[0] = jnp.sum(slot_z[...], axis=0)
    for i in range(2):
        y_copy(i).start()

    for e in (SAT, PRS, PERM):
        take_faces(e)

    def fraction(s):
        water = 2.0 * s * s
        rest = 1.0 - s
        return water / (water + rest * rest)

    inner_low_x = jnp.where(gx > 0, 1.0, 0.0)
    inner_high_x = jnp.where(gx < n_gx - 1, 1.0, 0.0)
    inner_low_y = jnp.where(gy > 0, 1.0, 0.0)
    inner_high_y = jnp.where(gy < n_gy - 1, 1.0, 0.0)
    first, final = pl.ds(0, cols), pl.ds(cells - cols, cols)

    t = inner_low_x * harmonic(halo_x[PERM, 0], perm[first, :])
    low_x[...] = t
    div[first, :] -= upwind(
        t, halo_x[PRS, 0], prs[first, :], fraction(halo_x[SAT, 0]), frac[first, :]
    )
    t = inner_high_x * harmonic(perm[final, :], halo_x[PERM, 1])
    face_x[final, :] = t
    div[final, :] += upwind(
        t, prs[final, :], halo_x[PRS, 1], frac[final, :], fraction(halo_x[SAT, 1])
    )
    t = inner_low_y * harmonic(halo_y[PERM, 0], pack_y[PERM, 0])
    side_y[0] = t
    flux = upwind(
        t, halo_y[PRS, 0], pack_y[PRS, 0], fraction(halo_y[SAT, 0]), fraction(pack_y[SAT, 0])
    )
    add_to(div, 0, -flux)
    t = inner_high_y * harmonic(pack_y[PERM, 1], halo_y[PERM, 1])
    side_y[1] = t
    flux = upwind(
        t, pack_y[PRS, 1], halo_y[PRS, 1], fraction(pack_y[SAT, 1]), fraction(halo_y[SAT, 1])
    )
    add_to(div, cols - 1, flux)

    for i in range(2):
        y_copy(i).wait_recv()
    sums = own_y[0] + slot_y[0] + slot_y[1]
    scale = jnp.where(sums > 0.0, rate_row / jnp.where(sums > 0.0, sums, 1.0), 0.0)
    diag[...] = lax.dot_general(
        select[...],
        spots[...] * scale,
        (((1,), (1,)), ((), ())),
        precision=HIGHEST,
        preferred_element_type=jnp.float32,
    )

    @pl.loop(0, rows)
    def _(x):
        here = row(x)
        source = mob[here, :] * diag[here, :]
        s = sat[here, :] - dtp[here, :] * (div[here, :] - source)
        satn[here, :] = s
        resid[here, :] = source
        rest = 1.0 - s
        total[here, :] = 2.0 * s * s + rest * rest

    pack_y[TOTAL, 0] = take(total, 0)
    pack_y[TOTAL, 1] = take(total, cols - 1)
    send_faces(TOTAL)
    store_satn = pltpu.make_async_copy(satn, satn_hbm, store_sem.at[0])
    store_satn.start()

    def residual_row(x, flux_last):
        here, there = row(x), row(jnp.minimum(x + 1, rows - 1))
        t, tx = total[here, :], total[there, :]
        p, px = prs[here, :], prs[there, :]
        cx = face_x[here, :] * (0.5 * (t + tx))
        cy = face_y[here, :] * (0.5 * (t + next_y(t)))
        cz = face_z[here, :] * (0.5 * (t + next_z(t)))

        @pl.when(x < rows - 1)
        def _():
            face_x[here, :] = cx

        face_y[here, :] = cy
        face_z[here, :] = cz
        d, e = well_d[here, :], well_e[here, :]
        diag[here, :] = poro[here, :] + d * t
        fx = cx * (p - px)
        fy = cy * (p - next_y(p))
        fz = cz * (p - next_z(p))
        resid[here, :] = (
            resid[here, :]
            + t * (e - d * p)
            - ((fx - flux_last) + (fy - last_y(fy)) + (fz - last_z(fz)))
        )
        return fx

    lax.fori_loop(0, rows, residual_row, zero_row)

    take_faces(TOTAL)
    c = low_x[...] * (0.5 * (total[first, :] + halo_x[TOTAL, 0]))
    low_x[...] = c
    resid[first, :] -= c * (prs[first, :] - halo_x[PRS, 0])
    c = face_x[final, :] * (0.5 * (total[final, :] + halo_x[TOTAL, 1]))
    face_x[final, :] = c
    resid[final, :] -= c * (prs[final, :] - halo_x[PRS, 1])
    for i, at in ((0, 0), (1, cols - 1)):
        c = side_y[i] * (0.5 * (pack_y[TOTAL, i] + halo_y[TOTAL, i]))
        side_y[i] = c
        add_to(resid, at, -c * (pack_y[PRS, i] - halo_y[PRS, i]))

    def precondition(src, dst, factor):
        for b in range(cols // BLOCK):
            parts = [
                src[pl.ds(x * cols + b * BLOCK, BLOCK), :] for x in range(rows)
            ]
            v = jnp.concatenate(parts, axis=0)
            if factor is not None:
                v = v * factor
            high = v.astype(jnp.bfloat16)
            low = (v - high.astype(jnp.float32)).astype(jnp.bfloat16)
            z = jnp.dot(high, prod_hi[b], preferred_element_type=jnp.float32)
            z += jnp.dot(high, prod_lo[b], preferred_element_type=jnp.float32)
            z += jnp.dot(low, prod_hi[b], preferred_element_type=jnp.float32)
            for x in range(rows):
                dst[pl.ds(x * cols + b * BLOCK, BLOCK), :] = z[x * BLOCK : (x + 1) * BLOCK]

    for k in range(BASIS):
        e = BASE + k
        vec, img = base.at[k], image.at[k]
        precondition(resid if k == 0 else image.at[k - 1], vec, None if k == 0 else SHIFT)
        pack_y[e, 0] = take(vec, 0)
        pack_y[e, 1] = take(vec, cols - 1)
        send_faces(e)

        def image_row(x, flux_last, vec=vec, img=img):
            here, there = row(x), row(jnp.minimum(x + 1, rows - 1))
            v, vx = vec[here, :], vec[there, :]
            fx = face_x[here, :] * (v - vx)
            fy = face_y[here, :] * (v - next_y(v))
            fz = face_z[here, :] * (v - next_z(v))
            img[here, :] = (
                diag[here, :] * v
                + (fx - flux_last)
                + (fy - last_y(fy))
                + (fz - last_z(fz))
            )
            return fx

        lax.fori_loop(0, rows, image_row, zero_row)
        take_faces(e)
        img[first, :] += low_x[...] * (vec[first, :] - halo_x[e, 0])
        img[final, :] += face_x[final, :] * (vec[final, :] - halo_x[e, 1])
        for i, at in ((0, 0), (1, cols - 1)):
            add_to(img, at, side_y[i] * (pack_y[e, i] - halo_y[e, i]))

    pairs = [(0, 0), (1, 0), (1, 1), (2, 0), (2, 1), (2, 2)]

    def dots_row(x, sums):
        here = row(x)
        v = [base[k, here, :] for k in range(BASIS)]
        u = [image[k, here, :] for k in range(BASIS)]
        r = resid[here, :]
        terms = [v[i] * u[j] for i, j in pairs] + [v[i] * r for i in range(BASIS)]
        out = []
        for s, term in zip(sums, terms):
            for i in range(cols // 8):
                s = s + term[8 * i : 8 * i + 8]
            out.append(s)
        return tuple(out)

    zero_sum = jnp.zeros((8, layers), jnp.float32)
    count = len(pairs) + BASIS
    sums = lax.fori_loop(0, rows, dots_row, (zero_sum,) * count)
    message = jnp.zeros((1, 128), jnp.float32)
    for i, s in enumerate(sums):
        s = jnp.sum(s, axis=0, keepdims=True)
        message = jnp.where(lane == i, jnp.sum(s, axis=1, keepdims=True), message)
    own_a[0] = message

    @pl.loop(1, plane)
    def _(p):
        plane_copy(p).start()

    @pl.loop(1, plane)
    def _(p):
        plane_copy(p).wait_recv()

    slot_a[0] = message
    own_b[0] = jnp.sum(slot_a[...], axis=0)

    @pl.loop(1, RING)
    def _(p):
        z_copy(p, own_b, slot_b, b_send, b_recv).start()

    @pl.loop(1, RING)
    def _(p):
        z_copy(p, own_b, slot_b, b_send, b_recv).wait_recv()

    slot_b[0] = own_b[0]
    result = jnp.sum(slot_b[...], axis=0)
    val = [result[:, i : i + 1] for i in range(count)]
    g00, g10, g11, g20, g21, g22, b0, b1, b2 = val

    def ratio(a, b):
        good = b > 0.0
        return jnp.where(good, a / jnp.where(good, b, 1.0), 0.0)

    l10, l20 = ratio(g10, g00), ratio(g20, g00)
    d1 = g11 - l10 * g10
    e21 = g21 - l20 * g10
    l21 = ratio(e21, d1)
    d2 = g22 - l20 * g20 - l21 * e21
    y1 = b1 - l10 * b0
    y2 = b2 - l20 * b0 - l21 * y1
    c2 = ratio(y2, d2)
    c1 = ratio(y1, d1) - l21 * c2
    c0 = ratio(b0, g00) - l10 * c1 - l20 * c2

    @pl.loop(0, rows)
    def _(x):
        here = row(x)
        div[here, :] = prs[here, :] + (
            c0 * base[0, here, :] + c1 * base[1, here, :] + c2 * base[2, here, :]
        )

    store_out = pltpu.make_async_copy(div, out_hbm, store_sem.at[1])
    store_out.start()

    @pl.loop(1, RING)
    def _(p):
        z_copy(p, own_z, slot_z, wz_send, wz_recv).wait_send()
        z_copy(p, own_b, slot_b, b_send, b_recv).wait_send()

    @pl.loop(1, plane)
    def _(p):
        plane_copy(p).wait_send()

    for i in range(2):
        y_copy(i).wait_send()
    for e in range(EXCHANGES):
        for d in range(4):
            face_copy(e, d).wait_send()
    store_satn.wait()
    store_out.wait()


def solution(mesh):
    n_gx, n_gy = mesh.shape["gx"], mesh.shape["gy"]

    def per_device(
        rock_type,
        perm_table,
        poro_table,
        saturation,
        pressure_old,
        factor_inverse,
        inject_cells,
        inject_index,
        inject_rate,
        produce_cells,
        produce_index,
        produce_pressure,
    ):
        rows, cols, layers = saturation.shape
        cells = rows * cols
        blocks = cols // BLOCK
        f32, bf16 = jnp.float32, jnp.bfloat16
        flat = (cells, layers)
        field = pltpu.VMEM(flat, f32)
        smem = pl.BlockSpec(memory_space=pltpu.SMEM)
        vmem = pl.BlockSpec(memory_space=pltpu.VMEM)
        hbm = pl.BlockSpec(memory_space=pl.ANY)
        plane = n_gx * (n_gy // RING)
        dma = pltpu.SemaphoreType.DMA
        scratch = [
            field,
            field,
            pltpu.VMEM(flat, jnp.int32),
            pltpu.VMEM((blocks, layers, layers), f32),
            pltpu.VMEM((blocks, layers, layers), bf16),
            pltpu.VMEM((blocks, layers, layers), bf16),
            field,
            field,
            field,
            field,
            field,
            pltpu.VMEM((cells, 128), f32),
            pltpu.VMEM((layers, 128), f32),
            field,
            field,
            field,
            pltpu.VMEM((cols, layers), f32),
            pltpu.VMEM((2, rows, layers), f32),
            field,
            field,
            field,
            field,
            field,
            field,
            field,
            pltpu.VMEM((BASIS,) + flat, f32),
            pltpu.VMEM((BASIS,) + flat, f32),
            pltpu.VMEM((EXCHANGES, 2, cols, layers), f32),
            pltpu.VMEM((EXCHANGES, 2, rows, layers), f32),
            pltpu.VMEM((EXCHANGES, 2, rows, layers), f32),
            pltpu.VMEM((1, 1, 128), f32),
            pltpu.VMEM((RING, 1, 128), f32),
            pltpu.VMEM((1, 1, 128), f32),
            pltpu.VMEM((2, 1, 128), f32),
            pltpu.VMEM((1, 1, 128), f32),
            pltpu.VMEM((plane, 1, 128), f32),
            pltpu.VMEM((1, 1, 128), f32),
            pltpu.VMEM((RING, 1, 128), f32),
            dma((4,)),
            dma((2,)),
            dma((EXCHANGES, 4)),
            dma((EXCHANGES, 4)),
            dma((RING,)),
            dma((RING,)),
            dma((2,)),
            dma((2,)),
            dma((plane,)),
            dma((plane,)),
            dma((RING,)),
            dma((RING,)),
        ]
        satn, out = pl.pallas_call(
            functools.partial(kernel, (rows, cols, layers, n_gx, n_gy)),
            out_shape=[jax.ShapeDtypeStruct(flat, f32)] * 2,
            in_specs=[smem] * 6 + [vmem] * 2 + [hbm] * 4,
            out_specs=[hbm] * 2,
            scratch_shapes=scratch,
            compiler_params=pltpu.CompilerParams(
                collective_id=0, has_side_effects=True, vmem_limit_bytes=60 * 1024 * 1024
            ),
            name="reservoir_step",
        )(
            jnp.swapaxes(inject_cells, 1, 2),
            inject_rate,
            jnp.swapaxes(produce_cells, 1, 2),
            produce_pressure,
            perm_table,
            poro_table,
            inject_index,
            produce_index,
            rock_type.reshape(flat),
            saturation.reshape(flat),
            pressure_old.reshape(flat),
            factor_inverse.reshape(blocks, layers, layers),
        )
        return satn.reshape(saturation.shape), out.reshape(saturation.shape)

    grid = P("gx", "gy", None)
    in_specs = (grid, P(), P(), grid, grid, P("gx", "gy", None, None)) + (P(),) * 6
    return jax.shard_map(
        per_device, mesh=mesh, in_specs=in_specs, out_specs=(grid, grid), check_vma=False
    )
```

```python
import functools

import jax
import jax.numpy as jnp
from jax import lax
from jax.experimental import pallas as pl
from jax.experimental.pallas import tpu as pltpu
from jax.sharding import PartitionSpec as P

MESH = pl.DeviceIdType.MESH
HIGHEST = lax.Precision.HIGHEST
BLOCK = 16
BASIS = 3
RING = 8
TIME_STEP = 0.002
SHIFT = 2.0**-14

INPUT, MOVED, BASE = 0, 1, 2
EXCHANGES = BASE + BASIS
SAT, PRS, PERM, DTP = 0, 1, 2, 3
LO_X, HI_X, LO_Y, HI_Y = 0, 1, 2, 3
REACH_X, REACH_Y = 1, 5


def harmonic(former, latter):
    return 2.0 * former * latter / (former + latter)


def upwind(face, p_a, p_b, f_a, f_b):
    flow = face * (p_a - p_b)
    return flow * jnp.where(flow > 0.0, f_a, f_b)


def kernel(
    sizes,
    inj_cell,
    inj_rate,
    pro_cell,
    pro_pressure,
    perm_table,
    poro_table,
    inj_index,
    pro_index,
    rock_hbm,
    sat_hbm,
    prs_hbm,
    fac_hbm,
    made_hbm,
    coef_out,
    inp,
    rock,
    fac,
    prod_hi,
    prod_lo,
    poro,
    frac,
    mob,
    select,
    spots,
    face_x,
    face_y,
    face_z,
    low_x,
    side_y,
    moved,
    well_d,
    well_e,
    source,
    satn,
    total,
    diag,
    resid,
    base,
    image,
    input_x,
    input_y,
    input_pack,
    halo_x,
    halo_y,
    pack_y,
    own,
    slot_w,
    slot_a,
    slot_b,
    load_sem,
    store_sem,
    face_send,
    face_recv,
    group_send,
    group_recv,
):
    rows, cols, layers, n_gx, n_gy = sizes
    cells = rows * cols
    full_cols = cols * n_gy
    n_y = n_gy // RING
    plane = n_gx * n_y
    injectors = inj_index.shape[0]
    producers = pro_index.shape[0]
    perfs = inj_index.shape[1]
    sat, prs, perm, dtp = (inp.at[i] for i in range(4))

    gx = lax.axis_index("gx")
    gy = lax.axis_index("gy")
    yy = gy // RING
    zz = gy % RING
    spot_a = gx * n_y + yy

    def row(x):
        return pl.ds(pl.multiple_of(x * cols, cols), cols)

    def take(ref, c):
        parts = [ref[pl.ds(x * cols + c, 1), :] for x in range(rows)]
        return jnp.concatenate(parts, axis=0)

    def add_to(ref, c, value):
        for x in range(rows):
            ref[pl.ds(x * cols + c, 1), :] += value[x : x + 1]

    neighbours = (
        (lax.rem(gx + n_gx - 1, n_gx), gy),
        (lax.rem(gx + 1, n_gx), gy),
        (gx, lax.rem(gy + n_gy - 1, n_gy)),
        (gx, lax.rem(gy + 1, n_gy)),
    )
    sends = (gx > 0, gx < n_gx - 1, gy > 0, gy < n_gy - 1)
    hears = (gx < n_gx - 1, gx > 0, gy < n_gy - 1, gy > 0)

    def z_peer(p):
        return (gx, yy * RING + lax.rem(zz + p, RING))

    def plane_peer(p):
        spot = lax.rem(spot_a + p, plane)
        return (spot // n_y, lax.rem(spot, n_y) * RING + zz)

    width = 2 * REACH_Y + 1
    window = (2 * REACH_X + 1) * width
    centre = window // 2

    def window_peer(q):
        return (
            lax.rem(gx + n_gx - REACH_X + q // width, n_gx),
            lax.rem(gy + n_gy - REACH_Y + lax.rem(q, width), n_gy),
        )

    def window_each(action):
        pl.loop(0, centre)(lambda q: action(q, q))
        pl.loop(centre + 1, window)(lambda q: action(q, q - 1))

    loads = [
        pltpu.make_async_copy(src, dst, load_sem.at[i])
        for i, (src, dst) in enumerate(
            ((sat_hbm, sat), (rock_hbm, rock), (prs_hbm, prs), (fac_hbm, fac))
        )
    ]
    for load in loads:
        load.start()

    barrier = pltpu.get_barrier_semaphore()

    def greet(peer):
        pl.semaphore_signal(barrier, inc=1, device_id=peer, device_id_type=MESH)

    window_each(lambda q, slot: greet(window_peer(q)))
    pl.loop(1, RING)(lambda p: greet(z_peer(p)))
    pl.loop(1, plane)(lambda p: greet(plane_peer(p)))

    def clear_x(at):
        input_x[at] = jnp.zeros(input_x.shape[1:], jnp.float32)
        for e in range(EXCHANGES - 1):
            halo_x[e, at] = jnp.zeros(halo_x.shape[2:], jnp.float32)

    def clear_y(at):
        input_y[at] = jnp.zeros(input_y.shape[1:], jnp.float32)
        for e in range(EXCHANGES - 1):
            halo_y[e, at] = jnp.zeros(halo_y.shape[2:], jnp.float32)

    pl.when(gx == 0)(lambda: clear_x(0))
    pl.when(gx == n_gx - 1)(lambda: clear_x(1))
    pl.when(gy == 0)(lambda: clear_y(0))
    pl.when(gy == n_gy - 1)(lambda: clear_y(1))

    lane = lax.broadcasted_iota(jnp.int32, (1, 128), 1)
    well_row = jnp.full((1, 128), -9, jnp.int32)
    well_layer = jnp.full((1, 128), -9, jnp.int32)
    pressure_row = jnp.zeros((1, 128), jnp.float32)
    rate_row = jnp.zeros((1, 128), jnp.float32)
    wide = cols + 16
    spread = lax.broadcasted_iota(jnp.int32, (wide, perfs), 0) - lax.broadcasted_iota(
        jnp.int32, (wide, perfs), 1
    )
    lane_wide = lax.broadcasted_iota(jnp.int32, (wide, 128), 1)
    column = jnp.zeros((wide, 128), jnp.float32)
    for w in range(producers + injectors):
        produces = w < producers
        cell_ref = pro_cell if produces else inj_cell
        index_ref = pro_index if produces else inj_index
        i = w if produces else w - producers
        cell = cell_ref[i, 0, 0]
        well_row = jnp.where(lane == w, cell // full_cols - gx * rows, well_row)
        well_layer = jnp.where(lane == w, cell_ref[i, 1, 0], well_layer)
        start = cell % full_cols
        offset = spread + (gy * cols - 8 - start)
        hit = jnp.where(
            (offset == 0) | (offset == full_cols) | (offset == -full_cols),
            index_ref[i : i + 1, :],
            0.0,
        )
        column = jnp.where(lane_wide == w, jnp.sum(hit, axis=1, keepdims=True), column)
        if produces:
            pressure_row = jnp.where(lane == w, pro_pressure[i], pressure_row)
        else:
            rate_row = jnp.where(lane == w, inj_rate[i], rate_row)
    is_producer = jnp.where(lane < producers, 1.0, 0.0)
    layer_pos = lax.broadcasted_iota(jnp.int32, (layers, 128), 0)
    spots[...] = jnp.where(layer_pos == well_layer, 1.0, 0.0)
    own_column = column[8 : 8 + cols]
    for x in range(rows):
        select[x * cols : (x + 1) * cols, :] = jnp.where(well_row == x, own_column, 0.0)
    select[cells : cells + cols, :] = jnp.where(well_row == -1, own_column, 0.0)
    select[cells + cols : cells + 2 * cols, :] = jnp.where(well_row == rows, own_column, 0.0)
    row_pos = lax.broadcasted_iota(jnp.int32, (rows, 128), 0)
    rim_y = cells + 2 * cols
    select[rim_y : rim_y + rows, :] = jnp.where(row_pos == well_row, column[7:8], 0.0)
    select[rim_y + rows : rim_y + 2 * rows, :] = jnp.where(
        row_pos == well_row, column[8 + cols : 9 + cols], 0.0
    )

    loads[0].wait()

    def mobility(s):
        water = 2.0 * s * s
        rest = 1.0 - s
        return water, water + rest * rest

    @pl.loop(0, rows)
    def _(x):
        water, t = mobility(sat[row(x), :])
        mob[row(x), :] = t
        frac[row(x), :] = water / t

    picked = jnp.dot(
        mob[...], spots[...], precision=HIGHEST, preferred_element_type=jnp.float32
    )
    own[0] = jnp.sum(picked * select[pl.ds(0, cells), :], axis=0, keepdims=True)

    loads[1].wait()

    @pl.loop(0, rows)
    def _(x):
        kind = rock[row(x), :]
        bit0 = (kind & 1) == 1
        bit1 = (kind & 2) == 2
        bit2 = kind >= 4

        def lookup(table):
            pairs = [jnp.where(bit0, table[2 * i + 1], table[2 * i]) for i in range(4)]
            return jnp.where(
                bit2, jnp.where(bit1, pairs[3], pairs[2]), jnp.where(bit1, pairs[1], pairs[0])
            )

        perm[row(x), :] = lookup(perm_table)
        porosity = lookup(poro_table)
        poro[row(x), :] = porosity
        dtp[row(x), :] = TIME_STEP / porosity

    loads[2].wait()
    for i in range(4):
        input_pack[0, i] = take(inp.at[i], 0)
        input_pack[1, i] = take(inp.at[i], cols - 1)

    def face_copy(e, d):
        if e == INPUT:
            if d < 2:
                src = inp.at[:, pl.ds(0 if d == LO_X else cells - cols, cols), :]
                dst = input_x.at[1 - d]
            else:
                src, dst = input_pack.at[d - 2], input_y.at[3 - d]
        else:
            field = moved if e == MOVED else base.at[e - BASE]
            if d < 2:
                src = field.at[pl.ds(0 if d == LO_X else cells - cols, cols), :]
                dst = halo_x.at[e - 1, 1 - d]
            else:
                src, dst = pack_y.at[e - 1, d - 2], halo_y.at[e - 1, 3 - d]
        return pltpu.make_async_remote_copy(
            src_ref=src,
            dst_ref=dst,
            send_sem=face_send.at[d],
            recv_sem=face_recv.at[e % 2, d],
            device_id=neighbours[d],
            device_id_type=MESH,
        )

    def send_faces(e):
        for d in (LO_Y, HI_Y, LO_X, HI_X):

            @pl.when(sends[d])
            def _():
                if e > 0:
                    face_copy(e - 1, d).wait_send()
                face_copy(e, d).start()

    def take_faces(e):
        for d in range(4):
            pl.when(hears[d])(lambda: face_copy(e, d).wait_recv())

    def group_copy(k, slot, peer, src, slots):
        return pltpu.make_async_remote_copy(
            src_ref=src,
            dst_ref=slots.at[slot],
            send_sem=group_send.at[k],
            recv_sem=group_recv.at[k],
            device_id=peer,
            device_id_type=MESH,
        )

    def group_all(k, peer, slots, low, count):
        held = slots.at[pl.ds(low, count)]
        return pltpu.make_async_remote_copy(
            src_ref=held,
            dst_ref=held,
            send_sem=group_send.at[k],
            recv_sem=group_recv.at[k],
            device_id=peer(low),
            device_id_type=MESH,
        )

    def plane_start(k, src, slots):
        pl.loop(1, plane)(lambda p: group_copy(k, p, plane_peer(p), src, slots).start())

    def plane_all(k, slots):
        return group_all(k, plane_peer, slots, 1, plane - 1)

    def ring_start(k, src, slots):
        pl.loop(1, RING)(lambda p: group_copy(k, p, z_peer(p), src, slots).start())

    def ring_all(k, slots):
        return group_all(k, z_peer, slots, 1, RING - 1)

    pl.semaphore_wait(barrier, (window - 1) + (RING - 1) + (plane - 1))
    window_each(
        lambda q, slot: group_copy(0, slot, window_peer(q), own.at[0], slot_w).start()
    )
    send_faces(INPUT)

    lane_z = lax.broadcasted_iota(jnp.int32, (cols, layers), 1)
    col_y = lax.broadcasted_iota(jnp.int32, (cols, layers), 0)
    inner_z = lane_z < layers - 1
    inner_y = col_y < cols - 1

    def next_y(v):
        return pltpu.roll(v, cols - 1, 0)

    def last_y(v):
        return pltpu.roll(v, 1, 0)

    def next_z(v):
        return pltpu.roll(v, layers - 1, 1)

    def last_z(v):
        return pltpu.roll(v, 1, 1)

    def place(chosen, weights):
        return lax.dot_general(
            chosen,
            spots[...] * weights,
            (((1,), (1,)), ((), ())),
            precision=HIGHEST,
            preferred_element_type=jnp.float32,
        )

    loads[3].wait()
    largest = jnp.zeros((1, 128), jnp.float32)
    for b in range(cols // BLOCK):
        lower = fac[b]
        gram = lax.dot_general(
            lower,
            lower,
            (((0,), (0,)), ((), ())),
            precision=HIGHEST,
            preferred_element_type=jnp.float32,
        )
        high = gram.astype(jnp.bfloat16)
        prod_hi[b] = high
        prod_lo[b] = (gram - high.astype(jnp.float32)).astype(jnp.bfloat16)
        row_sum = jnp.sum(jnp.abs(gram), axis=0, keepdims=True)
        largest = jnp.maximum(largest, jnp.max(row_sum, axis=1, keepdims=True))
    own[1] = largest
    plane_start(1, own.at[1], slot_a.at[0])

    well_d[...] = place(select[pl.ds(0, cells), :], is_producer)
    well_e[...] = place(select[pl.ds(0, cells), :], pressure_row)

    zero_row = jnp.zeros((cols, layers), jnp.float32)

    def flux_row(x, flux_last):
        here, there = row(x), row(jnp.minimum(x + 1, rows - 1))
        k, p, f = perm[here, :], prs[here, :], frac[here, :]
        kx, px, fx = perm[there, :], prs[there, :], frac[there, :]
        tx = harmonic(k, kx)
        ty = jnp.where(inner_y, harmonic(k, next_y(k)), 0.0)
        tz = jnp.where(inner_z, 0.1 * harmonic(k, next_z(k)), 0.0)
        face_x[here, :] = tx
        face_y[here, :] = ty
        face_z[here, :] = tz
        wx = upwind(tx, p, px, f, fx)
        wy = upwind(ty, p, next_y(p), f, next_y(f))
        wz = upwind(tz, p, next_z(p), f, next_z(f))
        s = sat[here, :]
        made = 2.0 * s * s * (p * well_d[here, :] - well_e[here, :])
        moved[here, :] = s - dtp[here, :] * (
            made + (wx - flux_last) + (wy - last_y(wy)) + (wz - last_z(wz))
        )
        return wx

    lax.fori_loop(0, rows, flux_row, zero_row)

    def fraction(s):
        water, t = mobility(s)
        return water / t

    first, final = pl.ds(0, cols), pl.ds(cells - cols, cols)
    take_faces(INPUT)
    t = harmonic(input_x[0, PERM], perm[first, :])
    low_x[...] = t
    moved[first, :] += dtp[first, :] * upwind(
        t, input_x[0, PRS], prs[first, :], fraction(input_x[0, SAT]), frac[first, :]
    )
    t = harmonic(perm[final, :], input_x[1, PERM])
    face_x[final, :] = t
    moved[final, :] -= dtp[final, :] * upwind(
        t, prs[final, :], input_x[1, PRS], frac[final, :], fraction(input_x[1, SAT])
    )
    pack, rim = input_pack, input_y
    t = harmonic(rim[0, PERM], pack[0, PERM])
    side_y[0] = t
    flux = upwind(t, rim[0, PRS], pack[0, PRS], fraction(rim[0, SAT]), fraction(pack[0, SAT]))
    add_to(moved, 0, pack[0, DTP] * flux)
    t = harmonic(pack[1, PERM], rim[1, PERM])
    side_y[1] = t
    flux = upwind(t, pack[1, PRS], rim[1, PRS], fraction(pack[1, SAT]), fraction(rim[1, SAT]))
    add_to(moved, cols - 1, -pack[1, DTP] * flux)
    for i, c in ((0, 0), (1, cols - 1)):
        pack_y[MOVED - 1, i] = take(moved, c)
    send_faces(MOVED)

    plane_all(1, slot_a.at[0]).wait_recv()
    slot_a[0, 0] = own[1]
    own[2] = jnp.max(slot_a[0], axis=0)
    ring_start(2, own.at[2], slot_b.at[0])

    group_all(0, window_peer, slot_w, 0, window - 1).wait_recv()
    slot_w[window - 1] = own[0]
    sums = jnp.sum(slot_w[...], axis=0)
    scale = jnp.where(sums > 0.0, rate_row / jnp.where(sums > 0.0, sums, 1.0), 0.0)
    source[...] = place(select[...], scale)

    @pl.loop(0, rows)
    def _(x):
        here = row(x)
        made = mob[here, :] * source[here, :]
        s = moved[here, :] + dtp[here, :] * made
        satn[here, :] = s
        resid[here, :] = made
        total[here, :] = mobility(s)[1]

    store_satn = pltpu.make_async_copy(satn, made_hbm.at[0], store_sem.at[0])
    store_satn.start()

    def residual_row(x, flux_last):
        here, there = row(x), row(jnp.minimum(x + 1, rows - 1))
        t, tx = total[here, :], total[there, :]
        p, px = prs[here, :], prs[there, :]
        cx = face_x[here, :] * (0.5 * (t + tx))
        cy = face_y[here, :] * (0.5 * (t + next_y(t)))
        cz = face_z[here, :] * (0.5 * (t + next_z(t)))

        @pl.when(x < rows - 1)
        def _():
            face_x[here, :] = cx

        face_y[here, :] = cy
        face_z[here, :] = cz
        d, e = well_d[here, :], well_e[here, :]
        diag[here, :] = poro[here, :] + d * t
        fx = cx * (p - px)
        fy = cy * (p - next_y(p))
        fz = cz * (p - next_z(p))
        resid[here, :] = (
            resid[here, :]
            + t * (e - d * p)
            - ((fx - flux_last) + (fy - last_y(fy)) + (fz - last_z(fz)))
        )
        return fx

    lax.fori_loop(0, rows, residual_row, zero_row)

    def rim_total(before, sat_rim, dtp_rim, weights):
        s = before + dtp_rim * (mobility(sat_rim)[1] * weights)
        return mobility(s)[1]

    pack_total = [take(total, 0), take(total, cols - 1)]
    take_faces(MOVED)
    t = rim_total(
        halo_x[MOVED - 1, 0], input_x[0, SAT], input_x[0, DTP], source[pl.ds(cells, cols), :]
    )
    c = low_x[...] * (0.5 * (total[first, :] + t))
    low_x[...] = c
    resid[first, :] -= c * (prs[first, :] - input_x[0, PRS])
    t = rim_total(
        halo_x[MOVED - 1, 1],
        input_x[1, SAT],
        input_x[1, DTP],
        source[pl.ds(cells + cols, cols), :],
    )
    c = face_x[final, :] * (0.5 * (total[final, :] + t))
    face_x[final, :] = c
    resid[final, :] -= c * (prs[final, :] - input_x[1, PRS])
    for i, at in ((0, 0), (1, cols - 1)):
        t = rim_total(
            halo_y[MOVED - 1, i],
            rim[i, SAT],
            rim[i, DTP],
            source[pl.ds(rim_y + i * rows, rows), :],
        )
        c = side_y[i] * (0.5 * (pack_total[i] + t))
        side_y[i] = c
        add_to(resid, at, -c * (pack[i, PRS] - rim[i, PRS]))

    ring_all(2, slot_b.at[0]).wait_recv()
    slot_b[0, 0] = own[2]
    norm = 1.0 / jnp.max(slot_b[0], axis=0)
    norm = jnp.concatenate([norm] * (layers // 128), axis=1)

    def precondition(src, dst, factor):
        for b in range(cols // BLOCK):
            parts = [
                src[pl.ds(x * cols + b * BLOCK, BLOCK), :] for x in range(rows)
            ]
            v = jnp.concatenate(parts, axis=0) * factor
            high = v.astype(jnp.bfloat16)
            low = (v - high.astype(jnp.float32)).astype(jnp.bfloat16)
            z = jnp.dot(high, prod_hi[b], preferred_element_type=jnp.float32)
            z += jnp.dot(high, prod_lo[b], preferred_element_type=jnp.float32)
            z += jnp.dot(low, prod_hi[b], preferred_element_type=jnp.float32)
            for x in range(rows):
                dst[pl.ds(x * cols + b * BLOCK, BLOCK), :] = z[x * BLOCK : (x + 1) * BLOCK]

    stores = [store_satn]
    for k in range(BASIS):
        e = BASE + k
        vec, img = base.at[k], image.at[k]
        precondition(
            resid if k == 0 else image.at[k - 1], vec, norm if k == 0 else norm * SHIFT
        )
        pack_y[e - 1, 0] = take(vec, 0)
        pack_y[e - 1, 1] = take(vec, cols - 1)
        send_faces(e)
        store = pltpu.make_async_copy(vec, made_hbm.at[1 + k], store_sem.at[1 + k])
        store.start()
        stores.append(store)

        def image_row(x, flux_last, vec=vec, img=img):
            here, there = row(x), row(jnp.minimum(x + 1, rows - 1))
            v, vx = vec[here, :], vec[there, :]
            fx = face_x[here, :] * (v - vx)
            fy = face_y[here, :] * (v - next_y(v))
            fz = face_z[here, :] * (v - next_z(v))
            img[here, :] = (
                diag[here, :] * v
                + (fx - flux_last)
                + (fy - last_y(fy))
                + (fz - last_z(fz))
            )
            return fx

        lax.fori_loop(0, rows, image_row, zero_row)
        take_faces(e)
        h = e - 1
        img[first, :] += low_x[...] * (vec[first, :] - halo_x[h, 0])
        img[final, :] += face_x[final, :] * (vec[final, :] - halo_x[h, 1])
        for i, at in ((0, 0), (1, cols - 1)):
            add_to(img, at, side_y[i] * (pack_y[h, i] - halo_y[h, i]))

    pairs = [(0, 0), (1, 0), (1, 1), (2, 0), (2, 1), (2, 2)]

    def dots_row(x, sums):
        here = row(x)
        v = [base[k, here, :] for k in range(BASIS)]
        u = [image[k, here, :] for k in range(BASIS)]
        r = resid[here, :]
        terms = [v[i] * u[j] for i, j in pairs] + [v[i] * r for i in range(BASIS)]
        out = []
        for s, term in zip(sums, terms):
            for i in range(cols // 8):
                s = s + term[8 * i : 8 * i + 8]
            out.append(s)
        return tuple(out)

    zero_sum = jnp.zeros((8, layers), jnp.float32)
    count = len(pairs) + BASIS
    sums = lax.fori_loop(0, rows, dots_row, (zero_sum,) * count)
    message = jnp.zeros((1, 128), jnp.float32)
    for i, s in enumerate(sums):
        s = jnp.sum(s, axis=0, keepdims=True)
        message = jnp.where(lane == i, jnp.sum(s, axis=1, keepdims=True), message)
    own[3] = message
    plane_start(3, own.at[3], slot_a.at[1])
    plane_all(3, slot_a.at[1]).wait_recv()
    slot_a[1, 0] = own[3]
    own[4] = jnp.sum(slot_a[1], axis=0)
    ring_start(4, own.at[4], slot_b.at[1])
    ring_all(4, slot_b.at[1]).wait_recv()
    slot_b[1, 0] = own[4]
    result = jnp.sum(slot_b[1], axis=0)
    val = [result[:, i : i + 1] for i in range(count)]
    g00, g10, g11, g20, g21, g22, b0, b1, b2 = val

    def ratio(a, b):
        good = b > 0.0
        return jnp.where(good, a / jnp.where(good, b, 1.0), 0.0)

    l10, l20 = ratio(g10, g00), ratio(g20, g00)
    d1 = g11 - l10 * g10
    e21 = g21 - l20 * g10
    l21 = ratio(e21, d1)
    d2 = g22 - l20 * g20 - l21 * e21
    y1 = b1 - l10 * b0
    y2 = b2 - l20 * b0 - l21 * y1
    c2 = ratio(y2, d2)
    c1 = ratio(y1, d1) - l21 * c2
    c0 = ratio(b0, g00) - l10 * c1 - l20 * c2
    for k, c in enumerate((c0, c1, c2)):
        coef_out[k] = jnp.broadcast_to(c, (1, layers))

    group_all(0, window_peer, slot_w, 0, window - 1).wait_send()
    plane_all(1, slot_a.at[0]).wait_send()
    ring_all(2, slot_b.at[0]).wait_send()
    plane_all(3, slot_a.at[1]).wait_send()
    ring_all(4, slot_b.at[1]).wait_send()
    for d in range(4):
        pl.when(sends[d])(lambda: face_copy(EXCHANGES - 1, d).wait_send())
    for store in stores:
        store.wait()


def solution(mesh):
    n_gx, n_gy = mesh.shape["gx"], mesh.shape["gy"]

    def per_device(
        rock_type,
        perm_table,
        poro_table,
        saturation,
        pressure_old,
        factor_inverse,
        inject_cells,
        inject_index,
        inject_rate,
        produce_cells,
        produce_index,
        produce_pressure,
    ):
        rows, cols, layers = saturation.shape
        cells = rows * cols
        blocks = cols // BLOCK
        f32, bf16 = jnp.float32, jnp.bfloat16
        flat = (cells, layers)
        field = pltpu.VMEM(flat, f32)
        smem = pl.BlockSpec(memory_space=pltpu.SMEM)
        vmem = pl.BlockSpec(memory_space=pltpu.VMEM)
        hbm = pl.BlockSpec(memory_space=pl.ANY)
        plane = n_gx * (n_gy // RING)
        dma = pltpu.SemaphoreType.DMA
        window = (2 * REACH_X + 1) * (2 * REACH_Y + 1)
        scratch = [
            pltpu.VMEM((4,) + flat, f32),
            pltpu.VMEM(flat, jnp.int32),
            pltpu.VMEM((blocks, layers, layers), f32),
            pltpu.VMEM((blocks, layers, layers), bf16),
            pltpu.VMEM((blocks, layers, layers), bf16),
            field,
            field,
            field,
            pltpu.VMEM((cells + 2 * cols + 2 * rows, 128), f32),
            pltpu.VMEM((layers, 128), f32),
            field,
            field,
            field,
            pltpu.VMEM((cols, layers), f32),
            pltpu.VMEM((2, rows, layers), f32),
            field,
            field,
            field,
            pltpu.VMEM((cells + 2 * cols + 2 * rows, layers), f32),
            field,
            field,
            field,
            field,
            pltpu.VMEM((BASIS,) + flat, f32),
            pltpu.VMEM((BASIS,) + flat, f32),
            pltpu.VMEM((2, 4, cols, layers), f32),
            pltpu.VMEM((2, 4, rows, layers), f32),
            pltpu.VMEM((2, 4, rows, layers), f32),
            pltpu.VMEM((EXCHANGES - 1, 2, cols, layers), f32),
            pltpu.VMEM((EXCHANGES - 1, 2, rows, layers), f32),
            pltpu.VMEM((EXCHANGES - 1, 2, rows, layers), f32),
            pltpu.VMEM((5, 1, 128), f32),
            pltpu.VMEM((window, 1, 128), f32),
            pltpu.VMEM((2, plane, 1, 128), f32),
            pltpu.VMEM((2, RING, 1, 128), f32),
            dma((4,)),
            dma((1 + BASIS,)),
            dma((4,)),
            dma((2, 4)),
            dma((5,)),
            dma((5,)),
        ]
        made, coef = pl.pallas_call(
            functools.partial(kernel, (rows, cols, layers, n_gx, n_gy)),
            out_shape=[
                jax.ShapeDtypeStruct((1 + BASIS,) + flat, f32),
                jax.ShapeDtypeStruct((BASIS, 1, layers), f32),
            ],
            in_specs=[smem] * 6 + [vmem] * 2 + [hbm] * 4,
            out_specs=[hbm, vmem],
            scratch_shapes=scratch,
            compiler_params=pltpu.CompilerParams(
                collective_id=0, has_side_effects=True, vmem_limit_bytes=60 * 1024 * 1024
            ),
            name="reservoir_step",
        )(
            jnp.swapaxes(inject_cells, 1, 2),
            inject_rate,
            jnp.swapaxes(produce_cells, 1, 2),
            produce_pressure,
            perm_table,
            poro_table,
            inject_index,
            produce_index,
            rock_type.reshape(flat),
            saturation.reshape(flat),
            pressure_old.reshape(flat),
            factor_inverse.reshape(blocks, layers, layers),
        )
        change = coef[0] * made[1] + coef[1] * made[2] + coef[2] * made[3]
        pressure = pressure_old.reshape(flat) + change
        return made[0].reshape(saturation.shape), pressure.reshape(saturation.shape)

    grid = P("gx", "gy", None)
    in_specs = (grid, P(), P(), grid, grid, P("gx", "gy", None, None)) + (P(),) * 6
    return jax.shard_map(
        per_device, mesh=mesh, in_specs=in_specs, out_specs=(grid, grid), check_vma=False
    )
```

```python
import functools

import jax
import jax.numpy as jnp
from jax import lax
from jax.experimental import pallas as pl
from jax.experimental.pallas import tpu as pltpu
from jax.sharding import PartitionSpec as P

MESH = pl.DeviceIdType.MESH
HIGHEST = lax.Precision.HIGHEST
BLOCK = 16
BASIS = 3
RING = 8
TIME_STEP = 0.002
SHIFT = 2.0**-14

INPUT, MOVED, BASE = 0, 1, 2
EXCHANGES = BASE + BASIS
SAT, PRS, PERM, DTP = 0, 1, 2, 3
LO_X, HI_X, LO_Y, HI_Y = 0, 1, 2, 3
REACH_X, REACH_Y = 1, 5


def harmonic(former, latter):
    return 2.0 * former * latter / (former + latter)


def upwind(face, p_a, p_b, f_a, f_b):
    flow = face * (p_a - p_b)
    return flow * jnp.where(flow > 0.0, f_a, f_b)


def kernel(
    sizes,
    inj_cell,
    inj_rate,
    pro_cell,
    pro_pressure,
    perm_table,
    poro_table,
    inj_index,
    pro_index,
    rock_hbm,
    sat_hbm,
    prs_hbm,
    fac_hbm,
    satn_out,
    z0_out,
    z1_out,
    z2_out,
    coef_out,
    inp,
    rock,
    fac,
    prod_hi,
    prod_lo,
    poro,
    frac,
    mob,
    select,
    spots,
    face_x,
    face_y,
    face_z,
    low_x,
    side_y,
    moved,
    well_d,
    well_e,
    source,
    satn,
    total,
    diag,
    resid,
    base,
    image,
    input_x,
    input_y,
    input_pack,
    halo_x,
    halo_y,
    pack_y,
    own,
    slot_w,
    slot_a,
    slot_b,
    load_sem,
    store_sem,
    face_send,
    face_recv,
    group_send,
    group_recv,
):
    rows, cols, layers, n_gx, n_gy = sizes
    cells = rows * cols
    full_cols = cols * n_gy
    n_y = n_gy // RING
    plane = n_gx * n_y
    injectors = inj_index.shape[0]
    producers = pro_index.shape[0]
    perfs = inj_index.shape[1]
    sat, prs, perm, dtp = (inp.at[i] for i in range(4))

    gx = lax.axis_index("gx")
    gy = lax.axis_index("gy")
    yy = gy // RING
    zz = gy % RING
    spot_a = gx * n_y + yy

    def row(x):
        return pl.ds(pl.multiple_of(x * cols, cols), cols)

    def take(ref, c):
        parts = [ref[pl.ds(x * cols + c, 1), :] for x in range(rows)]
        return jnp.concatenate(parts, axis=0)

    def add_to(ref, c, value):
        for x in range(rows):
            ref[pl.ds(x * cols + c, 1), :] += value[x : x + 1]

    neighbours = (
        (lax.rem(gx + n_gx - 1, n_gx), gy),
        (lax.rem(gx + 1, n_gx), gy),
        (gx, lax.rem(gy + n_gy - 1, n_gy)),
        (gx, lax.rem(gy + 1, n_gy)),
    )
    sends = (gx > 0, gx < n_gx - 1, gy > 0, gy < n_gy - 1)
    hears = (gx < n_gx - 1, gx > 0, gy < n_gy - 1, gy > 0)

    def z_peer(p):
        return (gx, yy * RING + lax.rem(zz + p, RING))

    def plane_peer(p):
        spot = lax.rem(spot_a + p, plane)
        return (spot // n_y, lax.rem(spot, n_y) * RING + zz)

    width = 2 * REACH_Y + 1
    window = (2 * REACH_X + 1) * width
    centre = window // 2

    def window_peer(q):
        return (
            lax.rem(gx + n_gx - REACH_X + q // width, n_gx),
            lax.rem(gy + n_gy - REACH_Y + lax.rem(q, width), n_gy),
        )

    def window_each(action):
        pl.loop(0, centre)(lambda q: action(q, q))
        pl.loop(centre + 1, window)(lambda q: action(q, q - 1))

    loads = [
        pltpu.make_async_copy(src, dst, load_sem.at[i])
        for i, (src, dst) in enumerate(
            ((sat_hbm, sat), (rock_hbm, rock), (prs_hbm, prs), (fac_hbm, fac))
        )
    ]
    for load in loads:
        load.start()

    barrier = pltpu.get_barrier_semaphore()

    def greet(peer):
        pl.semaphore_signal(barrier, inc=1, device_id=peer, device_id_type=MESH)

    window_each(lambda q, slot: greet(window_peer(q)))
    pl.loop(1, RING)(lambda p: greet(z_peer(p)))
    pl.loop(1, plane)(lambda p: greet(plane_peer(p)))

    def clear_x(at):
        input_x[at] = jnp.zeros(input_x.shape[1:], jnp.float32)
        for e in range(EXCHANGES - 1):
            halo_x[e, at] = jnp.zeros(halo_x.shape[2:], jnp.float32)

    def clear_y(at):
        input_y[at] = jnp.zeros(input_y.shape[1:], jnp.float32)
        for e in range(EXCHANGES - 1):
            halo_y[e, at] = jnp.zeros(halo_y.shape[2:], jnp.float32)

    pl.when(gx == 0)(lambda: clear_x(0))
    pl.when(gx == n_gx - 1)(lambda: clear_x(1))
    pl.when(gy == 0)(lambda: clear_y(0))
    pl.when(gy == n_gy - 1)(lambda: clear_y(1))

    lane = lax.broadcasted_iota(jnp.int32, (1, 128), 1)
    well_row = jnp.full((1, 128), -9, jnp.int32)
    well_layer = jnp.full((1, 128), -9, jnp.int32)
    pressure_row = jnp.zeros((1, 128), jnp.float32)
    rate_row = jnp.zeros((1, 128), jnp.float32)
    wide = cols + 16
    spread = lax.broadcasted_iota(jnp.int32, (wide, perfs), 0) - lax.broadcasted_iota(
        jnp.int32, (wide, perfs), 1
    )
    lane_wide = lax.broadcasted_iota(jnp.int32, (wide, 128), 1)
    column = jnp.zeros((wide, 128), jnp.float32)
    for w in range(producers + injectors):
        produces = w < producers
        cell_ref = pro_cell if produces else inj_cell
        index_ref = pro_index if produces else inj_index
        i = w if produces else w - producers
        cell = cell_ref[i, 0, 0]
        well_row = jnp.where(lane == w, cell // full_cols - gx * rows, well_row)
        well_layer = jnp.where(lane == w, cell_ref[i, 1, 0], well_layer)
        start = cell % full_cols
        offset = spread + (gy * cols - 8 - start)
        hit = jnp.where(
            (offset == 0) | (offset == full_cols) | (offset == -full_cols),
            index_ref[i : i + 1, :],
            0.0,
        )
        column = jnp.where(lane_wide == w, jnp.sum(hit, axis=1, keepdims=True), column)
        if produces:
            pressure_row = jnp.where(lane == w, pro_pressure[i], pressure_row)
        else:
            rate_row = jnp.where(lane == w, inj_rate[i], rate_row)
    is_producer = jnp.where(lane < producers, 1.0, 0.0)
    layer_pos = lax.broadcasted_iota(jnp.int32, (layers, 128), 0)
    spots[...] = jnp.where(layer_pos == well_layer, 1.0, 0.0)
    own_column = column[8 : 8 + cols]
    for x in range(rows):
        select[x * cols : (x + 1) * cols, :] = jnp.where(well_row == x, own_column, 0.0)
    select[cells : cells + cols, :] = jnp.where(well_row == -1, own_column, 0.0)
    select[cells + cols : cells + 2 * cols, :] = jnp.where(well_row == rows, own_column, 0.0)
    row_pos = lax.broadcasted_iota(jnp.int32, (rows, 128), 0)
    rim_y = cells + 2 * cols
    select[rim_y : rim_y + rows, :] = jnp.where(row_pos == well_row, column[7:8], 0.0)
    select[rim_y + rows : rim_y + 2 * rows, :] = jnp.where(
        row_pos == well_row, column[8 + cols : 9 + cols], 0.0
    )

    loads[0].wait()

    def mobility(s):
        water = 2.0 * s * s
        rest = 1.0 - s
        return water, water + rest * rest

    @pl.loop(0, rows)
    def _(x):
        water, t = mobility(sat[row(x), :])
        mob[row(x), :] = t
        frac[row(x), :] = water / t

    picked = jnp.dot(
        mob[...], spots[...], precision=HIGHEST, preferred_element_type=jnp.float32
    )
    own[0] = jnp.sum(picked * select[pl.ds(0, cells), :], axis=0, keepdims=True)

    loads[1].wait()

    @pl.loop(0, rows)
    def _(x):
        kind = rock[row(x), :]
        bit0 = (kind & 1) == 1
        bit1 = (kind & 2) == 2
        bit2 = kind >= 4

        def lookup(table):
            pairs = [jnp.where(bit0, table[2 * i + 1], table[2 * i]) for i in range(4)]
            return jnp.where(
                bit2, jnp.where(bit1, pairs[3], pairs[2]), jnp.where(bit1, pairs[1], pairs[0])
            )

        perm[row(x), :] = lookup(perm_table)
        porosity = lookup(poro_table)
        poro[row(x), :] = porosity
        dtp[row(x), :] = TIME_STEP / porosity

    loads[2].wait()
    for i in range(4):
        input_pack[0, i] = take(inp.at[i], 0)
        input_pack[1, i] = take(inp.at[i], cols - 1)

    def face_copy(e, d):
        if e == INPUT:
            if d < 2:
                src = inp.at[:, pl.ds(0 if d == LO_X else cells - cols, cols), :]
                dst = input_x.at[1 - d]
            else:
                src, dst = input_pack.at[d - 2], input_y.at[3 - d]
        else:
            field = moved if e == MOVED else base.at[e - BASE]
            if d < 2:
                src = field.at[pl.ds(0 if d == LO_X else cells - cols, cols), :]
                dst = halo_x.at[e - 1, 1 - d]
            else:
                src, dst = pack_y.at[e - 1, d - 2], halo_y.at[e - 1, 3 - d]
        return pltpu.make_async_remote_copy(
            src_ref=src,
            dst_ref=dst,
            send_sem=face_send.at[d],
            recv_sem=face_recv.at[e % 2, d],
            device_id=neighbours[d],
            device_id_type=MESH,
        )

    def send_faces(e):
        for d in (LO_Y, HI_Y, LO_X, HI_X):

            @pl.when(sends[d])
            def _():
                if e > 0:
                    face_copy(e - 1, d).wait_send()
                face_copy(e, d).start()

    def take_faces(e):
        for d in range(4):
            pl.when(hears[d])(lambda: face_copy(e, d).wait_recv())

    def group_copy(k, slot, peer, src, slots):
        return pltpu.make_async_remote_copy(
            src_ref=src,
            dst_ref=slots.at[slot],
            send_sem=group_send.at[k],
            recv_sem=group_recv.at[k],
            device_id=peer,
            device_id_type=MESH,
        )

    def group_all(k, peer, slots, low, count):
        held = slots.at[pl.ds(low, count)]
        return pltpu.make_async_remote_copy(
            src_ref=held,
            dst_ref=held,
            send_sem=group_send.at[k],
            recv_sem=group_recv.at[k],
            device_id=peer(low),
            device_id_type=MESH,
        )

    def plane_start(k, src, slots):
        pl.loop(1, plane)(lambda p: group_copy(k, p, plane_peer(p), src, slots).start())

    def plane_all(k, slots):
        return group_all(k, plane_peer, slots, 1, plane - 1)

    def ring_start(k, src, slots):
        pl.loop(1, RING)(lambda p: group_copy(k, p, z_peer(p), src, slots).start())

    def ring_all(k, slots):
        return group_all(k, z_peer, slots, 1, RING - 1)

    pl.semaphore_wait(barrier, (window - 1) + (RING - 1) + (plane - 1))
    window_each(
        lambda q, slot: group_copy(0, slot, window_peer(q), own.at[0], slot_w).start()
    )
    send_faces(INPUT)

    lane_z = lax.broadcasted_iota(jnp.int32, (cols, layers), 1)
    col_y = lax.broadcasted_iota(jnp.int32, (cols, layers), 0)
    inner_z = lane_z < layers - 1
    inner_y = col_y < cols - 1

    def next_y(v):
        return pltpu.roll(v, cols - 1, 0)

    def last_y(v):
        return pltpu.roll(v, 1, 0)

    def next_z(v):
        return pltpu.roll(v, layers - 1, 1)

    def last_z(v):
        return pltpu.roll(v, 1, 1)

    def place(chosen, weights):
        return lax.dot_general(
            chosen,
            spots[...] * weights,
            (((1,), (1,)), ((), ())),
            precision=HIGHEST,
            preferred_element_type=jnp.float32,
        )

    loads[3].wait()
    largest = jnp.zeros((1, 128), jnp.float32)
    for b in range(cols // BLOCK):
        lower = fac[b]
        gram = lax.dot_general(
            lower,
            lower,
            (((0,), (0,)), ((), ())),
            precision=HIGHEST,
            preferred_element_type=jnp.float32,
        )
        high = gram.astype(jnp.bfloat16)
        prod_hi[b] = high
        prod_lo[b] = (gram - high.astype(jnp.float32)).astype(jnp.bfloat16)
        row_sum = jnp.sum(jnp.abs(gram), axis=0, keepdims=True)
        largest = jnp.maximum(largest, jnp.max(row_sum, axis=1, keepdims=True))
    own[1] = largest
    plane_start(1, own.at[1], slot_a.at[0])

    well_d[...] = place(select[pl.ds(0, cells), :], is_producer)
    well_e[...] = place(select[pl.ds(0, cells), :], pressure_row)

    zero_row = jnp.zeros((cols, layers), jnp.float32)

    def flux_row(x, flux_last):
        here, there = row(x), row(jnp.minimum(x + 1, rows - 1))
        k, p, f = perm[here, :], prs[here, :], frac[here, :]
        kx, px, fx = perm[there, :], prs[there, :], frac[there, :]
        tx = harmonic(k, kx)
        ty = jnp.where(inner_y, harmonic(k, next_y(k)), 0.0)
        tz = jnp.where(inner_z, 0.1 * harmonic(k, next_z(k)), 0.0)
        face_x[here, :] = tx
        face_y[here, :] = ty
        face_z[here, :] = tz
        wx = upwind(tx, p, px, f, fx)
        wy = upwind(ty, p, next_y(p), f, next_y(f))
        wz = upwind(tz, p, next_z(p), f, next_z(f))
        s = sat[here, :]
        made = 2.0 * s * s * (p * well_d[here, :] - well_e[here, :])
        moved[here, :] = s - dtp[here, :] * (
            made + (wx - flux_last) + (wy - last_y(wy)) + (wz - last_z(wz))
        )
        return wx

    lax.fori_loop(0, rows, flux_row, zero_row)

    def fraction(s):
        water, t = mobility(s)
        return water / t

    first, final = pl.ds(0, cols), pl.ds(cells - cols, cols)
    take_faces(INPUT)
    t = harmonic(input_x[0, PERM], perm[first, :])
    low_x[...] = t
    moved[first, :] += dtp[first, :] * upwind(
        t, input_x[0, PRS], prs[first, :], fraction(input_x[0, SAT]), frac[first, :]
    )
    t = harmonic(perm[final, :], input_x[1, PERM])
    face_x[final, :] = t
    moved[final, :] -= dtp[final, :] * upwind(
        t, prs[final, :], input_x[1, PRS], frac[final, :], fraction(input_x[1, SAT])
    )
    pack, rim = input_pack, input_y
    t = harmonic(rim[0, PERM], pack[0, PERM])
    side_y[0] = t
    flux = upwind(t, rim[0, PRS], pack[0, PRS], fraction(rim[0, SAT]), fraction(pack[0, SAT]))
    add_to(moved, 0, pack[0, DTP] * flux)
    t = harmonic(pack[1, PERM], rim[1, PERM])
    side_y[1] = t
    flux = upwind(t, pack[1, PRS], rim[1, PRS], fraction(pack[1, SAT]), fraction(rim[1, SAT]))
    add_to(moved, cols - 1, -pack[1, DTP] * flux)
    for i, c in ((0, 0), (1, cols - 1)):
        pack_y[MOVED - 1, i] = take(moved, c)
    send_faces(MOVED)

    plane_all(1, slot_a.at[0]).wait_recv()
    slot_a[0, 0] = own[1]
    own[2] = jnp.max(slot_a[0], axis=0)
    ring_start(2, own.at[2], slot_b.at[0])

    group_all(0, window_peer, slot_w, 0, window - 1).wait_recv()
    slot_w[window - 1] = own[0]
    sums = jnp.sum(slot_w[...], axis=0)
    scale = jnp.where(sums > 0.0, rate_row / jnp.where(sums > 0.0, sums, 1.0), 0.0)
    source[...] = place(select[...], scale)

    @pl.loop(0, rows)
    def _(x):
        here = row(x)
        made = mob[here, :] * source[here, :]
        s = moved[here, :] + dtp[here, :] * made
        satn[here, :] = s
        resid[here, :] = made
        total[here, :] = mobility(s)[1]

    store_satn = pltpu.make_async_copy(satn, satn_out, store_sem.at[0])
    store_satn.start()

    def residual_row(x, flux_last):
        here, there = row(x), row(jnp.minimum(x + 1, rows - 1))
        t, tx = total[here, :], total[there, :]
        p, px = prs[here, :], prs[there, :]
        cx = face_x[here, :] * (0.5 * (t + tx))
        cy = face_y[here, :] * (0.5 * (t + next_y(t)))
        cz = face_z[here, :] * (0.5 * (t + next_z(t)))

        @pl.when(x < rows - 1)
        def _():
            face_x[here, :] = cx

        face_y[here, :] = cy
        face_z[here, :] = cz
        d, e = well_d[here, :], well_e[here, :]
        diag[here, :] = poro[here, :] + d * t
        fx = cx * (p - px)
        fy = cy * (p - next_y(p))
        fz = cz * (p - next_z(p))
        resid[here, :] = (
            resid[here, :]
            + t * (e - d * p)
            - ((fx - flux_last) + (fy - last_y(fy)) + (fz - last_z(fz)))
        )
        return fx

    lax.fori_loop(0, rows, residual_row, zero_row)

    def rim_total(before, sat_rim, dtp_rim, weights):
        s = before + dtp_rim * (mobility(sat_rim)[1] * weights)
        return mobility(s)[1]

    pack_total = [take(total, 0), take(total, cols - 1)]
    take_faces(MOVED)
    t = rim_total(
        halo_x[MOVED - 1, 0], input_x[0, SAT], input_x[0, DTP], source[pl.ds(cells, cols), :]
    )
    c = low_x[...] * (0.5 * (total[first, :] + t))
    low_x[...] = c
    resid[first, :] -= c * (prs[first, :] - input_x[0, PRS])
    t = rim_total(
        halo_x[MOVED - 1, 1],
        input_x[1, SAT],
        input_x[1, DTP],
        source[pl.ds(cells + cols, cols), :],
    )
    c = face_x[final, :] * (0.5 * (total[final, :] + t))
    face_x[final, :] = c
    resid[final, :] -= c * (prs[final, :] - input_x[1, PRS])
    for i, at in ((0, 0), (1, cols - 1)):
        t = rim_total(
            halo_y[MOVED - 1, i],
            rim[i, SAT],
            rim[i, DTP],
            source[pl.ds(rim_y + i * rows, rows), :],
        )
        c = side_y[i] * (0.5 * (pack_total[i] + t))
        side_y[i] = c
        add_to(resid, at, -c * (pack[i, PRS] - rim[i, PRS]))

    ring_all(2, slot_b.at[0]).wait_recv()
    slot_b[0, 0] = own[2]
    norm = 1.0 / jnp.max(slot_b[0], axis=0)
    norm = jnp.concatenate([norm] * (layers // 128), axis=1)

    def precondition(src, dst, factor):
        for b in range(cols // BLOCK):
            parts = [
                src[pl.ds(x * cols + b * BLOCK, BLOCK), :] for x in range(rows)
            ]
            v = jnp.concatenate(parts, axis=0) * factor
            high = v.astype(jnp.bfloat16)
            low = (v - high.astype(jnp.float32)).astype(jnp.bfloat16)
            z = jnp.dot(high, prod_hi[b], preferred_element_type=jnp.float32)
            z += jnp.dot(high, prod_lo[b], preferred_element_type=jnp.float32)
            z += jnp.dot(low, prod_hi[b], preferred_element_type=jnp.float32)
            for x in range(rows):
                dst[pl.ds(x * cols + b * BLOCK, BLOCK), :] = z[x * BLOCK : (x + 1) * BLOCK]

    stores = [store_satn]
    for k in range(BASIS):
        e = BASE + k
        vec, img = base.at[k], image.at[k]
        precondition(
            resid if k == 0 else image.at[k - 1], vec, norm if k == 0 else norm * SHIFT
        )
        pack_y[e - 1, 0] = take(vec, 0)
        pack_y[e - 1, 1] = take(vec, cols - 1)
        send_faces(e)
        store = pltpu.make_async_copy(
            vec, (z0_out, z1_out, z2_out)[k], store_sem.at[1 + k]
        )
        store.start()
        stores.append(store)

        def image_row(x, flux_last, vec=vec, img=img):
            here, there = row(x), row(jnp.minimum(x + 1, rows - 1))
            v, vx = vec[here, :], vec[there, :]
            fx = face_x[here, :] * (v - vx)
            fy = face_y[here, :] * (v - next_y(v))
            fz = face_z[here, :] * (v - next_z(v))
            img[here, :] = (
                diag[here, :] * v
                + (fx - flux_last)
                + (fy - last_y(fy))
                + (fz - last_z(fz))
            )
            return fx

        lax.fori_loop(0, rows, image_row, zero_row)
        take_faces(e)
        h = e - 1
        img[first, :] += low_x[...] * (vec[first, :] - halo_x[h, 0])
        img[final, :] += face_x[final, :] * (vec[final, :] - halo_x[h, 1])
        for i, at in ((0, 0), (1, cols - 1)):
            add_to(img, at, side_y[i] * (pack_y[h, i] - halo_y[h, i]))

    pairs = [(0, 0), (1, 0), (1, 1), (2, 0), (2, 1), (2, 2)]

    def dots_row(x, sums):
        here = row(x)
        v = [base[k, here, :] for k in range(BASIS)]
        u = [image[k, here, :] for k in range(BASIS)]
        r = resid[here, :]
        terms = [v[i] * u[j] for i, j in pairs] + [v[i] * r for i in range(BASIS)]
        out = []
        for s, term in zip(sums, terms):
            for i in range(cols // 8):
                s = s + term[8 * i : 8 * i + 8]
            out.append(s)
        return tuple(out)

    zero_sum = jnp.zeros((8, layers), jnp.float32)
    count = len(pairs) + BASIS
    sums = lax.fori_loop(0, rows, dots_row, (zero_sum,) * count)
    message = jnp.zeros((1, 128), jnp.float32)
    for i, s in enumerate(sums):
        s = jnp.sum(s, axis=0, keepdims=True)
        message = jnp.where(lane == i, jnp.sum(s, axis=1, keepdims=True), message)
    own[3] = message
    plane_start(3, own.at[3], slot_a.at[1])
    plane_all(3, slot_a.at[1]).wait_recv()
    slot_a[1, 0] = own[3]
    own[4] = jnp.sum(slot_a[1], axis=0)
    ring_start(4, own.at[4], slot_b.at[1])
    ring_all(4, slot_b.at[1]).wait_recv()
    slot_b[1, 0] = own[4]
    result = jnp.sum(slot_b[1], axis=0)
    val = [result[:, i : i + 1] for i in range(count)]
    g00, g10, g11, g20, g21, g22, b0, b1, b2 = val

    def ratio(a, b):
        good = b > 0.0
        return jnp.where(good, a / jnp.where(good, b, 1.0), 0.0)

    l10, l20 = ratio(g10, g00), ratio(g20, g00)
    d1 = g11 - l10 * g10
    e21 = g21 - l20 * g10
    l21 = ratio(e21, d1)
    d2 = g22 - l20 * g20 - l21 * e21
    y1 = b1 - l10 * b0
    y2 = b2 - l20 * b0 - l21 * y1
    c2 = ratio(y2, d2)
    c1 = ratio(y1, d1) - l21 * c2
    c0 = ratio(b0, g00) - l10 * c1 - l20 * c2
    for k, c in enumerate((c0, c1, c2)):
        coef_out[k : k + 1, :] = jnp.broadcast_to(c, (1, layers))

    group_all(0, window_peer, slot_w, 0, window - 1).wait_send()
    plane_all(1, slot_a.at[0]).wait_send()
    ring_all(2, slot_b.at[0]).wait_send()
    plane_all(3, slot_a.at[1]).wait_send()
    ring_all(4, slot_b.at[1]).wait_send()
    for d in range(4):
        pl.when(sends[d])(lambda: face_copy(EXCHANGES - 1, d).wait_send())
    for store in stores:
        store.wait()


def solution(mesh):
    n_gx, n_gy = mesh.shape["gx"], mesh.shape["gy"]

    def per_device(
        rock_type,
        perm_table,
        poro_table,
        saturation,
        pressure_old,
        factor_inverse,
        inject_cells,
        inject_index,
        inject_rate,
        produce_cells,
        produce_index,
        produce_pressure,
    ):
        rows, cols, layers = saturation.shape
        cells = rows * cols
        blocks = cols // BLOCK
        f32, bf16 = jnp.float32, jnp.bfloat16
        flat = (cells, layers)
        field = pltpu.VMEM(flat, f32)
        smem = pl.BlockSpec(memory_space=pltpu.SMEM)
        vmem = pl.BlockSpec(memory_space=pltpu.VMEM)
        hbm = pl.BlockSpec(memory_space=pltpu.HBM)
        out = pl.BlockSpec(memory_space=pl.ANY)
        plane = n_gx * (n_gy // RING)
        dma = pltpu.SemaphoreType.DMA
        window = (2 * REACH_X + 1) * (2 * REACH_Y + 1)
        scratch = [
            pltpu.VMEM((4,) + flat, f32),
            pltpu.VMEM(flat, jnp.int32),
            pltpu.VMEM((blocks, layers, layers), f32),
            pltpu.VMEM((blocks, layers, layers), bf16),
            pltpu.VMEM((blocks, layers, layers), bf16),
            field,
            field,
            field,
            pltpu.VMEM((cells + 2 * cols + 2 * rows, 128), f32),
            pltpu.VMEM((layers, 128), f32),
            field,
            field,
            field,
            pltpu.VMEM((cols, layers), f32),
            pltpu.VMEM((2, rows, layers), f32),
            field,
            field,
            field,
            pltpu.VMEM((cells + 2 * cols + 2 * rows, layers), f32),
            field,
            field,
            field,
            field,
            pltpu.VMEM((BASIS,) + flat, f32),
            pltpu.VMEM((BASIS,) + flat, f32),
            pltpu.VMEM((2, 4, cols, layers), f32),
            pltpu.VMEM((2, 4, rows, layers), f32),
            pltpu.VMEM((2, 4, rows, layers), f32),
            pltpu.VMEM((EXCHANGES - 1, 2, cols, layers), f32),
            pltpu.VMEM((EXCHANGES - 1, 2, rows, layers), f32),
            pltpu.VMEM((EXCHANGES - 1, 2, rows, layers), f32),
            pltpu.VMEM((5, 1, 128), f32),
            pltpu.VMEM((window, 1, 128), f32),
            pltpu.VMEM((2, plane, 1, 128), f32),
            pltpu.VMEM((2, RING, 1, 128), f32),
            dma((4,)),
            dma((1 + BASIS,)),
            dma((4,)),
            dma((2, 4)),
            dma((5,)),
            dma((5,)),
        ]
        operands = (
            jnp.swapaxes(inject_cells, 1, 2),
            inject_rate,
            jnp.swapaxes(produce_cells, 1, 2),
            produce_pressure,
            perm_table,
            poro_table,
            inject_index,
            produce_index,
            rock_type.reshape(flat),
            saturation.reshape(flat),
            pressure_old.reshape(flat),
            factor_inverse.reshape(blocks, layers, layers),
        )
        satn, z0, z1, z2, coef = pl.pallas_call(
            functools.partial(kernel, (rows, cols, layers, n_gx, n_gy)),
            out_shape=[
                *[jax.ShapeDtypeStruct(flat, f32)] * (1 + BASIS),
                jax.ShapeDtypeStruct((BASIS, layers), f32),
            ],
            in_specs=[smem] * 6 + [vmem] * 2 + [hbm] * 4,
            out_specs=[out] * (1 + BASIS) + [vmem],
            scratch_shapes=scratch,
            compiler_params=pltpu.CompilerParams(
                collective_id=0, has_side_effects=True, vmem_limit_bytes=24 * 1024 * 1024
            ),
            name="reservoir_step",
        )(*(pltpu.with_memory_space_constraint(a, pltpu.HBM) for a in operands))
        change = coef[0:1] * z0 + coef[1:2] * z1 + coef[2:3] * z2
        pressure = pressure_old.reshape(flat) + change
        return satn.reshape(saturation.shape), pressure.reshape(saturation.shape)

    grid = P("gx", "gy", None)
    in_specs = (grid, P(), P(), grid, grid, P("gx", "gy", None, None)) + (P(),) * 6
    return jax.shard_map(
        per_device, mesh=mesh, in_specs=in_specs, out_specs=(grid, grid), check_vma=False
    )
```

```python
import functools

import jax
import jax.numpy as jnp
from jax import lax
from jax.experimental import pallas as pl
from jax.experimental.pallas import tpu as pltpu
from jax.sharding import PartitionSpec as P

MESH = pl.DeviceIdType.MESH
HIGHEST = lax.Precision.HIGHEST
BLOCK = 16
BASIS = 3
RING = 8
TIME_STEP = 0.002
SHIFT = 2.0**-14

INPUT, MOVED, BASE = 0, 1, 2
EXCHANGES = BASE + BASIS
SAT, PRS, PERM, DTP = 0, 1, 2, 3
LO_X, HI_X, LO_Y, HI_Y = 0, 1, 2, 3
REACH = 5
FAR_X = (4, 3, 5, 2, 6, 1, 7)
FAR_Y = (2, 1, 3)
FAR_Z = (4, 3, 5, 2, 6, 1, 7)


def harmonic(former, latter):
    return 2.0 * former * latter / (former + latter)


def upwind(face, p_a, p_b, f_a, f_b):
    flow = face * (p_a - p_b)
    return flow * jnp.where(flow > 0.0, f_a, f_b)


def kernel(
    sizes,
    inj_cell,
    inj_rate,
    pro_cell,
    pro_pressure,
    perm_table,
    poro_table,
    inj_index,
    pro_index,
    rock_hbm,
    sat_hbm,
    prs_hbm,
    fac_hbm,
    satn_out,
    z0_out,
    z1_out,
    z2_out,
    coef_out,
    inp,
    rock,
    fac,
    prod_hi,
    prod_lo,
    poro,
    frac,
    mob,
    select,
    spots,
    face_x,
    face_y,
    face_z,
    low_x,
    side_y,
    moved,
    well_d,
    well_e,
    source,
    satn,
    total,
    diag,
    resid,
    base,
    image,
    input_x,
    input_y,
    input_pack,
    halo_x,
    halo_y,
    pack_x,
    pack_y,
    own,
    slot_w,
    slot_v,
    slot_x,
    slot_y,
    slot_s,
    slot_a,
    slot_b,
    load_sem,
    store_sem,
    face_send,
    face_recv,
    group_send,
    group_recv,
):
    rows, cols, layers, n_gx, n_gy = sizes
    blocks = cols // BLOCK
    cells = rows * cols
    full_cols = cols * n_gy
    n_y = n_gy // RING
    plane = n_gx * n_y
    injectors = inj_index.shape[0]
    producers = pro_index.shape[0]
    perfs = inj_index.shape[1]
    sat, prs, perm, dtp = (inp.at[i] for i in range(4))

    gx = lax.axis_index("gx")
    gy = lax.axis_index("gy")
    yy = gy // RING
    zz = gy % RING
    spot_a = gx * n_y + yy

    def row(x):
        return pl.ds(pl.multiple_of(x * cols, cols), cols)

    def take(ref, c):
        parts = [ref[pl.ds(x * cols + c, 1), :] for x in range(rows)]
        return jnp.concatenate(parts, axis=0)

    def add_to(ref, c, value):
        for x in range(rows):
            ref[pl.ds(x * cols + c, 1), :] += value[x : x + 1]

    def put(ref, c, value):
        for x in range(rows):
            ref[pl.ds(x * cols + c, 1), :] = value[x : x + 1]

    neighbours = (
        (lax.rem(gx + n_gx - 1, n_gx), gy),
        (lax.rem(gx + 1, n_gx), gy),
        (gx, lax.rem(gy + n_gy - 1, n_gy)),
        (gx, lax.rem(gy + 1, n_gy)),
    )
    sends = (gx > 0, gx < n_gx - 1, gy > 0, gy < n_gy - 1)
    hears = (gx < n_gx - 1, gx > 0, gy < n_gy - 1, gy > 0)

    def near(a, b, c=0):
        y = lax.rem(yy + b, n_y) if b else yy
        z = lax.rem(zz + c, RING) if c else zz
        return (lax.rem(gx + a, n_gx) if a else gx, y * RING + z)

    def along_gy(b):
        return (gx, lax.rem(gy + n_gy + b, n_gy))

    reach = [b for d in range(REACH, 0, -1) for b in (d, -d)]
    line_peers = [along_gy(b) for b in reach]
    side_peers = [near(n_gx - 1, 0), near(1, 0)]
    x_peers = [near(a, 0) for a in FAR_X]
    y_peers = [near(0, b) for b in FAR_Y]
    z_peers = [near(0, 0, c) for c in FAR_Z]
    plane_peers = [near(a, b) for a in FAR_X + (0,) for b in FAR_Y + (0,) if a or b]

    loads = [
        pltpu.make_async_copy(src, dst, load_sem.at[i])
        for i, (src, dst) in enumerate(
            ((sat_hbm, sat), (rock_hbm, rock), (prs_hbm, prs), (fac_hbm, fac))
        )
    ]
    for load in loads:
        load.start()

    barrier = pltpu.get_barrier_semaphore()

    def greet(peer):
        pl.semaphore_signal(barrier, inc=1, device_id=peer, device_id_type=MESH)

    for peer in plane_peers + line_peers + z_peers:
        greet(peer)

    def clear_x(at):
        input_x[at] = jnp.zeros(input_x.shape[1:], jnp.float32)
        for e in range(EXCHANGES - 1):
            halo_x[e, at] = jnp.zeros(halo_x.shape[2:], jnp.float32)

    def clear_y(at):
        input_y[at] = jnp.zeros(input_y.shape[1:], jnp.float32)
        for e in range(EXCHANGES - 1):
            halo_y[e, at] = jnp.zeros(halo_y.shape[2:], jnp.float32)

    pl.when(gx == 0)(lambda: clear_x(0))
    pl.when(gx == n_gx - 1)(lambda: clear_x(1))
    pl.when(gy == 0)(lambda: clear_y(0))
    pl.when(gy == n_gy - 1)(lambda: clear_y(1))

    def lookup(kind, table):
        bit0 = (kind & 1) == 1
        bit1 = (kind & 2) == 2
        pairs = [jnp.where(bit0, table[2 * i + 1], table[2 * i]) for i in range(4)]
        high = jnp.where(bit1, pairs[3], pairs[2])
        return jnp.where(kind >= 4, high, jnp.where(bit1, pairs[1], pairs[0]))

    def fill_row(x):
        kind = rock[row(x), :]
        perm[row(x), :] = lookup(kind, perm_table)
        porosity = lookup(kind, poro_table)
        poro[row(x), :] = porosity
        dtp[row(x), :] = TIME_STEP / porosity

    loads[1].wait()
    for i, c in ((0, 0), (1, cols - 1)):
        kind = take(rock, c)
        input_pack[i, PERM] = lookup(kind, perm_table)
        input_pack[i, DTP] = TIME_STEP / lookup(kind, poro_table)
    fill_row(0)
    fill_row(rows - 1)
    loads[0].wait()
    loads[2].wait()
    for i, c in ((0, 0), (1, cols - 1)):
        input_pack[i, SAT] = take(sat, c)
        input_pack[i, PRS] = take(prs, c)

    def face_copy(e, d):
        if e == INPUT:
            if d < 2:
                src = inp.at[:, pl.ds(0 if d == LO_X else cells - cols, cols), :]
                dst = input_x.at[1 - d]
            else:
                src, dst = input_pack.at[d - 2], input_y.at[3 - d]
        else:
            if d < 2:
                at = pl.ds(0 if d == LO_X else cells - cols, cols)
                src = moved.at[at, :] if e == MOVED else pack_x.at[e - BASE, d]
                dst = halo_x.at[e - 1, 1 - d]
            else:
                src, dst = pack_y.at[e - 1, d - 2], halo_y.at[e - 1, 3 - d]
        return pltpu.make_async_remote_copy(
            src_ref=src,
            dst_ref=dst,
            send_sem=face_send.at[d],
            recv_sem=face_recv.at[e % 2, d],
            device_id=neighbours[d],
            device_id_type=MESH,
        )

    def send_faces(e):
        for d in (LO_Y, HI_Y, LO_X, HI_X):

            @pl.when(sends[d])
            def _():
                if e > 0:
                    face_copy(e - 1, d).wait_send()
                face_copy(e, d).start()

    def take_faces(e):
        for d in range(4):
            pl.when(hears[d])(lambda: face_copy(e, d).wait_recv())

    class Group:
        def __init__(self, k, peers, slots):
            self.k, self.peers, self.slots = k, peers, slots

        def copy(self, src, dst, peer):
            return pltpu.make_async_remote_copy(
                src_ref=src,
                dst_ref=dst,
                send_sem=group_send.at[self.k],
                recv_sem=group_recv.at[self.k],
                device_id=peer,
                device_id_type=MESH,
            )

        def start(self, src):
            for i, peer in enumerate(self.peers):
                self.copy(src, self.slots.at[i], peer).start()

        def whole(self):
            held = self.slots.at[pl.ds(0, len(self.peers))]
            return self.copy(held, held, self.peers[0])

        def take(self, mine):
            self.whole().wait_recv()
            self.slots[len(self.peers)] = mine
            return self.slots[...]

    line = Group(0, line_peers, slot_w)
    sides = Group(1, side_peers, slot_v)
    scale_x = Group(2, x_peers, slot_x)
    scale_y = Group(3, y_peers, slot_y)
    scale_z = Group(4, z_peers, slot_s)
    sum_plane = Group(5, plane_peers, slot_a)
    sum_z = Group(6, z_peers, slot_b)
    groups = (line, sides, scale_x, scale_y, scale_z, sum_plane, sum_z)

    pl.semaphore_wait(barrier, len(plane_peers) + len(line_peers) + len(z_peers))
    send_faces(INPUT)

    lane = lax.broadcasted_iota(jnp.int32, (1, 128), 1)
    well_row = jnp.full((1, 128), -9, jnp.int32)
    well_layer = jnp.full((1, 128), -9, jnp.int32)
    pressure_row = jnp.zeros((1, 128), jnp.float32)
    rate_row = jnp.zeros((1, 128), jnp.float32)
    wide = cols + 16
    spread = lax.broadcasted_iota(jnp.int32, (wide, perfs), 0) - lax.broadcasted_iota(
        jnp.int32, (wide, perfs), 1
    )
    lane_wide = lax.broadcasted_iota(jnp.int32, (wide, 128), 1)
    column = jnp.zeros((wide, 128), jnp.float32)
    for w in range(producers + injectors):
        produces = w < producers
        cell_ref = pro_cell if produces else inj_cell
        index_ref = pro_index if produces else inj_index
        i = w if produces else w - producers
        cell = cell_ref[i, 0, 0]
        well_row = jnp.where(lane == w, cell // full_cols - gx * rows, well_row)
        well_layer = jnp.where(lane == w, cell_ref[i, 1, 0], well_layer)
        start = cell % full_cols
        offset = spread + (gy * cols - 8 - start)
        hit = jnp.where(
            (offset == 0) | (offset == full_cols) | (offset == -full_cols),
            index_ref[i : i + 1, :],
            0.0,
        )
        column = jnp.where(lane_wide == w, jnp.sum(hit, axis=1, keepdims=True), column)
        if produces:
            pressure_row = jnp.where(lane == w, pro_pressure[i], pressure_row)
        else:
            rate_row = jnp.where(lane == w, inj_rate[i], rate_row)
    is_producer = jnp.where(lane < producers, 1.0, 0.0)
    layer_pos = lax.broadcasted_iota(jnp.int32, (layers, 128), 0)
    spots[...] = jnp.where(layer_pos == well_layer, 1.0, 0.0)
    own_column = column[8 : 8 + cols]
    for x in range(rows):
        select[x * cols : (x + 1) * cols, :] = jnp.where(well_row == x, own_column, 0.0)
    select[cells : cells + cols, :] = jnp.where(well_row == -1, own_column, 0.0)
    select[cells + cols : cells + 2 * cols, :] = jnp.where(well_row == rows, own_column, 0.0)
    row_pos = lax.broadcasted_iota(jnp.int32, (rows, 128), 0)
    rim_y = cells + 2 * cols
    select[rim_y : rim_y + rows, :] = jnp.where(row_pos == well_row, column[7:8], 0.0)
    select[rim_y + rows : rim_y + 2 * rows, :] = jnp.where(
        row_pos == well_row, column[8 + cols : 9 + cols], 0.0
    )

    pl.loop(1, rows - 1)(fill_row)

    def mobility(s):
        water = 2.0 * s * s
        rest = 1.0 - s
        return water, water + rest * rest

    @pl.loop(0, rows)
    def _(x):
        water, t = mobility(sat[row(x), :])
        mob[row(x), :] = t
        frac[row(x), :] = water / t

    picked = jnp.dot(
        mob[...], spots[...], precision=HIGHEST, preferred_element_type=jnp.float32
    )
    own[0] = jnp.sum(picked * select[pl.ds(0, cells), :], axis=0, keepdims=True)
    line.start(own.at[0])

    lane_z = lax.broadcasted_iota(jnp.int32, (cols, layers), 1)
    col_y = lax.broadcasted_iota(jnp.int32, (cols, layers), 0)
    inner_z = lane_z < layers - 1
    inner_y = col_y < cols - 1

    def next_y(v):
        return pltpu.roll(v, cols - 1, 0)

    def last_y(v):
        return pltpu.roll(v, 1, 0)

    def next_z(v):
        return pltpu.roll(v, layers - 1, 1)

    def last_z(v):
        return pltpu.roll(v, 1, 1)

    def place(chosen, weights):
        return lax.dot_general(
            chosen,
            spots[...] * weights,
            (((1,), (1,)), ((), ())),
            precision=HIGHEST,
            preferred_element_type=jnp.float32,
        )

    loads[3].wait()
    largest = jnp.zeros((1, 128), jnp.float32)
    for b in range(blocks):
        lower = fac[b]
        gram = lax.dot_general(
            lower,
            lower,
            (((0,), (0,)), ((), ())),
            precision=HIGHEST,
            preferred_element_type=jnp.float32,
        )
        high = gram.astype(jnp.bfloat16)
        prod_hi[b] = high
        prod_lo[b] = (gram - high.astype(jnp.float32)).astype(jnp.bfloat16)
        row_sum = jnp.sum(jnp.abs(gram), axis=0, keepdims=True)
        largest = jnp.maximum(largest, jnp.max(row_sum, axis=1, keepdims=True))
    own[1] = largest
    scale_x.start(own.at[1])

    well_d[...] = place(select[pl.ds(0, cells), :], is_producer)
    well_e[...] = place(select[pl.ds(0, cells), :], pressure_row)

    zero_row = jnp.zeros((cols, layers), jnp.float32)

    def flux_row(x, flux_last):
        here, there = row(x), row(jnp.minimum(x + 1, rows - 1))
        k, p, f = perm[here, :], prs[here, :], frac[here, :]
        kx, px, fx = perm[there, :], prs[there, :], frac[there, :]
        tx = harmonic(k, kx)
        ty = jnp.where(inner_y, harmonic(k, next_y(k)), 0.0)
        tz = jnp.where(inner_z, 0.1 * harmonic(k, next_z(k)), 0.0)
        face_x[here, :] = tx
        face_y[here, :] = ty
        face_z[here, :] = tz
        wx = upwind(tx, p, px, f, fx)
        wy = upwind(ty, p, next_y(p), f, next_y(f))
        wz = upwind(tz, p, next_z(p), f, next_z(f))
        s = sat[here, :]
        made = 2.0 * s * s * (p * well_d[here, :] - well_e[here, :])
        moved[here, :] = s - dtp[here, :] * (
            made + (wx - flux_last) + (wy - last_y(wy)) + (wz - last_z(wz))
        )
        return wx

    lax.fori_loop(0, rows, flux_row, zero_row)

    def fraction(s):
        water, t = mobility(s)
        return water / t

    first, final = pl.ds(0, cols), pl.ds(cells - cols, cols)
    take_faces(INPUT)
    t = harmonic(input_x[0, PERM], perm[first, :])
    low_x[...] = t
    moved[first, :] += dtp[first, :] * upwind(
        t, input_x[0, PRS], prs[first, :], fraction(input_x[0, SAT]), frac[first, :]
    )
    t = harmonic(perm[final, :], input_x[1, PERM])
    face_x[final, :] = t
    moved[final, :] -= dtp[final, :] * upwind(
        t, prs[final, :], input_x[1, PRS], frac[final, :], fraction(input_x[1, SAT])
    )
    pack, rim = input_pack, input_y
    t = harmonic(rim[0, PERM], pack[0, PERM])
    side_y[0] = t
    flux = upwind(t, rim[0, PRS], pack[0, PRS], fraction(rim[0, SAT]), fraction(pack[0, SAT]))
    add_to(moved, 0, pack[0, DTP] * flux)
    t = harmonic(pack[1, PERM], rim[1, PERM])
    side_y[1] = t
    flux = upwind(t, pack[1, PRS], rim[1, PRS], fraction(pack[1, SAT]), fraction(rim[1, SAT]))
    add_to(moved, cols - 1, -pack[1, DTP] * flux)
    for i, c in ((0, 0), (1, cols - 1)):
        pack_y[MOVED - 1, i] = take(moved, c)
    send_faces(MOVED)
    own[3] = jnp.sum(line.take(own[0]), axis=0)
    sides.start(own.at[3])

    own[2] = jnp.max(scale_x.take(own[1]), axis=0)
    scale_y.start(own.at[2])
    sums = jnp.sum(sides.take(own[3]), axis=0)
    scale = jnp.where(sums > 0.0, rate_row / jnp.where(sums > 0.0, sums, 1.0), 0.0)
    source[...] = place(select[...], scale)

    @pl.loop(0, rows)
    def _(x):
        here = row(x)
        made = mob[here, :] * source[here, :]
        s = moved[here, :] + dtp[here, :] * made
        satn[here, :] = s
        resid[here, :] = made
        total[here, :] = mobility(s)[1]

    store_satn = pltpu.make_async_copy(satn, satn_out, store_sem.at[0])
    store_satn.start()

    def residual_row(x, flux_last):
        here, there = row(x), row(jnp.minimum(x + 1, rows - 1))
        t, tx = total[here, :], total[there, :]
        p, px = prs[here, :], prs[there, :]
        cx = face_x[here, :] * (0.5 * (t + tx))
        cy = face_y[here, :] * (0.5 * (t + next_y(t)))
        cz = face_z[here, :] * (0.5 * (t + next_z(t)))

        @pl.when(x < rows - 1)
        def _():
            face_x[here, :] = cx

        face_y[here, :] = cy
        face_z[here, :] = cz
        d, e = well_d[here, :], well_e[here, :]
        diag[here, :] = poro[here, :] + d * t
        fx = cx * (p - px)
        fy = cy * (p - next_y(p))
        fz = cz * (p - next_z(p))
        resid[here, :] = (
            resid[here, :]
            + t * (e - d * p)
            - ((fx - flux_last) + (fy - last_y(fy)) + (fz - last_z(fz)))
        )
        return fx

    lax.fori_loop(0, rows, residual_row, zero_row)

    def rim_total(before, sat_rim, dtp_rim, weights):
        s = before + dtp_rim * (mobility(sat_rim)[1] * weights)
        return mobility(s)[1]

    pack_total = [take(total, 0), take(total, cols - 1)]
    edge = []
    take_faces(MOVED)
    t = rim_total(
        halo_x[MOVED - 1, 0], input_x[0, SAT], input_x[0, DTP], source[pl.ds(cells, cols), :]
    )
    c = low_x[...] * (0.5 * (total[first, :] + t))
    low_x[...] = c
    resid[first, :] -= c * (prs[first, :] - input_x[0, PRS])
    t = rim_total(
        halo_x[MOVED - 1, 1],
        input_x[1, SAT],
        input_x[1, DTP],
        source[pl.ds(cells + cols, cols), :],
    )
    c = face_x[final, :] * (0.5 * (total[final, :] + t))
    face_x[final, :] = c
    resid[final, :] -= c * (prs[final, :] - input_x[1, PRS])
    for i, at in ((0, 0), (1, cols - 1)):
        t = rim_total(
            halo_y[MOVED - 1, i],
            rim[i, SAT],
            rim[i, DTP],
            source[pl.ds(rim_y + i * rows, rows), :],
        )
        c = side_y[i] * (0.5 * (pack_total[i] + t))
        side_y[i] = c
        edge.append(take(resid, at) - c * (pack[i, PRS] - rim[i, PRS]))
        put(resid, at, edge[i])

    def apply(v, b, factor):
        if factor is not None:
            v = v * factor
        high = v.astype(jnp.bfloat16)
        low = (v - high.astype(jnp.float32)).astype(jnp.bfloat16)
        z = jnp.dot(high, prod_hi[b], preferred_element_type=jnp.float32)
        z += jnp.dot(high, prod_lo[b], preferred_element_type=jnp.float32)
        return z + jnp.dot(low, prod_hi[b], preferred_element_type=jnp.float32)

    def precondition(src, dst, factor):
        for b in range(blocks):
            parts = [
                src[pl.ds(x * cols + b * BLOCK, BLOCK), :] for x in range(rows)
            ]
            z = apply(jnp.concatenate(parts, axis=0), b, factor)
            for x in range(rows):
                dst[pl.ds(x * cols + b * BLOCK, BLOCK), :] = z[x * BLOCK : (x + 1) * BLOCK]

    def precondition_rim(k, src, low_column, high_column, factor):
        for b in range(blocks):
            here = pl.ds(b * BLOCK, BLOCK)
            parts = [src[here, :], src[pl.ds(cells - cols + b * BLOCK, BLOCK), :]]
            if b == 0:
                parts.append(low_column)
            if b == blocks - 1:
                parts.append(high_column)
            z = apply(jnp.concatenate(parts, axis=0), b, factor)
            pack_x[k, 0, here, :] = z[:BLOCK]
            pack_x[k, 1, here, :] = z[BLOCK : 2 * BLOCK]
            if b == 0:
                pack_y[BASE - 1 + k, 0] = z[2 * BLOCK : 2 * BLOCK + rows]
            if b == blocks - 1:
                pack_y[BASE - 1 + k, 1] = z[-rows:]

    stores = [store_satn]
    for k in range(BASIS):
        e = BASE + k
        vec, img = base.at[k], image.at[k]
        if k == 1:
            top = jnp.max(scale_z.take(own[4]), axis=0)
            norm = jnp.concatenate([1.0 / top] * (layers // 128), axis=1)
        factor = (lambda: None, lambda: (SHIFT * norm) * norm, lambda: SHIFT * norm)[k]()
        prior = resid if k == 0 else image.at[k - 1]
        precondition_rim(k, prior, edge[0], edge[1], factor)
        send_faces(e)
        if k == 0:
            own[4] = jnp.max(scale_y.take(own[2]), axis=0)
            scale_z.start(own.at[4])
        precondition(prior, vec, factor)
        store = pltpu.make_async_copy(
            vec, (z0_out, z1_out, z2_out)[k], store_sem.at[1 + k]
        )
        store.start()
        stores.append(store)

        def image_row(x, flux_last, vec=vec, img=img):
            here, there = row(x), row(jnp.minimum(x + 1, rows - 1))
            v, vx = vec[here, :], vec[there, :]
            fx = face_x[here, :] * (v - vx)
            fy = face_y[here, :] * (v - next_y(v))
            fz = face_z[here, :] * (v - next_z(v))
            img[here, :] = (
                diag[here, :] * v
                + (fx - flux_last)
                + (fy - last_y(fy))
                + (fz - last_z(fz))
            )
            return fx

        lax.fori_loop(0, rows, image_row, zero_row)
        take_faces(e)
        h = e - 1
        img[first, :] += low_x[...] * (vec[first, :] - halo_x[h, 0])
        img[final, :] += face_x[final, :] * (vec[final, :] - halo_x[h, 1])
        for i, at in ((0, 0), (1, cols - 1)):
            edge[i] = take(img, at) + side_y[i] * (pack_y[h, i] - halo_y[h, i])
            put(img, at, edge[i])

    pairs = [(0, 0), (1, 0), (1, 1), (2, 0), (2, 1), (2, 2)]

    def dots_row(x, sums):
        here = row(x)
        v = [base[k, here, :] for k in range(BASIS)]
        u = [image[k, here, :] for k in range(BASIS)]
        r = resid[here, :]
        terms = [v[i] * u[j] for i, j in pairs] + [v[i] * r for i in range(BASIS)]
        out = []
        for s, term in zip(sums, terms):
            for i in range(cols // 8):
                s = s + term[8 * i : 8 * i + 8]
            out.append(s)
        return tuple(out)

    zero_sum = jnp.zeros((8, layers), jnp.float32)
    count = len(pairs) + BASIS
    sums = lax.fori_loop(0, rows, dots_row, (zero_sum,) * count)
    message = jnp.zeros((1, 128), jnp.float32)
    for i, s in enumerate(sums):
        s = jnp.sum(s, axis=0, keepdims=True)
        message = jnp.where(lane == i, jnp.sum(s, axis=1, keepdims=True), message)
    own[5] = message
    sum_plane.start(own.at[5])
    own[6] = jnp.sum(sum_plane.take(own[5]), axis=0)
    sum_z.start(own.at[6])
    result = jnp.sum(sum_z.take(own[6]), axis=0)
    val = [result[:, i : i + 1] for i in range(count)]
    g00, g10, g11, g20, g21, g22, b0, b1, b2 = val

    def ratio(a, b):
        good = b > 0.0
        return jnp.where(good, a / jnp.where(good, b, 1.0), 0.0)

    l10, l20 = ratio(g10, g00), ratio(g20, g00)
    d1 = g11 - l10 * g10
    e21 = g21 - l20 * g10
    l21 = ratio(e21, d1)
    d2 = g22 - l20 * g20 - l21 * e21
    y1 = b1 - l10 * b0
    y2 = b2 - l20 * b0 - l21 * y1
    c2 = ratio(y2, d2)
    c1 = ratio(y1, d1) - l21 * c2
    c0 = ratio(b0, g00) - l10 * c1 - l20 * c2
    for k, c in enumerate((c0, c1, c2)):
        coef_out[k : k + 1, :] = jnp.broadcast_to(c, (1, layers))

    for group in groups:
        group.whole().wait_send()
    for d in range(4):
        pl.when(sends[d])(lambda: face_copy(EXCHANGES - 1, d).wait_send())
    for store in stores:
        store.wait()


def solution(mesh):
    n_gx, n_gy = mesh.shape["gx"], mesh.shape["gy"]

    def per_device(
        rock_type,
        perm_table,
        poro_table,
        saturation,
        pressure_old,
        factor_inverse,
        inject_cells,
        inject_index,
        inject_rate,
        produce_cells,
        produce_index,
        produce_pressure,
    ):
        rows, cols, layers = saturation.shape
        cells = rows * cols
        blocks = cols // BLOCK
        f32, bf16 = jnp.float32, jnp.bfloat16
        flat = (cells, layers)
        field = pltpu.VMEM(flat, f32)
        smem = pl.BlockSpec(memory_space=pltpu.SMEM)
        vmem = pl.BlockSpec(memory_space=pltpu.VMEM)
        hbm = pl.BlockSpec(memory_space=pltpu.HBM)
        out = pl.BlockSpec(memory_space=pl.ANY)
        plane = n_gx * (n_gy // RING)
        dma = pltpu.SemaphoreType.DMA
        scratch = [
            pltpu.VMEM((4,) + flat, f32),
            pltpu.VMEM(flat, jnp.int32),
            pltpu.VMEM((blocks, layers, layers), f32),
            pltpu.VMEM((blocks, layers, layers), bf16),
            pltpu.VMEM((blocks, layers, layers), bf16),
            field,
            field,
            field,
            pltpu.VMEM((cells + 2 * cols + 2 * rows, 128), f32),
            pltpu.VMEM((layers, 128), f32),
            field,
            field,
            field,
            pltpu.VMEM((cols, layers), f32),
            pltpu.VMEM((2, rows, layers), f32),
            field,
            field,
            field,
            pltpu.VMEM((cells + 2 * cols + 2 * rows, layers), f32),
            field,
            field,
            field,
            field,
            pltpu.VMEM((BASIS,) + flat, f32),
            pltpu.VMEM((BASIS,) + flat, f32),
            pltpu.VMEM((2, 4, cols, layers), f32),
            pltpu.VMEM((2, 4, rows, layers), f32),
            pltpu.VMEM((2, 4, rows, layers), f32),
            pltpu.VMEM((EXCHANGES - 1, 2, cols, layers), f32),
            pltpu.VMEM((EXCHANGES - 1, 2, rows, layers), f32),
            pltpu.VMEM((BASIS, 2, cols, layers), f32),
            pltpu.VMEM((EXCHANGES - 1, 2, rows, layers), f32),
            pltpu.VMEM((7, 1, 128), f32),
            pltpu.VMEM((2 * REACH + 1, 1, 128), f32),
            pltpu.VMEM((3, 1, 128), f32),
            pltpu.VMEM((n_gx, 1, 128), f32),
            pltpu.VMEM((n_gy // RING, 1, 128), f32),
            pltpu.VMEM((RING, 1, 128), f32),
            pltpu.VMEM((plane, 1, 128), f32),
            pltpu.VMEM((RING, 1, 128), f32),
            dma((4,)),
            dma((1 + BASIS,)),
            dma((4,)),
            dma((2, 4)),
            dma((7,)),
            dma((7,)),
        ]
        operands = (
            jnp.swapaxes(inject_cells, 1, 2),
            inject_rate,
            jnp.swapaxes(produce_cells, 1, 2),
            produce_pressure,
            perm_table,
            poro_table,
            inject_index,
            produce_index,
            rock_type.reshape(flat),
            saturation.reshape(flat),
            pressure_old.reshape(flat),
            factor_inverse.reshape(blocks, layers, layers),
        )
        satn, z0, z1, z2, coef = pl.pallas_call(
            functools.partial(kernel, (rows, cols, layers, n_gx, n_gy)),
            out_shape=[
                *[jax.ShapeDtypeStruct(flat, f32)] * (1 + BASIS),
                jax.ShapeDtypeStruct((BASIS, layers), f32),
            ],
            in_specs=[smem] * 6 + [vmem] * 2 + [hbm] * 4,
            out_specs=[out] * (1 + BASIS) + [vmem],
            scratch_shapes=scratch,
            compiler_params=pltpu.CompilerParams(
                collective_id=0, has_side_effects=True, vmem_limit_bytes=24 * 1024 * 1024
            ),
            name="reservoir_step",
        )(*(pltpu.with_memory_space_constraint(a, pltpu.HBM) for a in operands))
        change = coef[0:1] * z0 + coef[1:2] * z1 + coef[2:3] * z2
        pressure = pressure_old.reshape(flat) + change
        return satn.reshape(saturation.shape), pressure.reshape(saturation.shape)

    grid = P("gx", "gy", None)
    in_specs = (grid, P(), P(), grid, grid, P("gx", "gy", None, None)) + (P(),) * 6
    return jax.shard_map(
        per_device, mesh=mesh, in_specs=in_specs, out_specs=(grid, grid), check_vma=False
    )
```

```python
import functools

import jax
import jax.numpy as jnp
from jax import lax
from jax.experimental import pallas as pl
from jax.experimental.pallas import tpu as pltpu
from jax.sharding import PartitionSpec as P

MESH = pl.DeviceIdType.MESH
BLOCK = 16
BASIS = 3
UNROLL = 4
RING = 8
TIME_STEP = 0.002
SHIFT = 2.0**-14

INPUT, MOVED, BASE = 0, 1, 2
EXCHANGES = BASE + BASIS
SAT, PRS, PERM, DTP = 0, 1, 2, 3
LO_X, HI_X, LO_Y, HI_Y = 0, 1, 2, 3
REACH = 5
FAR_X = (4, 3, 5, 2, 6, 1, 7)
FAR_Y = (2, 1, 3)
FAR_Z = (4, 3, 5, 2, 6, 1, 7)


def harmonic(former, latter):
    return 2.0 * former * latter / (former + latter)


def upwind(face, p_a, p_b, f_a, f_b):
    flow = face * (p_a - p_b)
    return flow * jnp.where(flow > 0.0, f_a, f_b)


def kernel(
    sizes,
    inj_cell,
    inj_rate,
    pro_cell,
    pro_pressure,
    perm_table,
    poro_table,
    inj_index,
    pro_index,
    rock_hbm,
    sat_hbm,
    prs_hbm,
    fac_hbm,
    satn_out,
    z0_out,
    z1_out,
    z2_out,
    coef_out,
    inp,
    rock,
    fac,
    prod_hi,
    prod_lo,
    poro,
    frac,
    mob,
    select,
    spots,
    face_x,
    face_y,
    face_z,
    low_x,
    high_x,
    side_y,
    moved,
    well_d,
    well_e,
    source,
    satn,
    total,
    diag,
    resid,
    base,
    image,
    input_x,
    input_y,
    input_pack,
    halo_x,
    halo_y,
    pack_x,
    pack_y,
    own,
    slot_w,
    slot_x,
    slot_y,
    slot_s,
    slot_a,
    slot_b,
    load_sem,
    store_sem,
    face_send,
    face_recv,
    group_send,
    group_recv,
):
    rows, cols, layers, n_gx, n_gy = sizes
    blocks = cols // BLOCK
    cells = rows * cols
    full_cols = cols * n_gy
    n_y = n_gy // RING
    plane = n_gx * n_y
    injectors = inj_index.shape[0]
    producers = pro_index.shape[0]
    perfs = inj_index.shape[1]
    sat, prs, perm, dtp = (inp.at[i] for i in range(4))

    gx = lax.axis_index("gx")
    gy = lax.axis_index("gy")
    yy = gy // RING
    zz = gy % RING
    spot_a = gx * n_y + yy

    def row(x):
        return pl.ds(pl.multiple_of(x * cols, cols), cols)

    def take(ref, c):
        parts = [ref[pl.ds(x * cols + c, 1), :] for x in range(rows)]
        return jnp.concatenate(parts, axis=0)

    def add_to(ref, c, value):
        for x in range(rows):
            ref[pl.ds(x * cols + c, 1), :] += value[x : x + 1]

    def put(ref, c, value):
        for x in range(rows):
            ref[pl.ds(x * cols + c, 1), :] = value[x : x + 1]

    neighbours = (
        (lax.rem(gx + n_gx - 1, n_gx), gy),
        (lax.rem(gx + 1, n_gx), gy),
        (gx, lax.rem(gy + n_gy - 1, n_gy)),
        (gx, lax.rem(gy + 1, n_gy)),
    )
    sends = (gx > 0, gx < n_gx - 1, gy > 0, gy < n_gy - 1)
    hears = (gx < n_gx - 1, gx > 0, gy < n_gy - 1, gy > 0)

    def near(a, b, c=0):
        y = lax.rem(yy + b, n_y) if b else yy
        z = lax.rem(zz + c, RING) if c else zz
        return (lax.rem(gx + a, n_gx) if a else gx, y * RING + z)

    def line(a, b):
        return (lax.rem(gx + n_gx + a, n_gx), lax.rem(gy + n_gy + b, n_gy))

    reach = [b for d in range(REACH, 0, -1) for b in (d, -d)] + [0]
    window_peers = [line(a, b) for b in reach for a in (-1, 1, 0) if a or b]
    x_peers = [near(a, 0) for a in FAR_X]
    y_peers = [near(0, b) for b in FAR_Y]
    z_peers = [near(0, 0, c) for c in FAR_Z]
    plane_peers = [near(a, b) for a in FAR_X + (0,) for b in FAR_Y + (0,) if a or b]

    def each_row(body, carry=None):
        def step(i, kept):
            for j in range(UNROLL):
                kept = body(i * UNROLL + j, kept)
            return kept

        if carry is None:
            pl.loop(0, rows // UNROLL)(lambda i: step(i, None) and None)
        else:
            lax.fori_loop(0, rows // UNROLL, step, carry)

    def split(v):
        high = v.astype(jnp.bfloat16)
        return high, (v - high.astype(jnp.float32)).astype(jnp.bfloat16)

    def product(a, b, dims):
        return lax.dot_general(a, b, (dims, ((), ())), preferred_element_type=jnp.float32)

    loads = [
        pltpu.make_async_copy(src, dst, load_sem.at[i])
        for i, (src, dst) in enumerate(
            ((sat_hbm, sat), (rock_hbm, rock), (prs_hbm, prs), (fac_hbm, fac))
        )
    ]
    for load in loads:
        load.start()

    barrier = pltpu.get_barrier_semaphore()

    def greet(peer):
        pl.semaphore_signal(barrier, inc=1, device_id=peer, device_id_type=MESH)

    for peer in plane_peers + window_peers + z_peers:
        greet(peer)

    def clear_x(at):
        input_x[at] = jnp.zeros(input_x.shape[1:], jnp.float32)
        for e in range(EXCHANGES - 1):
            halo_x[e, at] = jnp.zeros(halo_x.shape[2:], jnp.float32)

    def clear_y(at):
        input_y[at] = jnp.zeros(input_y.shape[1:], jnp.float32)
        for e in range(EXCHANGES - 1):
            halo_y[e, at] = jnp.zeros(halo_y.shape[2:], jnp.float32)

    pl.when(gx == 0)(lambda: clear_x(0))
    pl.when(gx == n_gx - 1)(lambda: clear_x(1))
    pl.when(gy == 0)(lambda: clear_y(0))
    pl.when(gy == n_gy - 1)(lambda: clear_y(1))

    def lookup(kind, table):
        bit0 = (kind & 1) == 1
        bit1 = (kind & 2) == 2
        pairs = [jnp.where(bit0, table[2 * i + 1], table[2 * i]) for i in range(4)]
        high = jnp.where(bit1, pairs[3], pairs[2])
        return jnp.where(kind >= 4, high, jnp.where(bit1, pairs[1], pairs[0]))

    def fill_row(x, _=None):
        kind = rock[row(x), :]
        perm[row(x), :] = lookup(kind, perm_table)
        porosity = lookup(kind, poro_table)
        poro[row(x), :] = porosity
        dtp[row(x), :] = TIME_STEP / porosity

    loads[1].wait()
    for i, c in ((0, 0), (1, cols - 1)):
        kind = take(rock, c)
        input_pack[i, PERM] = lookup(kind, perm_table)
        input_pack[i, DTP] = TIME_STEP / lookup(kind, poro_table)
    fill_row(0)
    fill_row(rows - 1)
    loads[0].wait()
    loads[2].wait()
    for i, c in ((0, 0), (1, cols - 1)):
        input_pack[i, SAT] = take(sat, c)
        input_pack[i, PRS] = take(prs, c)

    def face_copy(e, d):
        if e == INPUT:
            if d < 2:
                src = inp.at[:, pl.ds(0 if d == LO_X else cells - cols, cols), :]
                dst = input_x.at[1 - d]
            else:
                src, dst = input_pack.at[d - 2], input_y.at[3 - d]
        else:
            if d < 2:
                at = pl.ds(0 if d == LO_X else cells - cols, cols)
                src = moved.at[at, :] if e == MOVED else pack_x.at[e - BASE, d]
                dst = halo_x.at[e - 1, 1 - d]
            else:
                src, dst = pack_y.at[e - 1, d - 2], halo_y.at[e - 1, 3 - d]
        return pltpu.make_async_remote_copy(
            src_ref=src,
            dst_ref=dst,
            send_sem=face_send.at[d],
            recv_sem=face_recv.at[e % 2, d],
            device_id=neighbours[d],
            device_id_type=MESH,
        )

    def send_faces(e):
        for d in (LO_Y, HI_Y, LO_X, HI_X):

            @pl.when(sends[d])
            def _():
                if e > 0:
                    face_copy(e - 1, d).wait_send()
                face_copy(e, d).start()

    def take_faces(e):
        for d in range(4):
            pl.when(hears[d])(lambda: face_copy(e, d).wait_recv())

    class Group:
        def __init__(self, k, peers, slots):
            self.k, self.peers, self.slots = k, peers, slots

        def copy(self, src, dst, peer):
            return pltpu.make_async_remote_copy(
                src_ref=src,
                dst_ref=dst,
                send_sem=group_send.at[self.k],
                recv_sem=group_recv.at[self.k],
                device_id=peer,
                device_id_type=MESH,
            )

        def start(self, src):
            for i, peer in enumerate(self.peers):
                self.copy(src, self.slots.at[i], peer).start()

        def whole(self):
            held = self.slots.at[pl.ds(0, len(self.peers))]
            return self.copy(held, held, self.peers[0])

        def take(self, mine):
            self.whole().wait_recv()
            self.slots[len(self.peers)] = mine
            return self.slots[...]

    window = Group(0, window_peers, slot_w)
    scale_x = Group(1, x_peers, slot_x)
    scale_y = Group(2, y_peers, slot_y)
    scale_z = Group(3, z_peers, slot_s)
    sum_plane = Group(4, plane_peers, slot_a)
    sum_z = Group(5, z_peers, slot_b)
    groups = (window, scale_x, scale_y, scale_z, sum_plane, sum_z)

    pl.semaphore_wait(barrier, len(plane_peers) + len(window_peers) + len(z_peers))
    send_faces(INPUT)

    lane = lax.broadcasted_iota(jnp.int32, (1, 128), 1)
    well_row = jnp.full((1, 128), -9, jnp.int32)
    well_layer = jnp.full((1, 128), -9, jnp.int32)
    pressure_row = jnp.zeros((1, 128), jnp.float32)
    rate_row = jnp.zeros((1, 128), jnp.float32)
    wide = cols + 16
    spread = lax.broadcasted_iota(jnp.int32, (wide, perfs), 0) - lax.broadcasted_iota(
        jnp.int32, (wide, perfs), 1
    )
    lane_wide = lax.broadcasted_iota(jnp.int32, (wide, 128), 1)
    column = jnp.zeros((wide, 128), jnp.float32)
    for w in range(producers + injectors):
        produces = w < producers
        cell_ref = pro_cell if produces else inj_cell
        index_ref = pro_index if produces else inj_index
        i = w if produces else w - producers
        cell = cell_ref[i, 0, 0]
        well_row = jnp.where(lane == w, cell // full_cols - gx * rows, well_row)
        well_layer = jnp.where(lane == w, cell_ref[i, 1, 0], well_layer)
        start = cell % full_cols
        offset = spread + (gy * cols - 8 - start)
        hit = jnp.where(
            (offset == 0) | (offset == full_cols) | (offset == -full_cols),
            index_ref[i : i + 1, :],
            0.0,
        )
        column = jnp.where(lane_wide == w, jnp.sum(hit, axis=1, keepdims=True), column)
        if produces:
            pressure_row = jnp.where(lane == w, pro_pressure[i], pressure_row)
        else:
            rate_row = jnp.where(lane == w, inj_rate[i], rate_row)
    is_producer = jnp.where(lane < producers, 1.0, 0.0)
    layer_pos = lax.broadcasted_iota(jnp.int32, (layers, 128), 0)
    spots[...] = jnp.where(layer_pos == well_layer, 1.0, 0.0).astype(jnp.bfloat16)
    own_column = column[8 : 8 + cols]
    for x in range(rows):
        select[x * cols : (x + 1) * cols, :] = jnp.where(well_row == x, own_column, 0.0)
    select[cells : cells + cols, :] = jnp.where(well_row == -1, own_column, 0.0)
    select[cells + cols : cells + 2 * cols, :] = jnp.where(well_row == rows, own_column, 0.0)
    row_pos = lax.broadcasted_iota(jnp.int32, (rows, 128), 0)
    rim_y = cells + 2 * cols
    select[rim_y : rim_y + rows, :] = jnp.where(row_pos == well_row, column[7:8], 0.0)
    select[rim_y + rows : rim_y + 2 * rows, :] = jnp.where(
        row_pos == well_row, column[8 + cols : 9 + cols], 0.0
    )


    def mobility(s):
        water = 2.0 * s * s
        rest = 1.0 - s
        return water, water + rest * rest

    def mobility_row(x, _):
        water, t = mobility(sat[row(x), :])
        mob[row(x), :] = t
        frac[row(x), :] = water / t

    each_row(mobility_row)
    spot = spots[...]
    picked = sum(product(v, spot, ((1,), (0,))) for v in split(mob[...]))
    own[0] = jnp.sum(picked * select[pl.ds(0, cells), :], axis=0, keepdims=True)
    window.start(own.at[0])

    lane_z = lax.broadcasted_iota(jnp.int32, (cols, layers), 1)
    col_y = lax.broadcasted_iota(jnp.int32, (cols, layers), 0)
    inner_z = lane_z < layers - 1
    inner_y = col_y < cols - 1

    def next_y(v):
        return pltpu.roll(v, cols - 1, 0)

    def last_y(v):
        return pltpu.roll(v, 1, 0)

    def next_z(v):
        return pltpu.roll(v, layers - 1, 1)

    def last_z(v):
        return pltpu.roll(v, 1, 1)

    def place(chosen):
        return sum(product(v, spot, ((1,), (1,))) for v in split(chosen))

    loads[3].wait()
    largest = jnp.zeros((1, 128), jnp.float32)
    for b in range(blocks):
        lower = fac[b]
        high, low = split(lower)
        over = ((0,), (0,))
        gram = product(high, high, over) + product(high, low, over) + product(low, high, over)
        prod_hi[b], prod_lo[b] = split(gram)
        row_sum = jnp.sum(jnp.abs(gram), axis=0, keepdims=True)
        largest = jnp.maximum(largest, jnp.max(row_sum, axis=1, keepdims=True))
    own[1] = largest
    scale_x.start(own.at[1])

    for x in range(1, rows - 1):
        fill_row(x)
    chosen = select[pl.ds(0, cells), :]
    well_d[...] = place(chosen * is_producer)
    well_e[...] = place(chosen * pressure_row)

    zero_row = jnp.zeros((cols, layers), jnp.float32)

    def flux_row(x, flux_last):
        here, there = row(x), row(jnp.minimum(x + 1, rows - 1))
        k, p, f = perm[here, :], prs[here, :], frac[here, :]
        kx, px, fx = perm[there, :], prs[there, :], frac[there, :]
        tx = harmonic(k, kx)
        ty = jnp.where(inner_y, harmonic(k, next_y(k)), 0.0)
        tz = jnp.where(inner_z, 0.1 * harmonic(k, next_z(k)), 0.0)
        face_x[here, :] = tx
        face_y[here, :] = ty
        face_z[here, :] = tz
        wx = upwind(tx, p, px, f, fx)
        wy = upwind(ty, p, next_y(p), f, next_y(f))
        wz = upwind(tz, p, next_z(p), f, next_z(f))
        s = sat[here, :]
        made = 2.0 * s * s * (p * well_d[here, :] - well_e[here, :])
        moved[here, :] = s - dtp[here, :] * (
            made + (wx - flux_last) + (wy - last_y(wy)) + (wz - last_z(wz))
        )
        return wx

    each_row(flux_row, zero_row)

    def fraction(s):
        water, t = mobility(s)
        return water / t

    first, final = pl.ds(0, cols), pl.ds(cells - cols, cols)
    take_faces(INPUT)
    t = harmonic(input_x[0, PERM], perm[first, :])
    low_x[...] = t
    moved[first, :] += dtp[first, :] * upwind(
        t, input_x[0, PRS], prs[first, :], fraction(input_x[0, SAT]), frac[first, :]
    )
    t = harmonic(perm[final, :], input_x[1, PERM])
    high_x[...] = t
    moved[final, :] -= dtp[final, :] * upwind(
        t, prs[final, :], input_x[1, PRS], frac[final, :], fraction(input_x[1, SAT])
    )
    pack, rim = input_pack, input_y
    t = harmonic(rim[0, PERM], pack[0, PERM])
    side_y[0] = t
    flux = upwind(t, rim[0, PRS], pack[0, PRS], fraction(rim[0, SAT]), fraction(pack[0, SAT]))
    add_to(moved, 0, pack[0, DTP] * flux)
    t = harmonic(pack[1, PERM], rim[1, PERM])
    side_y[1] = t
    flux = upwind(t, pack[1, PRS], rim[1, PRS], fraction(pack[1, SAT]), fraction(rim[1, SAT]))
    add_to(moved, cols - 1, -pack[1, DTP] * flux)
    for i, c in ((0, 0), (1, cols - 1)):
        pack_y[MOVED - 1, i] = take(moved, c)
    send_faces(MOVED)

    own[2] = jnp.max(scale_x.take(own[1]), axis=0)
    scale_y.start(own.at[2])
    sums = jnp.sum(window.take(own[0]), axis=0)
    scale = jnp.where(sums > 0.0, rate_row / jnp.where(sums > 0.0, sums, 1.0), 0.0)
    source[...] = place(select[...] * scale)

    def moved_row(x, _):
        here = row(x)
        made = mob[here, :] * source[here, :]
        s = moved[here, :] + dtp[here, :] * made
        satn[here, :] = s
        resid[here, :] = made
        total[here, :] = mobility(s)[1]

    each_row(moved_row)

    store_satn = pltpu.make_async_copy(satn, satn_out, store_sem.at[0])
    store_satn.start()

    def residual_row(x, flux_last):
        here, there = row(x), row(jnp.minimum(x + 1, rows - 1))
        t, tx = total[here, :], total[there, :]
        p, px = prs[here, :], prs[there, :]
        cx = face_x[here, :] * (0.5 * (t + tx))
        cy = face_y[here, :] * (0.5 * (t + next_y(t)))
        cz = face_z[here, :] * (0.5 * (t + next_z(t)))
        face_x[here, :] = cx
        face_y[here, :] = cy
        face_z[here, :] = cz
        d, e = well_d[here, :], well_e[here, :]
        diag[here, :] = poro[here, :] + d * t
        fx = cx * (p - px)
        fy = cy * (p - next_y(p))
        fz = cz * (p - next_z(p))
        resid[here, :] = (
            resid[here, :]
            + t * (e - d * p)
            - ((fx - flux_last) + (fy - last_y(fy)) + (fz - last_z(fz)))
        )
        return fx

    each_row(residual_row, zero_row)

    own[4] = jnp.max(scale_y.take(own[2]), axis=0)
    scale_z.start(own.at[4])

    def rim_total(before, sat_rim, dtp_rim, weights):
        s = before + dtp_rim * (mobility(sat_rim)[1] * weights)
        return mobility(s)[1]

    pack_total = [take(total, 0), take(total, cols - 1)]
    edge = []
    take_faces(MOVED)
    t = rim_total(
        halo_x[MOVED - 1, 0], input_x[0, SAT], input_x[0, DTP], source[pl.ds(cells, cols), :]
    )
    c = low_x[...] * (0.5 * (total[first, :] + t))
    low_x[...] = c
    resid[first, :] -= c * (prs[first, :] - input_x[0, PRS])
    t = rim_total(
        halo_x[MOVED - 1, 1],
        input_x[1, SAT],
        input_x[1, DTP],
        source[pl.ds(cells + cols, cols), :],
    )
    c = high_x[...] * (0.5 * (total[final, :] + t))
    high_x[...] = c
    resid[final, :] -= c * (prs[final, :] - input_x[1, PRS])
    for i, at in ((0, 0), (1, cols - 1)):
        t = rim_total(
            halo_y[MOVED - 1, i],
            rim[i, SAT],
            rim[i, DTP],
            source[pl.ds(rim_y + i * rows, rows), :],
        )
        c = side_y[i] * (0.5 * (pack_total[i] + t))
        side_y[i] = c
        edge.append(take(resid, at) - c * (pack[i, PRS] - rim[i, PRS]))
        put(resid, at, edge[i])

    def apply(v, b, factor):
        high, low = split(v if factor is None else v * factor)
        z = jnp.dot(high, prod_hi[b], preferred_element_type=jnp.float32)
        z += jnp.dot(high, prod_lo[b], preferred_element_type=jnp.float32)
        return z + jnp.dot(low, prod_hi[b], preferred_element_type=jnp.float32)

    def precondition(src, dst, factor):
        for b in range(blocks):
            parts = [
                src[pl.ds(x * cols + b * BLOCK, BLOCK), :] for x in range(rows)
            ]
            z = apply(jnp.concatenate(parts, axis=0), b, factor)
            for x in range(rows):
                dst[pl.ds(x * cols + b * BLOCK, BLOCK), :] = z[x * BLOCK : (x + 1) * BLOCK]

    def precondition_rim(k, src, low_column, high_column, factor):
        for b in range(blocks):
            here = pl.ds(b * BLOCK, BLOCK)
            parts = [src[here, :], src[pl.ds(cells - cols + b * BLOCK, BLOCK), :]]
            if b == 0:
                parts.append(low_column)
            if b == blocks - 1:
                parts.append(high_column)
            z = apply(jnp.concatenate(parts, axis=0), b, factor)
            pack_x[k, 0, here, :] = z[:BLOCK]
            pack_x[k, 1, here, :] = z[BLOCK : 2 * BLOCK]
            if b == 0:
                pack_y[BASE - 1 + k, 0] = z[2 * BLOCK : 2 * BLOCK + rows]
            if b == blocks - 1:
                pack_y[BASE - 1 + k, 1] = z[-rows:]

    stores = [store_satn]
    for k in range(BASIS):
        e = BASE + k
        vec, img = base.at[k], image.at[k]
        if k == 1:
            top = jnp.max(scale_z.take(own[4]), axis=0)
            norm = jnp.concatenate([1.0 / top] * (layers // 128), axis=1)
        factor = (lambda: None, lambda: (SHIFT * norm) * norm, lambda: SHIFT * norm)[k]()
        prior = resid if k == 0 else image.at[k - 1]
        precondition_rim(k, prior, edge[0], edge[1], factor)
        send_faces(e)
        precondition(prior, vec, factor)
        store = pltpu.make_async_copy(
            vec, (z0_out, z1_out, z2_out)[k], store_sem.at[1 + k]
        )
        store.start()
        stores.append(store)

        def image_row(x, flux_last, vec=vec, img=img):
            here, there = row(x), row(jnp.minimum(x + 1, rows - 1))
            v, vx = vec[here, :], vec[there, :]
            fx = face_x[here, :] * (v - vx)
            fy = face_y[here, :] * (v - next_y(v))
            fz = face_z[here, :] * (v - next_z(v))
            img[here, :] = (
                diag[here, :] * v
                + (fx - flux_last)
                + (fy - last_y(fy))
                + (fz - last_z(fz))
            )
            return fx

        each_row(image_row, zero_row)
        take_faces(e)
        h = e - 1
        img[first, :] += low_x[...] * (vec[first, :] - halo_x[h, 0])
        img[final, :] += high_x[...] * (vec[final, :] - halo_x[h, 1])
        for i, at in ((0, 0), (1, cols - 1)):
            edge[i] = take(img, at) + side_y[i] * (pack_y[h, i] - halo_y[h, i])
            put(img, at, edge[i])

    pairs = [(0, 0), (1, 0), (1, 1), (2, 0), (2, 1), (2, 2)]

    def dots_row(x, sums):
        here = row(x)
        v = [base[k, here, :] for k in range(BASIS)]
        u = [image[k, here, :] for k in range(BASIS)]
        r = resid[here, :]
        terms = [v[i] * u[j] for i, j in pairs] + [v[i] * r for i in range(BASIS)]
        out = []
        for s, term in zip(sums, terms):
            for i in range(cols // 8):
                s = s + term[8 * i : 8 * i + 8]
            out.append(s)
        return tuple(out)

    zero_sum = jnp.zeros((8, layers), jnp.float32)
    count = len(pairs) + BASIS
    sums = lax.fori_loop(0, rows, dots_row, (zero_sum,) * count)
    message = jnp.zeros((1, 128), jnp.float32)
    for i, s in enumerate(sums):
        s = jnp.sum(s, axis=0, keepdims=True)
        message = jnp.where(lane == i, jnp.sum(s, axis=1, keepdims=True), message)
    own[5] = message
    sum_plane.start(own.at[5])
    own[6] = jnp.sum(sum_plane.take(own[5]), axis=0)
    sum_z.start(own.at[6])
    result = jnp.sum(sum_z.take(own[6]), axis=0)
    val = [result[:, i : i + 1] for i in range(count)]
    g00, g10, g11, g20, g21, g22, b0, b1, b2 = val

    def ratio(a, b):
        good = b > 0.0
        return jnp.where(good, a / jnp.where(good, b, 1.0), 0.0)

    l10, l20 = ratio(g10, g00), ratio(g20, g00)
    d1 = g11 - l10 * g10
    e21 = g21 - l20 * g10
    l21 = ratio(e21, d1)
    d2 = g22 - l20 * g20 - l21 * e21
    y1 = b1 - l10 * b0
    y2 = b2 - l20 * b0 - l21 * y1
    c2 = ratio(y2, d2)
    c1 = ratio(y1, d1) - l21 * c2
    c0 = ratio(b0, g00) - l10 * c1 - l20 * c2
    for k, c in enumerate((c0, c1, c2)):
        coef_out[k : k + 1, :] = jnp.broadcast_to(c, (1, layers))

    for group in groups:
        group.whole().wait_send()
    for d in range(4):
        pl.when(sends[d])(lambda: face_copy(EXCHANGES - 1, d).wait_send())
    for store in stores:
        store.wait()


def solution(mesh):
    n_gx, n_gy = mesh.shape["gx"], mesh.shape["gy"]

    def per_device(
        rock_type,
        perm_table,
        poro_table,
        saturation,
        pressure_old,
        factor_inverse,
        inject_cells,
        inject_index,
        inject_rate,
        produce_cells,
        produce_index,
        produce_pressure,
    ):
        rows, cols, layers = saturation.shape
        cells = rows * cols
        blocks = cols // BLOCK
        f32, bf16 = jnp.float32, jnp.bfloat16
        flat = (cells, layers)
        field = pltpu.VMEM(flat, f32)
        smem = pl.BlockSpec(memory_space=pltpu.SMEM)
        vmem = pl.BlockSpec(memory_space=pltpu.VMEM)
        hbm = pl.BlockSpec(memory_space=pltpu.HBM)
        out = pl.BlockSpec(memory_space=pl.ANY)
        plane = n_gx * (n_gy // RING)
        dma = pltpu.SemaphoreType.DMA
        scratch = [
            pltpu.VMEM((4,) + flat, f32),
            pltpu.VMEM(flat, jnp.int32),
            pltpu.VMEM((blocks, layers, layers), f32),
            pltpu.VMEM((blocks, layers, layers), bf16),
            pltpu.VMEM((blocks, layers, layers), bf16),
            field,
            field,
            field,
            pltpu.VMEM((cells + 2 * cols + 2 * rows, 128), f32),
            pltpu.VMEM((layers, 128), bf16),
            field,
            field,
            field,
            pltpu.VMEM((cols, layers), f32),
            pltpu.VMEM((cols, layers), f32),
            pltpu.VMEM((2, rows, layers), f32),
            field,
            field,
            field,
            pltpu.VMEM((cells + 2 * cols + 2 * rows, layers), f32),
            field,
            field,
            field,
            field,
            pltpu.VMEM((BASIS,) + flat, f32),
            pltpu.VMEM((BASIS,) + flat, f32),
            pltpu.VMEM((2, 4, cols, layers), f32),
            pltpu.VMEM((2, 4, rows, layers), f32),
            pltpu.VMEM((2, 4, rows, layers), f32),
            pltpu.VMEM((EXCHANGES - 1, 2, cols, layers), f32),
            pltpu.VMEM((EXCHANGES - 1, 2, rows, layers), f32),
            pltpu.VMEM((BASIS, 2, cols, layers), f32),
            pltpu.VMEM((EXCHANGES - 1, 2, rows, layers), f32),
            pltpu.VMEM((7, 1, 128), f32),
            pltpu.VMEM((3 * (2 * REACH + 1), 1, 128), f32),
            pltpu.VMEM((n_gx, 1, 128), f32),
            pltpu.VMEM((n_gy // RING, 1, 128), f32),
            pltpu.VMEM((RING, 1, 128), f32),
            pltpu.VMEM((plane, 1, 128), f32),
            pltpu.VMEM((RING, 1, 128), f32),
            dma((4,)),
            dma((1 + BASIS,)),
            dma((4,)),
            dma((2, 4)),
            dma((6,)),
            dma((6,)),
        ]
        operands = (
            jnp.swapaxes(inject_cells, 1, 2),
            inject_rate,
            jnp.swapaxes(produce_cells, 1, 2),
            produce_pressure,
            perm_table,
            poro_table,
            inject_index,
            produce_index,
            rock_type.reshape(flat),
            saturation.reshape(flat),
            pressure_old.reshape(flat),
            factor_inverse.reshape(blocks, layers, layers),
        )
        satn, z0, z1, z2, coef = pl.pallas_call(
            functools.partial(kernel, (rows, cols, layers, n_gx, n_gy)),
            out_shape=[
                *[jax.ShapeDtypeStruct(flat, f32)] * (1 + BASIS),
                jax.ShapeDtypeStruct((BASIS, layers), f32),
            ],
            in_specs=[smem] * 6 + [vmem] * 2 + [hbm] * 4,
            out_specs=[out] * (1 + BASIS) + [vmem],
            scratch_shapes=scratch,
            compiler_params=pltpu.CompilerParams(
                collective_id=0, has_side_effects=True, vmem_limit_bytes=24 * 1024 * 1024
            ),
            name="reservoir_step",
        )(*(pltpu.with_memory_space_constraint(a, pltpu.HBM) for a in operands))
        change = coef[0:1] * z0 + coef[1:2] * z1 + coef[2:3] * z2
        pressure = pressure_old.reshape(flat) + change
        return satn.reshape(saturation.shape), pressure.reshape(saturation.shape)

    grid = P("gx", "gy", None)
    in_specs = (grid, P(), P(), grid, grid, P("gx", "gy", None, None)) + (P(),) * 6
    return jax.shard_map(
        per_device, mesh=mesh, in_specs=in_specs, out_specs=(grid, grid), check_vma=False
    )
```

```python
import functools

import jax
import jax.numpy as jnp
from jax import lax
from jax.experimental import pallas as pl
from jax.experimental.pallas import tpu as pltpu
from jax.sharding import PartitionSpec as P

MESH = pl.DeviceIdType.MESH
BLOCK = 16
BASIS = 3
UNROLL = 4
RING = 8
TIME_STEP = 0.002
SHIFT = 2.0**-14

INPUT, MOVED, BASE = 0, 1, 2
EXCHANGES = BASE + BASIS
SAT, PRS, PERM, DTP = 0, 1, 2, 3
LO_X, HI_X, LO_Y, HI_Y = 0, 1, 2, 3
REACH = 5
FAR_X = (4, 3, 5, 2, 6, 1, 7)
FAR_Y = (2, 1, 3)
FAR_Z = (4, 3, 5, 2, 6, 1, 7)


def harmonic(former, latter):
    return 2.0 * former * latter / (former + latter)


def upwind(face, p_a, p_b, f_a, f_b):
    flow = face * (p_a - p_b)
    return flow * jnp.where(flow > 0.0, f_a, f_b)


def kernel(
    sizes,
    inj_cell,
    inj_rate,
    pro_cell,
    pro_pressure,
    perm_table,
    poro_table,
    inj_index,
    pro_index,
    rock_hbm,
    sat_hbm,
    prs_hbm,
    fac_hbm,
    satn_out,
    z0_out,
    z1_out,
    z2_out,
    coef_out,
    inp,
    rock,
    fac,
    prod_hi,
    prod_lo,
    poro,
    frac,
    mob,
    select,
    spots,
    face_x,
    face_y,
    face_z,
    low_x,
    high_x,
    side_y,
    moved,
    well_d,
    well_e,
    source,
    satn,
    total,
    diag,
    resid,
    base,
    image,
    input_x,
    input_y,
    input_pack,
    halo_x,
    halo_y,
    pack_x,
    pack_y,
    own,
    slot_w,
    slot_x,
    slot_y,
    slot_s,
    slot_a,
    slot_b,
    load_sem,
    store_sem,
    face_send,
    face_recv,
    group_send,
    group_recv,
):
    rows, cols, layers, n_gx, n_gy = sizes
    blocks = cols // BLOCK
    cells = rows * cols
    full_cols = cols * n_gy
    n_y = n_gy // RING
    plane = n_gx * n_y
    injectors = inj_index.shape[0]
    producers = pro_index.shape[0]
    perfs = inj_index.shape[1]
    sat, prs, perm, dtp = (inp.at[i] for i in range(4))

    gx = lax.axis_index("gx")
    gy = lax.axis_index("gy")
    yy = gy // RING
    zz = gy % RING
    spot_a = gx * n_y + yy

    def row(x):
        return pl.ds(pl.multiple_of(x * cols, cols), cols)

    def take(ref, c):
        parts = [ref[pl.ds(x * cols + c, 1), :] for x in range(rows)]
        return jnp.concatenate(parts, axis=0)

    def add_to(ref, c, value):
        for x in range(rows):
            ref[pl.ds(x * cols + c, 1), :] += value[x : x + 1]

    def put(ref, c, value):
        for x in range(rows):
            ref[pl.ds(x * cols + c, 1), :] = value[x : x + 1]

    neighbours = (
        (lax.rem(gx + n_gx - 1, n_gx), gy),
        (lax.rem(gx + 1, n_gx), gy),
        (gx, lax.rem(gy + n_gy - 1, n_gy)),
        (gx, lax.rem(gy + 1, n_gy)),
    )
    sends = (gx > 0, gx < n_gx - 1, gy > 0, gy < n_gy - 1)
    hears = (gx < n_gx - 1, gx > 0, gy < n_gy - 1, gy > 0)

    def near(a, b, c=0):
        y = lax.rem(yy + b, n_y) if b else yy
        z = lax.rem(zz + c, RING) if c else zz
        return (lax.rem(gx + a, n_gx) if a else gx, y * RING + z)

    def line(a, b):
        return (lax.rem(gx + n_gx + a, n_gx), lax.rem(gy + n_gy + b, n_gy))

    reach = [b for d in range(REACH, 0, -1) for b in (d, -d)] + [0]
    window_peers = [line(a, b) for b in reach for a in (-1, 1, 0) if a or b]
    x_peers = [near(a, 0) for a in FAR_X]
    y_peers = [near(0, b) for b in FAR_Y]
    z_peers = [near(0, 0, c) for c in FAR_Z]
    plane_peers = [near(a, b) for a in FAR_X + (0,) for b in FAR_Y + (0,) if a or b]

    def each_row(body, carry=None):
        def step(i, kept):
            for j in range(UNROLL):
                kept = body(i * UNROLL + j, kept)
            return kept

        if carry is None:
            pl.loop(0, rows // UNROLL)(lambda i: step(i, None) and None)
        else:
            carry = lax.fori_loop(0, rows // UNROLL, step, carry)
        return carry

    def split(v):
        high = v.astype(jnp.bfloat16)
        return high, (v - high.astype(jnp.float32)).astype(jnp.bfloat16)

    def product(a, b, dims):
        return lax.dot_general(a, b, (dims, ((), ())), preferred_element_type=jnp.float32)

    loads = [
        pltpu.make_async_copy(src, dst, load_sem.at[i])
        for i, (src, dst) in enumerate(
            ((sat_hbm, sat), (rock_hbm, rock), (prs_hbm, prs), (fac_hbm, fac))
        )
    ]
    for load in loads:
        load.start()

    barrier = pltpu.get_barrier_semaphore()

    def greet(peer):
        pl.semaphore_signal(barrier, inc=1, device_id=peer, device_id_type=MESH)

    for peer in window_peers[::-1] + plane_peers + z_peers:
        greet(peer)

    def clear_x(at):
        input_x[at] = jnp.zeros(input_x.shape[1:], jnp.float32)
        for e in range(EXCHANGES - 1):
            halo_x[e, at] = jnp.zeros(halo_x.shape[2:], jnp.float32)

    def clear_y(at):
        input_y[at] = jnp.zeros(input_y.shape[1:], jnp.float32)
        for e in range(EXCHANGES - 1):
            halo_y[e, at] = jnp.zeros(halo_y.shape[2:], jnp.float32)

    pl.when(gx == 0)(lambda: clear_x(0))
    pl.when(gx == n_gx - 1)(lambda: clear_x(1))
    pl.when(gy == 0)(lambda: clear_y(0))
    pl.when(gy == n_gy - 1)(lambda: clear_y(1))

    def lookup(kind, table):
        bit0 = (kind & 1) == 1
        bit1 = (kind & 2) == 2
        pairs = [jnp.where(bit0, table[2 * i + 1], table[2 * i]) for i in range(4)]
        high = jnp.where(bit1, pairs[3], pairs[2])
        return jnp.where(kind >= 4, high, jnp.where(bit1, pairs[1], pairs[0]))

    def fill_row(x, _=None):
        kind = rock[row(x), :]
        perm[row(x), :] = lookup(kind, perm_table)
        porosity = lookup(kind, poro_table)
        poro[row(x), :] = porosity
        dtp[row(x), :] = TIME_STEP / porosity

    loads[1].wait()
    for i, c in ((0, 0), (1, cols - 1)):
        kind = take(rock, c)
        input_pack[i, PERM] = lookup(kind, perm_table)
        input_pack[i, DTP] = TIME_STEP / lookup(kind, poro_table)
    fill_row(0)
    fill_row(rows - 1)
    loads[0].wait()
    loads[2].wait()
    for i, c in ((0, 0), (1, cols - 1)):
        input_pack[i, SAT] = take(sat, c)
        input_pack[i, PRS] = take(prs, c)

    def face_copy(e, d):
        if e == INPUT:
            if d < 2:
                src = inp.at[:, pl.ds(0 if d == LO_X else cells - cols, cols), :]
                dst = input_x.at[1 - d]
            else:
                src, dst = input_pack.at[d - 2], input_y.at[3 - d]
        else:
            if d < 2:
                at = pl.ds(0 if d == LO_X else cells - cols, cols)
                src = moved.at[at, :] if e == MOVED else pack_x.at[e - BASE, d]
                dst = halo_x.at[e - 1, 1 - d]
            else:
                src, dst = pack_y.at[e - 1, d - 2], halo_y.at[e - 1, 3 - d]
        return pltpu.make_async_remote_copy(
            src_ref=src,
            dst_ref=dst,
            send_sem=face_send.at[d],
            recv_sem=face_recv.at[e % 2, d],
            device_id=neighbours[d],
            device_id_type=MESH,
        )

    def send_faces(e):
        for d in (LO_Y, HI_Y, LO_X, HI_X):

            @pl.when(sends[d])
            def _():
                if e > 0:
                    face_copy(e - 1, d).wait_send()
                face_copy(e, d).start()

    def take_faces(e):
        for d in range(4):
            pl.when(hears[d])(lambda: face_copy(e, d).wait_recv())

    class Group:
        def __init__(self, k, peers, slots):
            self.k, self.peers, self.slots = k, peers, slots

        def copy(self, src, dst, peer):
            return pltpu.make_async_remote_copy(
                src_ref=src,
                dst_ref=dst,
                send_sem=group_send.at[self.k],
                recv_sem=group_recv.at[self.k],
                device_id=peer,
                device_id_type=MESH,
            )

        def start(self, src):
            for i, peer in enumerate(self.peers):
                self.copy(src, self.slots.at[i], peer).start()

        def whole(self):
            held = self.slots.at[pl.ds(0, len(self.peers))]
            return self.copy(held, held, self.peers[0])

        def take(self, mine):
            self.whole().wait_recv()
            self.slots[len(self.peers)] = mine
            return self.slots[...]

    window = Group(0, window_peers, slot_w)
    scale_x = Group(1, x_peers, slot_x)
    scale_y = Group(2, y_peers, slot_y)
    scale_z = Group(3, z_peers, slot_s)
    sum_plane = Group(4, plane_peers, slot_a)
    sum_z = Group(5, z_peers, slot_b)
    groups = (window, scale_x, scale_y, scale_z, sum_plane, sum_z)

    pl.semaphore_wait(barrier, len(plane_peers) + len(window_peers) + len(z_peers))
    send_faces(INPUT)

    lane = lax.broadcasted_iota(jnp.int32, (1, 128), 1)
    well_row = jnp.full((1, 128), -9, jnp.int32)
    well_layer = jnp.full((1, 128), -9, jnp.int32)
    pressure_row = jnp.zeros((1, 128), jnp.float32)
    rate_row = jnp.zeros((1, 128), jnp.float32)
    wide = cols + 16
    spread = lax.broadcasted_iota(jnp.int32, (wide, perfs), 0) - lax.broadcasted_iota(
        jnp.int32, (wide, perfs), 1
    )
    lane_wide = lax.broadcasted_iota(jnp.int32, (wide, 128), 1)
    column = jnp.zeros((wide, 128), jnp.float32)
    for w in range(producers + injectors):
        produces = w < producers
        cell_ref = pro_cell if produces else inj_cell
        index_ref = pro_index if produces else inj_index
        i = w if produces else w - producers
        cell = cell_ref[i, 0, 0]
        well_row = jnp.where(lane == w, cell // full_cols - gx * rows, well_row)
        well_layer = jnp.where(lane == w, cell_ref[i, 1, 0], well_layer)
        start = cell % full_cols
        offset = spread + (gy * cols - 8 - start)
        hit = jnp.where(
            (offset == 0) | (offset == full_cols) | (offset == -full_cols),
            index_ref[i : i + 1, :],
            0.0,
        )
        column = jnp.where(lane_wide == w, jnp.sum(hit, axis=1, keepdims=True), column)
        if produces:
            pressure_row = jnp.where(lane == w, pro_pressure[i], pressure_row)
        else:
            rate_row = jnp.where(lane == w, inj_rate[i], rate_row)
    is_producer = jnp.where(lane < producers, 1.0, 0.0)
    layer_pos = lax.broadcasted_iota(jnp.int32, (layers, 128), 0)
    spots[...] = jnp.where(layer_pos == well_layer, 1.0, 0.0).astype(jnp.bfloat16)
    own_column = column[8 : 8 + cols]
    for x in range(rows):
        select[x * cols : (x + 1) * cols, :] = jnp.where(well_row == x, own_column, 0.0)
    select[cells : cells + cols, :] = jnp.where(well_row == -1, own_column, 0.0)
    select[cells + cols : cells + 2 * cols, :] = jnp.where(well_row == rows, own_column, 0.0)
    row_pos = lax.broadcasted_iota(jnp.int32, (rows, 128), 0)
    rim_y = cells + 2 * cols
    select[rim_y : rim_y + rows, :] = jnp.where(row_pos == well_row, column[7:8], 0.0)
    select[rim_y + rows : rim_y + 2 * rows, :] = jnp.where(
        row_pos == well_row, column[8 + cols : 9 + cols], 0.0
    )


    def mobility(s):
        water = 2.0 * s * s
        rest = 1.0 - s
        return water, water + rest * rest

    def mobility_row(x, _):
        water, t = mobility(sat[row(x), :])
        mob[row(x), :] = t
        frac[row(x), :] = water / t

    each_row(mobility_row)
    spot = spots[...]
    lane_spot = lax.broadcasted_iota(jnp.int32, (layers, 128), 1)
    picked = sum(product(v, spot, ((1,), (0,))) for v in split(mob[...]))
    own[0] = jnp.sum(picked * select[pl.ds(0, cells), :], axis=0, keepdims=True)
    window.start(own.at[0])

    lane_z = lax.broadcasted_iota(jnp.int32, (cols, layers), 1)
    col_y = lax.broadcasted_iota(jnp.int32, (cols, layers), 0)
    inner_z = lane_z < layers - 1
    inner_y = col_y < cols - 1

    def next_y(v):
        return pltpu.roll(v, cols - 1, 0)

    def last_y(v):
        return pltpu.roll(v, 1, 0)

    def next_z(v):
        return pltpu.roll(v, layers - 1, 1)

    def last_z(v):
        return pltpu.roll(v, 1, 1)

    def place(chosen):
        return sum(product(v, spot, ((1,), (1,))) for v in split(chosen))

    loads[3].wait()
    largest = jnp.zeros((1, 128), jnp.float32)
    for b in range(blocks):
        lower = fac[b]
        high, low = split(lower)
        over = ((0,), (0,))
        gram = product(high, high, over) + product(high, low, over) + product(low, high, over)
        prod_hi[b], prod_lo[b] = split(gram)
        row_sum = jnp.sum(jnp.abs(gram), axis=0, keepdims=True)
        largest = jnp.maximum(largest, jnp.max(row_sum, axis=1, keepdims=True))
    own[1] = largest
    scale_x.start(own.at[1])

    for x in range(1, rows - 1):
        fill_row(x)
    chosen = select[pl.ds(0, cells), :]
    well_d[...] = place(chosen * is_producer)
    well_e[...] = place(chosen * pressure_row)

    zero_row = jnp.zeros((cols, layers), jnp.float32)

    def flux_row(x, flux_last):
        here, there = row(x), row(jnp.minimum(x + 1, rows - 1))
        k, p, f = perm[here, :], prs[here, :], frac[here, :]
        kx, px, fx = perm[there, :], prs[there, :], frac[there, :]
        tx = harmonic(k, kx)
        ty = jnp.where(inner_y, harmonic(k, next_y(k)), 0.0)
        tz = jnp.where(inner_z, 0.1 * harmonic(k, next_z(k)), 0.0)
        face_x[here, :] = tx
        face_y[here, :] = ty
        face_z[here, :] = tz
        wx = upwind(tx, p, px, f, fx)
        wy = upwind(ty, p, next_y(p), f, next_y(f))
        wz = upwind(tz, p, next_z(p), f, next_z(f))
        s = sat[here, :]
        made = 2.0 * s * s * (p * well_d[here, :] - well_e[here, :])
        moved[here, :] = s - dtp[here, :] * (
            made + (wx - flux_last) + (wy - last_y(wy)) + (wz - last_z(wz))
        )
        return wx

    each_row(flux_row, zero_row)

    def fraction(s):
        water, t = mobility(s)
        return water / t

    first, final = pl.ds(0, cols), pl.ds(cells - cols, cols)
    take_faces(INPUT)
    t = harmonic(input_x[0, PERM], perm[first, :])
    low_x[...] = t
    moved[first, :] += dtp[first, :] * upwind(
        t, input_x[0, PRS], prs[first, :], fraction(input_x[0, SAT]), frac[first, :]
    )
    t = harmonic(perm[final, :], input_x[1, PERM])
    high_x[...] = t
    moved[final, :] -= dtp[final, :] * upwind(
        t, prs[final, :], input_x[1, PRS], frac[final, :], fraction(input_x[1, SAT])
    )
    pack, rim = input_pack, input_y
    t = harmonic(rim[0, PERM], pack[0, PERM])
    side_y[0] = t
    flux = upwind(t, rim[0, PRS], pack[0, PRS], fraction(rim[0, SAT]), fraction(pack[0, SAT]))
    add_to(moved, 0, pack[0, DTP] * flux)
    t = harmonic(pack[1, PERM], rim[1, PERM])
    side_y[1] = t
    flux = upwind(t, pack[1, PRS], rim[1, PRS], fraction(pack[1, SAT]), fraction(rim[1, SAT]))
    add_to(moved, cols - 1, -pack[1, DTP] * flux)
    for i, c in ((0, 0), (1, cols - 1)):
        pack_y[MOVED - 1, i] = take(moved, c)
    send_faces(MOVED)

    chosen = split(select[...])
    for w in range(injectors):
        alone = jnp.where(lane_spot == producers + w, spot, jnp.zeros_like(spot))
        source[w] = sum(product(v, alone, ((1,), (1,))) for v in chosen)

    own[2] = jnp.max(scale_x.take(own[1]), axis=0)
    scale_y.start(own.at[2])
    sums = jnp.sum(window.take(own[0]), axis=0)
    scale = jnp.where(sums > 0.0, rate_row / jnp.where(sums > 0.0, sums, 1.0), 0.0)
    shares = [scale[:, producers + w : producers + w + 1] for w in range(injectors)]

    def weights(at):
        return sum(share * source[w, at, :] for w, share in enumerate(shares))


    def moved_row(x, _):
        here = row(x)
        made = mob[here, :] * weights(here)
        s = moved[here, :] + dtp[here, :] * made
        satn[here, :] = s
        resid[here, :] = made
        total[here, :] = mobility(s)[1]

    each_row(moved_row)

    store_satn = pltpu.make_async_copy(satn, satn_out, store_sem.at[0])
    store_satn.start()

    def residual_row(x, flux_last):
        here, there = row(x), row(jnp.minimum(x + 1, rows - 1))
        t, tx = total[here, :], total[there, :]
        p, px = prs[here, :], prs[there, :]
        cx = face_x[here, :] * (0.5 * (t + tx))
        cy = face_y[here, :] * (0.5 * (t + next_y(t)))
        cz = face_z[here, :] * (0.5 * (t + next_z(t)))
        face_x[here, :] = cx
        face_y[here, :] = cy
        face_z[here, :] = cz
        d, e = well_d[here, :], well_e[here, :]
        diag[here, :] = poro[here, :] + d * t
        fx = cx * (p - px)
        fy = cy * (p - next_y(p))
        fz = cz * (p - next_z(p))
        resid[here, :] = (
            resid[here, :]
            + t * (e - d * p)
            - ((fx - flux_last) + (fy - last_y(fy)) + (fz - last_z(fz)))
        )
        return fx

    each_row(residual_row, zero_row)

    own[4] = jnp.max(scale_y.take(own[2]), axis=0)
    scale_z.start(own.at[4])

    def rim_total(before, sat_rim, dtp_rim, weight):
        s = before + dtp_rim * (mobility(sat_rim)[1] * weight)
        return mobility(s)[1]

    pack_total = [take(total, 0), take(total, cols - 1)]
    edge = []
    take_faces(MOVED)
    t = rim_total(
        halo_x[MOVED - 1, 0], input_x[0, SAT], input_x[0, DTP], weights(pl.ds(cells, cols))
    )
    c = low_x[...] * (0.5 * (total[first, :] + t))
    low_x[...] = c
    resid[first, :] -= c * (prs[first, :] - input_x[0, PRS])
    t = rim_total(
        halo_x[MOVED - 1, 1],
        input_x[1, SAT],
        input_x[1, DTP],
        weights(pl.ds(cells + cols, cols)),
    )
    c = high_x[...] * (0.5 * (total[final, :] + t))
    high_x[...] = c
    resid[final, :] -= c * (prs[final, :] - input_x[1, PRS])
    for i, at in ((0, 0), (1, cols - 1)):
        t = rim_total(
            halo_y[MOVED - 1, i],
            rim[i, SAT],
            rim[i, DTP],
            weights(pl.ds(rim_y + i * rows, rows)),
        )
        c = side_y[i] * (0.5 * (pack_total[i] + t))
        side_y[i] = c
        edge.append(take(resid, at) - c * (pack[i, PRS] - rim[i, PRS]))
        put(resid, at, edge[i])

    def apply(v, b, factor):
        high, low = split(v if factor is None else v * factor)
        z = jnp.dot(high, prod_hi[b], preferred_element_type=jnp.float32)
        z += jnp.dot(high, prod_lo[b], preferred_element_type=jnp.float32)
        return z + jnp.dot(low, prod_hi[b], preferred_element_type=jnp.float32)

    def precondition(src, dst, factor):
        for b in range(blocks):
            parts = [
                src[pl.ds(x * cols + b * BLOCK, BLOCK), :] for x in range(rows)
            ]
            z = apply(jnp.concatenate(parts, axis=0), b, factor)
            for x in range(rows):
                dst[pl.ds(x * cols + b * BLOCK, BLOCK), :] = z[x * BLOCK : (x + 1) * BLOCK]

    def precondition_rim(k, src, low_column, high_column, factor):
        for b in range(blocks):
            here = pl.ds(b * BLOCK, BLOCK)
            parts = [src[here, :], src[pl.ds(cells - cols + b * BLOCK, BLOCK), :]]
            if b == 0:
                parts.append(low_column)
            if b == blocks - 1:
                parts.append(high_column)
            z = apply(jnp.concatenate(parts, axis=0), b, factor)
            pack_x[k, 0, here, :] = z[:BLOCK]
            pack_x[k, 1, here, :] = z[BLOCK : 2 * BLOCK]
            if b == 0:
                pack_y[BASE - 1 + k, 0] = z[2 * BLOCK : 2 * BLOCK + rows]
            if b == blocks - 1:
                pack_y[BASE - 1 + k, 1] = z[-rows:]

    pairs = [(0, 0), (1, 0), (1, 1), (2, 0), (2, 1), (2, 2)]
    count = len(pairs) + BASIS
    last = len(pairs) - 1

    def fold(total_, term):
        for i in range(term.shape[0] // 8):
            total_ = total_ + term[8 * i : 8 * i + 8]
        return total_

    def dots_row(x, sums):
        here = row(x)
        v = [base[k, here, :] for k in range(BASIS)]
        u = [image[k, here, :] for k in range(BASIS)]
        r = resid[here, :]
        terms = [v[i] * u[j] for i, j in pairs] + [v[i] * r for i in range(BASIS)]
        return tuple(fold(s, term) for s, term in zip(sums, terms))

    def into_lane(i, s, message):
        s = jnp.sum(s, axis=0, keepdims=True)
        return jnp.where(lane == i, jnp.sum(s, axis=1, keepdims=True), message)

    stores = [store_satn]
    for k in range(BASIS):
        e = BASE + k
        vec, img = base.at[k], image.at[k]
        if k == 1:
            top = jnp.max(scale_z.take(own[4]), axis=0)
            norm = jnp.concatenate([1.0 / top] * (layers // 128), axis=1)
        factor = (lambda: None, lambda: (SHIFT * norm) * norm, lambda: SHIFT * norm)[k]()
        prior = resid if k == 0 else image.at[k - 1]
        precondition_rim(k, prior, edge[0], edge[1], factor)
        send_faces(e)
        precondition(prior, vec, factor)
        store = pltpu.make_async_copy(
            vec, (z0_out, z1_out, z2_out)[k], store_sem.at[1 + k]
        )
        store.start()
        stores.append(store)

        def image_row(x, flux_last, vec=vec, img=img):
            here, there = row(x), row(jnp.minimum(x + 1, rows - 1))
            v, vx = vec[here, :], vec[there, :]
            fx = face_x[here, :] * (v - vx)
            fy = face_y[here, :] * (v - next_y(v))
            fz = face_z[here, :] * (v - next_z(v))
            img[here, :] = (
                diag[here, :] * v
                + (fx - flux_last)
                + (fy - last_y(fy))
                + (fz - last_z(fz))
            )
            return fx

        each_row(image_row, zero_row)
        h = e - 1
        if k < BASIS - 1:
            take_faces(e)
            img[first, :] += low_x[...] * (vec[first, :] - halo_x[h, 0])
            img[final, :] += high_x[...] * (vec[final, :] - halo_x[h, 1])
            for i, at in ((0, 0), (1, cols - 1)):
                edge[i] = take(img, at) + side_y[i] * (pack_y[h, i] - halo_y[h, i])
                put(img, at, edge[i])
            continue
        sums = each_row(dots_row, (jnp.zeros((8, layers), jnp.float32),) * count)
        message = jnp.zeros((1, 128), jnp.float32)
        for i, s in enumerate(sums):
            if i != last:
                message = into_lane(i, s, message)
        take_faces(e)
        s = fold(sums[last], low_x[...] * (vec[first, :] - halo_x[h, 0]) * vec[first, :])
        s = fold(s, high_x[...] * (vec[final, :] - halo_x[h, 1]) * vec[final, :])
        for i in range(2):
            s = fold(s, side_y[i] * (pack_y[h, i] - halo_y[h, i]) * pack_y[h, i])
        message = into_lane(last, s, message)

    own[5] = message
    sum_plane.start(own.at[5])
    own[6] = jnp.sum(sum_plane.take(own[5]), axis=0)
    sum_z.start(own.at[6])
    result = jnp.sum(sum_z.take(own[6]), axis=0)
    val = [result[:, i : i + 1] for i in range(count)]
    g00, g10, g11, g20, g21, g22, b0, b1, b2 = val

    def ratio(a, b):
        good = b > 0.0
        return jnp.where(good, a / jnp.where(good, b, 1.0), 0.0)

    l10, l20 = ratio(g10, g00), ratio(g20, g00)
    d1 = g11 - l10 * g10
    e21 = g21 - l20 * g10
    l21 = ratio(e21, d1)
    d2 = g22 - l20 * g20 - l21 * e21
    y1 = b1 - l10 * b0
    y2 = b2 - l20 * b0 - l21 * y1
    c2 = ratio(y2, d2)
    c1 = ratio(y1, d1) - l21 * c2
    c0 = ratio(b0, g00) - l10 * c1 - l20 * c2
    for k, c in enumerate((c0, c1, c2)):
        coef_out[k : k + 1, :] = jnp.broadcast_to(c, (1, layers))

    for group in groups:
        group.whole().wait_send()
    for d in range(4):
        pl.when(sends[d])(lambda: face_copy(EXCHANGES - 1, d).wait_send())
    for store in stores:
        store.wait()


def solution(mesh):
    n_gx, n_gy = mesh.shape["gx"], mesh.shape["gy"]

    def per_device(
        rock_type,
        perm_table,
        poro_table,
        saturation,
        pressure_old,
        factor_inverse,
        inject_cells,
        inject_index,
        inject_rate,
        produce_cells,
        produce_index,
        produce_pressure,
    ):
        rows, cols, layers = saturation.shape
        cells = rows * cols
        blocks = cols // BLOCK
        f32, bf16 = jnp.float32, jnp.bfloat16
        flat = (cells, layers)
        field = pltpu.VMEM(flat, f32)
        smem = pl.BlockSpec(memory_space=pltpu.SMEM)
        vmem = pl.BlockSpec(memory_space=pltpu.VMEM)
        hbm = pl.BlockSpec(memory_space=pltpu.HBM)
        out = pl.BlockSpec(memory_space=pl.ANY)
        plane = n_gx * (n_gy // RING)
        dma = pltpu.SemaphoreType.DMA
        scratch = [
            pltpu.VMEM((4,) + flat, f32),
            pltpu.VMEM(flat, jnp.int32),
            pltpu.VMEM((blocks, layers, layers), f32),
            pltpu.VMEM((blocks, layers, layers), bf16),
            pltpu.VMEM((blocks, layers, layers), bf16),
            field,
            field,
            field,
            pltpu.VMEM((cells + 2 * cols + 2 * rows, 128), f32),
            pltpu.VMEM((layers, 128), bf16),
            field,
            field,
            field,
            pltpu.VMEM((cols, layers), f32),
            pltpu.VMEM((cols, layers), f32),
            pltpu.VMEM((2, rows, layers), f32),
            field,
            field,
            field,
            pltpu.VMEM(
                (inject_index.shape[0], cells + 2 * cols + 2 * rows, layers), f32
            ),
            field,
            field,
            field,
            field,
            pltpu.VMEM((BASIS,) + flat, f32),
            pltpu.VMEM((BASIS,) + flat, f32),
            pltpu.VMEM((2, 4, cols, layers), f32),
            pltpu.VMEM((2, 4, rows, layers), f32),
            pltpu.VMEM((2, 4, rows, layers), f32),
            pltpu.VMEM((EXCHANGES - 1, 2, cols, layers), f32),
            pltpu.VMEM((EXCHANGES - 1, 2, rows, layers), f32),
            pltpu.VMEM((BASIS, 2, cols, layers), f32),
            pltpu.VMEM((EXCHANGES - 1, 2, rows, layers), f32),
            pltpu.VMEM((7, 1, 128), f32),
            pltpu.VMEM((3 * (2 * REACH + 1), 1, 128), f32),
            pltpu.VMEM((n_gx, 1, 128), f32),
            pltpu.VMEM((n_gy // RING, 1, 128), f32),
            pltpu.VMEM((RING, 1, 128), f32),
            pltpu.VMEM((plane, 1, 128), f32),
            pltpu.VMEM((RING, 1, 128), f32),
            dma((4,)),
            dma((1 + BASIS,)),
            dma((4,)),
            dma((2, 4)),
            dma((6,)),
            dma((6,)),
        ]
        operands = (
            jnp.swapaxes(inject_cells, 1, 2),
            inject_rate,
            jnp.swapaxes(produce_cells, 1, 2),
            produce_pressure,
            perm_table,
            poro_table,
            inject_index,
            produce_index,
            rock_type.reshape(flat),
            saturation.reshape(flat),
            pressure_old.reshape(flat),
            factor_inverse.reshape(blocks, layers, layers),
        )
        satn, z0, z1, z2, coef = pl.pallas_call(
            functools.partial(kernel, (rows, cols, layers, n_gx, n_gy)),
            out_shape=[
                *[jax.ShapeDtypeStruct(flat, f32)] * (1 + BASIS),
                jax.ShapeDtypeStruct((BASIS, layers), f32),
            ],
            in_specs=[smem] * 6 + [vmem] * 2 + [hbm] * 4,
            out_specs=[out] * (1 + BASIS) + [vmem],
            scratch_shapes=scratch,
            compiler_params=pltpu.CompilerParams(
                collective_id=0, has_side_effects=True, vmem_limit_bytes=24 * 1024 * 1024
            ),
            name="reservoir_step",
        )(*(pltpu.with_memory_space_constraint(a, pltpu.HBM) for a in operands))
        change = coef[0:1] * z0 + coef[1:2] * z1 + coef[2:3] * z2
        pressure = pressure_old.reshape(flat) + change
        return satn.reshape(saturation.shape), pressure.reshape(saturation.shape)

    grid = P("gx", "gy", None)
    in_specs = (grid, P(), P(), grid, grid, P("gx", "gy", None, None)) + (P(),) * 6
    return jax.shard_map(
        per_device, mesh=mesh, in_specs=in_specs, out_specs=(grid, grid), check_vma=False
    )
```

```python
import functools

import jax
import jax.numpy as jnp
from jax import lax
from jax.experimental import pallas as pl
from jax.experimental.pallas import tpu as pltpu
from jax.sharding import PartitionSpec as P

MESH = pl.DeviceIdType.MESH
BLOCK = 16
BASIS = 3
UNROLL = 4
RING = 8
TIME_STEP = 0.002
SHIFT = 2.0**-14

INPUT, MOVED, BASE = 0, 1, 2
EXCHANGES = BASE + BASIS
SAT, PRS, PERM, DTP = 0, 1, 2, 3
LO_X, HI_X, LO_Y, HI_Y = 0, 1, 2, 3
REACH = 5
FAR_X = (4, 3, 5, 2, 6, 1, 7)
FAR_Y = (2, 1, 3)
FAR_Z = (4, 3, 5, 2, 6, 1, 7)


def harmonic(former, latter):
    return 2.0 * former * latter / (former + latter)


def upwind(face, p_a, p_b, f_a, f_b):
    flow = face * (p_a - p_b)
    return flow * jnp.where(flow > 0.0, f_a, f_b)


def kernel(
    sizes,
    inj_cell,
    inj_rate,
    pro_cell,
    pro_pressure,
    perm_table,
    poro_table,
    inj_index,
    pro_index,
    rock_hbm,
    sat_hbm,
    prs_hbm,
    fac_hbm,
    satn_out,
    z0_out,
    z1_out,
    z2_out,
    coef_out,
    inp,
    rock,
    fac,
    prod_hi,
    prod_lo,
    poro,
    frac,
    mob,
    select,
    spots,
    face_x,
    face_y,
    face_z,
    low_x,
    high_x,
    side_y,
    moved,
    well_d,
    well_e,
    source,
    satn,
    total,
    diag,
    resid,
    base,
    image,
    input_x,
    input_y,
    input_pack,
    halo_x,
    halo_y,
    pack_x,
    pack_y,
    own,
    slot_w,
    slot_x,
    slot_y,
    slot_s,
    slot_a,
    slot_b,
    load_sem,
    store_sem,
    face_send,
    face_recv,
    late_send,
    late_recv,
    group_send,
    group_recv,
):
    rows, cols, layers, n_gx, n_gy = sizes
    blocks = cols // BLOCK
    cells = rows * cols
    full_cols = cols * n_gy
    n_y = n_gy // RING
    plane = n_gx * n_y
    injectors = inj_index.shape[0]
    producers = pro_index.shape[0]
    perfs = inj_index.shape[1]
    sat, prs, perm, dtp = (inp.at[i] for i in range(4))

    gx = lax.axis_index("gx")
    gy = lax.axis_index("gy")
    yy = gy // RING
    zz = gy % RING
    spot_a = gx * n_y + yy

    def row(x):
        return pl.ds(pl.multiple_of(x * cols, cols), cols)

    def take(ref, c):
        parts = [ref[pl.ds(x * cols + c, 1), :] for x in range(rows)]
        return jnp.concatenate(parts, axis=0)

    def put(ref, c, value):
        for x in range(rows):
            ref[pl.ds(x * cols + c, 1), :] = value[x : x + 1]

    neighbours = (
        (lax.rem(gx + n_gx - 1, n_gx), gy),
        (lax.rem(gx + 1, n_gx), gy),
        (gx, lax.rem(gy + n_gy - 1, n_gy)),
        (gx, lax.rem(gy + 1, n_gy)),
    )
    sends = (gx > 0, gx < n_gx - 1, gy > 0, gy < n_gy - 1)
    hears = (gx < n_gx - 1, gx > 0, gy < n_gy - 1, gy > 0)

    def near(a, b, c=0):
        y = lax.rem(yy + b, n_y) if b else yy
        z = lax.rem(zz + c, RING) if c else zz
        return (lax.rem(gx + a, n_gx) if a else gx, y * RING + z)

    def line(a, b):
        return (lax.rem(gx + n_gx + a, n_gx), lax.rem(gy + n_gy + b, n_gy))

    reach = [b for d in range(REACH, 0, -1) for b in (d, -d)] + [0]
    window_peers = [line(a, b) for b in reach for a in (-1, 1, 0) if a or b]
    x_peers = [near(a, 0) for a in FAR_X]
    y_peers = [near(0, b) for b in FAR_Y]
    z_peers = [near(0, 0, c) for c in FAR_Z]
    plane_peers = [near(a, b) for a in FAR_X + (0,) for b in FAR_Y + (0,) if a or b]

    def each_row(body, carry=None):
        def step(i, kept):
            for j in range(UNROLL):
                kept = body(i * UNROLL + j, kept)
            return kept

        if carry is None:
            pl.loop(0, rows // UNROLL)(lambda i: step(i, None) and None)
        else:
            carry = lax.fori_loop(0, rows // UNROLL, step, carry)
        return carry

    def split(v):
        high = v.astype(jnp.bfloat16)
        return high, (v - high.astype(jnp.float32)).astype(jnp.bfloat16)

    def product(a, b, dims):
        return lax.dot_general(a, b, (dims, ((), ())), preferred_element_type=jnp.float32)

    loads = [
        pltpu.make_async_copy(src, dst, load_sem.at[i])
        for i, (src, dst) in enumerate(
            ((sat_hbm, sat), (rock_hbm, rock), (prs_hbm, prs), (fac_hbm, fac))
        )
    ]
    for load in loads:
        load.start()

    barrier = pltpu.get_barrier_semaphore()

    def greet(peer):
        pl.semaphore_signal(barrier, inc=1, device_id=peer, device_id_type=MESH)

    for peer in window_peers[::-1] + plane_peers + z_peers:
        greet(peer)

    def clear_x(at):
        input_x[at] = jnp.zeros(input_x.shape[1:], jnp.float32)
        for e in range(EXCHANGES - 1):
            halo_x[e, at] = jnp.zeros(halo_x.shape[2:], jnp.float32)

    def clear_y(at):
        input_y[at] = jnp.zeros(input_y.shape[1:], jnp.float32)
        for e in range(EXCHANGES - 1):
            halo_y[e, at] = jnp.zeros(halo_y.shape[2:], jnp.float32)

    pl.when(gx == 0)(lambda: clear_x(0))
    pl.when(gx == n_gx - 1)(lambda: clear_x(1))
    pl.when(gy == 0)(lambda: clear_y(0))
    pl.when(gy == n_gy - 1)(lambda: clear_y(1))

    def lookup(kind, table):
        bit0 = (kind & 1) == 1
        bit1 = (kind & 2) == 2
        pairs = [jnp.where(bit0, table[2 * i + 1], table[2 * i]) for i in range(4)]
        high = jnp.where(bit1, pairs[3], pairs[2])
        return jnp.where(kind >= 4, high, jnp.where(bit1, pairs[1], pairs[0]))

    def fill_row(x, _=None):
        kind = rock[row(x), :]
        perm[row(x), :] = lookup(kind, perm_table)
        porosity = lookup(kind, poro_table)
        poro[row(x), :] = porosity
        dtp[row(x), :] = TIME_STEP / porosity

    loads[1].wait()
    for i, c in ((0, 0), (1, cols - 1)):
        kind = take(rock, c)
        input_pack[i, PERM] = lookup(kind, perm_table)
        input_pack[i, DTP] = TIME_STEP / lookup(kind, poro_table)
    fill_row(0)
    fill_row(rows - 1)
    loads[0].wait()
    loads[2].wait()
    for i, c in ((0, 0), (1, cols - 1)):
        input_pack[i, SAT] = take(sat, c)
        input_pack[i, PRS] = take(prs, c)

    def face_copy(e, d):
        if e == INPUT:
            soon = pl.ds(0, DTP)
            if d < 2:
                src = inp.at[soon, pl.ds(0 if d == LO_X else cells - cols, cols), :]
                dst = input_x.at[1 - d, soon]
            else:
                src, dst = input_pack.at[d - 2, soon], input_y.at[3 - d, soon]
        else:
            if d < 2:
                at = pl.ds(0 if d == LO_X else cells - cols, cols)
                src = moved.at[at, :] if e == MOVED else pack_x.at[e - BASE, d]
                dst = halo_x.at[e - 1, 1 - d]
            else:
                src, dst = pack_y.at[e - 1, d - 2], halo_y.at[e - 1, 3 - d]
        return pltpu.make_async_remote_copy(
            src_ref=src,
            dst_ref=dst,
            send_sem=face_send.at[d],
            recv_sem=face_recv.at[e % 2, d],
            device_id=neighbours[d],
            device_id_type=MESH,
        )

    def send_faces(e):
        for d in (LO_Y, HI_Y, LO_X, HI_X):

            @pl.when(sends[d])
            def _():
                if e > 0:
                    face_copy(e - 1, d).wait_send()
                face_copy(e, d).start()

    def take_faces(e):
        for d in range(4):
            pl.when(hears[d])(lambda: face_copy(e, d).wait_recv())

    def late_copy(d):
        if d < 2:
            src = dtp.at[pl.ds(0 if d == LO_X else cells - cols, cols), :]
            dst = input_x.at[1 - d, DTP]
        else:
            src, dst = input_pack.at[d - 2, DTP], input_y.at[3 - d, DTP]
        return pltpu.make_async_remote_copy(
            src_ref=src,
            dst_ref=dst,
            send_sem=late_send.at[d],
            recv_sem=late_recv.at[d],
            device_id=neighbours[d],
            device_id_type=MESH,
        )

    class Group:
        def __init__(self, k, peers, slots):
            self.k, self.peers, self.slots = k, peers, slots

        def copy(self, src, dst, peer):
            return pltpu.make_async_remote_copy(
                src_ref=src,
                dst_ref=dst,
                send_sem=group_send.at[self.k],
                recv_sem=group_recv.at[self.k],
                device_id=peer,
                device_id_type=MESH,
            )

        def start(self, src):
            for i, peer in enumerate(self.peers):
                self.copy(src, self.slots.at[i], peer).start()

        def whole(self):
            held = self.slots.at[pl.ds(0, len(self.peers))]
            return self.copy(held, held, self.peers[0])

        def take(self, mine):
            self.whole().wait_recv()
            self.slots[len(self.peers)] = mine
            return self.slots[...]

    window = Group(0, window_peers, slot_w)
    scale_x = Group(1, x_peers, slot_x)
    scale_y = Group(2, y_peers, slot_y)
    scale_z = Group(3, z_peers, slot_s)
    sum_plane = Group(4, plane_peers, slot_a)
    sum_z = Group(5, z_peers, slot_b)
    groups = (window, scale_x, scale_y, scale_z, sum_plane, sum_z)

    pl.semaphore_wait(barrier, len(plane_peers) + len(window_peers) + len(z_peers))
    send_faces(INPUT)
    for d in range(4):
        pl.when(sends[d])(lambda: late_copy(d).start())

    lane = lax.broadcasted_iota(jnp.int32, (1, 128), 1)
    well_row = jnp.full((1, 128), -9, jnp.int32)
    well_layer = jnp.full((1, 128), -9, jnp.int32)
    pressure_row = jnp.zeros((1, 128), jnp.float32)
    rate_row = jnp.zeros((1, 128), jnp.float32)
    wide = cols + 16
    spread = lax.broadcasted_iota(jnp.int32, (wide, perfs), 0) - lax.broadcasted_iota(
        jnp.int32, (wide, perfs), 1
    )
    lane_wide = lax.broadcasted_iota(jnp.int32, (wide, 128), 1)
    column = jnp.zeros((wide, 128), jnp.float32)
    for w in range(producers + injectors):
        produces = w < producers
        cell_ref = pro_cell if produces else inj_cell
        index_ref = pro_index if produces else inj_index
        i = w if produces else w - producers
        cell = cell_ref[i, 0, 0]
        well_row = jnp.where(lane == w, cell // full_cols - gx * rows, well_row)
        well_layer = jnp.where(lane == w, cell_ref[i, 1, 0], well_layer)
        start = cell % full_cols
        offset = spread + (gy * cols - 8 - start)
        hit = jnp.where(
            (offset == 0) | (offset == full_cols) | (offset == -full_cols),
            index_ref[i : i + 1, :],
            0.0,
        )
        column = jnp.where(lane_wide == w, jnp.sum(hit, axis=1, keepdims=True), column)
        if produces:
            pressure_row = jnp.where(lane == w, pro_pressure[i], pressure_row)
        else:
            rate_row = jnp.where(lane == w, inj_rate[i], rate_row)
    is_producer = jnp.where(lane < producers, 1.0, 0.0)
    layer_pos = lax.broadcasted_iota(jnp.int32, (layers, 128), 0)
    spots[...] = jnp.where(layer_pos == well_layer, 1.0, 0.0).astype(jnp.bfloat16)
    own_column = column[8 : 8 + cols]
    for x in range(rows):
        select[x * cols : (x + 1) * cols, :] = jnp.where(well_row == x, own_column, 0.0)
    select[cells : cells + cols, :] = jnp.where(well_row == -1, own_column, 0.0)
    select[cells + cols : cells + 2 * cols, :] = jnp.where(well_row == rows, own_column, 0.0)
    row_pos = lax.broadcasted_iota(jnp.int32, (rows, 128), 0)
    rim_y = cells + 2 * cols
    select[rim_y : rim_y + rows, :] = jnp.where(row_pos == well_row, column[7:8], 0.0)
    select[rim_y + rows : rim_y + 2 * rows, :] = jnp.where(
        row_pos == well_row, column[8 + cols : 9 + cols], 0.0
    )


    def mobility(s):
        water = 2.0 * s * s
        rest = 1.0 - s
        return water, water + rest * rest

    def mobility_row(x, _):
        water, t = mobility(sat[row(x), :])
        mob[row(x), :] = t
        frac[row(x), :] = water / t

    each_row(mobility_row)
    spot = spots[...]
    lane_spot = lax.broadcasted_iota(jnp.int32, (layers, 128), 1)
    picked = sum(product(v, spot, ((1,), (0,))) for v in split(mob[...]))
    own[0] = jnp.sum(picked * select[pl.ds(0, cells), :], axis=0, keepdims=True)
    window.start(own.at[0])

    lane_z = lax.broadcasted_iota(jnp.int32, (cols, layers), 1)
    col_y = lax.broadcasted_iota(jnp.int32, (cols, layers), 0)
    inner_z = lane_z < layers - 1
    inner_y = col_y < cols - 1

    def next_y(v):
        return pltpu.roll(v, cols - 1, 0)

    def last_y(v):
        return pltpu.roll(v, 1, 0)

    def next_z(v):
        return pltpu.roll(v, layers - 1, 1)

    def last_z(v):
        return pltpu.roll(v, 1, 1)

    def place(chosen):
        return sum(product(v, spot, ((1,), (1,))) for v in split(chosen))

    loads[3].wait()
    largest = jnp.zeros((1, 128), jnp.float32)
    for b in range(blocks):
        lower = fac[b]
        high, low = split(lower)
        over = ((0,), (0,))
        gram = product(high, high, over) + product(high, low, over) + product(low, high, over)
        prod_hi[b], prod_lo[b] = split(gram)
        row_sum = jnp.sum(jnp.abs(gram), axis=0, keepdims=True)
        largest = jnp.maximum(largest, jnp.max(row_sum, axis=1, keepdims=True))
    own[1] = largest
    scale_x.start(own.at[1])

    for x in range(1, rows - 1):
        fill_row(x)
    chosen = select[pl.ds(0, cells), :]
    well_d[...] = place(chosen * is_producer)
    well_e[...] = place(chosen * pressure_row)

    zero_row = jnp.zeros((cols, layers), jnp.float32)

    def flux_row(x, flux_last):
        here, there = row(x), row(jnp.minimum(x + 1, rows - 1))
        k, p, f = perm[here, :], prs[here, :], frac[here, :]
        kx, px, fx = perm[there, :], prs[there, :], frac[there, :]
        tx = harmonic(k, kx)
        ty = jnp.where(inner_y, harmonic(k, next_y(k)), 0.0)
        tz = jnp.where(inner_z, 0.1 * harmonic(k, next_z(k)), 0.0)
        face_x[here, :] = tx
        face_y[here, :] = ty
        face_z[here, :] = tz
        wx = upwind(tx, p, px, f, fx)
        wy = upwind(ty, p, next_y(p), f, next_y(f))
        wz = upwind(tz, p, next_z(p), f, next_z(f))
        s = sat[here, :]
        made = 2.0 * s * s * (p * well_d[here, :] - well_e[here, :])
        moved[here, :] = s - dtp[here, :] * (
            made + (wx - flux_last) + (wy - last_y(wy)) + (wz - last_z(wz))
        )
        return wx

    each_row(flux_row, zero_row)

    def fraction(s):
        water, t = mobility(s)
        return water / t

    first, final = pl.ds(0, cols), pl.ds(cells - cols, cols)
    take_faces(INPUT)
    t = harmonic(input_x[0, PERM], perm[first, :])
    low_x[...] = t
    moved[first, :] += dtp[first, :] * upwind(
        t, input_x[0, PRS], prs[first, :], fraction(input_x[0, SAT]), frac[first, :]
    )
    t = harmonic(perm[final, :], input_x[1, PERM])
    high_x[...] = t
    moved[final, :] -= dtp[final, :] * upwind(
        t, prs[final, :], input_x[1, PRS], frac[final, :], fraction(input_x[1, SAT])
    )
    pack, rim = input_pack, input_y
    t = harmonic(rim[0, PERM], pack[0, PERM])
    side_y[0] = t
    flux = upwind(t, rim[0, PRS], pack[0, PRS], fraction(rim[0, SAT]), fraction(pack[0, SAT]))
    rims = [take(moved, 0) + pack[0, DTP] * flux]
    t = harmonic(pack[1, PERM], rim[1, PERM])
    side_y[1] = t
    flux = upwind(t, pack[1, PRS], rim[1, PRS], fraction(pack[1, SAT]), fraction(rim[1, SAT]))
    rims.append(take(moved, cols - 1) - pack[1, DTP] * flux)
    for i, c in ((0, 0), (1, cols - 1)):
        pack_y[MOVED - 1, i] = rims[i]
        put(moved, c, rims[i])
    send_faces(MOVED)
    own[2] = jnp.max(scale_x.take(own[1]), axis=0)
    scale_y.start(own.at[2])

    chosen = split(select[...])
    for w in range(injectors):
        alone = jnp.where(lane_spot == producers + w, spot, jnp.zeros_like(spot))
        source[w] = sum(product(v, alone, ((1,), (1,))) for v in chosen)

    sums = jnp.sum(window.take(own[0]), axis=0)
    scale = jnp.where(sums > 0.0, rate_row / jnp.where(sums > 0.0, sums, 1.0), 0.0)
    shares = [scale[:, producers + w : producers + w + 1] for w in range(injectors)]

    def weights(at):
        return sum(share * source[w, at, :] for w, share in enumerate(shares))


    def moved_row(x, _):
        here = row(x)
        made = mob[here, :] * weights(here)
        s = moved[here, :] + dtp[here, :] * made
        satn[here, :] = s
        resid[here, :] = made
        total[here, :] = mobility(s)[1]

    each_row(moved_row)

    store_satn = pltpu.make_async_copy(satn, satn_out, store_sem.at[0])
    store_satn.start()

    def residual_row(x, flux_last):
        here, there = row(x), row(jnp.minimum(x + 1, rows - 1))
        t, tx = total[here, :], total[there, :]
        p, px = prs[here, :], prs[there, :]
        cx = face_x[here, :] * (0.5 * (t + tx))
        cy = face_y[here, :] * (0.5 * (t + next_y(t)))
        cz = face_z[here, :] * (0.5 * (t + next_z(t)))
        face_x[here, :] = cx
        face_y[here, :] = cy
        face_z[here, :] = cz
        d, e = well_d[here, :], well_e[here, :]
        diag[here, :] = poro[here, :] + d * t
        fx = cx * (p - px)
        fy = cy * (p - next_y(p))
        fz = cz * (p - next_z(p))
        resid[here, :] = (
            resid[here, :]
            + t * (e - d * p)
            - ((fx - flux_last) + (fy - last_y(fy)) + (fz - last_z(fz)))
        )
        return fx

    each_row(residual_row, zero_row)

    own[4] = jnp.max(scale_y.take(own[2]), axis=0)
    scale_z.start(own.at[4])

    def rim_total(before, sat_rim, dtp_rim, weight):
        s = before + dtp_rim * (mobility(sat_rim)[1] * weight)
        return mobility(s)[1]

    pack_total = [take(total, 0), take(total, cols - 1)]
    edge = []
    take_faces(MOVED)
    for d in range(4):
        pl.when(hears[d])(lambda: late_copy(d).wait_recv())
    t = rim_total(
        halo_x[MOVED - 1, 0], input_x[0, SAT], input_x[0, DTP], weights(pl.ds(cells, cols))
    )
    c = low_x[...] * (0.5 * (total[first, :] + t))
    low_x[...] = c
    resid[first, :] -= c * (prs[first, :] - input_x[0, PRS])
    t = rim_total(
        halo_x[MOVED - 1, 1],
        input_x[1, SAT],
        input_x[1, DTP],
        weights(pl.ds(cells + cols, cols)),
    )
    c = high_x[...] * (0.5 * (total[final, :] + t))
    high_x[...] = c
    resid[final, :] -= c * (prs[final, :] - input_x[1, PRS])
    for i, at in ((0, 0), (1, cols - 1)):
        t = rim_total(
            halo_y[MOVED - 1, i],
            rim[i, SAT],
            rim[i, DTP],
            weights(pl.ds(rim_y + i * rows, rows)),
        )
        c = side_y[i] * (0.5 * (pack_total[i] + t))
        side_y[i] = c
        edge.append(take(resid, at) - c * (pack[i, PRS] - rim[i, PRS]))
        put(resid, at, edge[i])

    def apply(v, b, factor):
        high, low = split(v if factor is None else v * factor)
        z = jnp.dot(high, prod_hi[b], preferred_element_type=jnp.float32)
        z += jnp.dot(high, prod_lo[b], preferred_element_type=jnp.float32)
        return z + jnp.dot(low, prod_hi[b], preferred_element_type=jnp.float32)

    def precondition(src, dst, factor):
        for b in range(blocks):
            parts = [
                src[pl.ds(x * cols + b * BLOCK, BLOCK), :] for x in range(rows)
            ]
            z = apply(jnp.concatenate(parts, axis=0), b, factor)
            for x in range(rows):
                dst[pl.ds(x * cols + b * BLOCK, BLOCK), :] = z[x * BLOCK : (x + 1) * BLOCK]

    def precondition_rim(k, src, low_column, high_column, factor):
        for b in range(blocks):
            here = pl.ds(b * BLOCK, BLOCK)
            parts = [src[here, :], src[pl.ds(cells - cols + b * BLOCK, BLOCK), :]]
            if b == 0:
                parts.append(low_column)
            if b == blocks - 1:
                parts.append(high_column)
            z = apply(jnp.concatenate(parts, axis=0), b, factor)
            pack_x[k, 0, here, :] = z[:BLOCK]
            pack_x[k, 1, here, :] = z[BLOCK : 2 * BLOCK]
            if b == 0:
                pack_y[BASE - 1 + k, 0] = z[2 * BLOCK : 2 * BLOCK + rows]
            if b == blocks - 1:
                pack_y[BASE - 1 + k, 1] = z[-rows:]

    pairs = [(0, 0), (1, 0), (1, 1), (2, 0), (2, 1), (2, 2)]
    count = len(pairs) + BASIS
    last = len(pairs) - 1

    def fold(total_, term):
        for i in range(term.shape[0] // 8):
            total_ = total_ + term[8 * i : 8 * i + 8]
        return total_

    def dots_row(x, sums):
        here = row(x)
        v = [base[k, here, :] for k in range(BASIS)]
        u = [image[k, here, :] for k in range(BASIS)]
        r = resid[here, :]
        terms = [v[i] * u[j] for i, j in pairs] + [v[i] * r for i in range(BASIS)]
        return tuple(fold(s, term) for s, term in zip(sums, terms))

    def into_lane(i, s, message):
        s = jnp.sum(s, axis=0, keepdims=True)
        return jnp.where(lane == i, jnp.sum(s, axis=1, keepdims=True), message)

    stores = [store_satn]
    for k in range(BASIS):
        e = BASE + k
        vec, img = base.at[k], image.at[k]
        if k == 1:
            top = jnp.max(scale_z.take(own[4]), axis=0)
            norm = jnp.concatenate([1.0 / top] * (layers // 128), axis=1)
        factor = (lambda: None, lambda: (SHIFT * norm) * norm, lambda: SHIFT * norm)[k]()
        prior = resid if k == 0 else image.at[k - 1]
        precondition_rim(k, prior, edge[0], edge[1], factor)
        send_faces(e)
        precondition(prior, vec, factor)
        store = pltpu.make_async_copy(
            vec, (z0_out, z1_out, z2_out)[k], store_sem.at[1 + k]
        )
        store.start()
        stores.append(store)

        def image_row(x, flux_last, vec=vec, img=img):
            here, there = row(x), row(jnp.minimum(x + 1, rows - 1))
            v, vx = vec[here, :], vec[there, :]
            fx = face_x[here, :] * (v - vx)
            fy = face_y[here, :] * (v - next_y(v))
            fz = face_z[here, :] * (v - next_z(v))
            img[here, :] = (
                diag[here, :] * v
                + (fx - flux_last)
                + (fy - last_y(fy))
                + (fz - last_z(fz))
            )
            return fx

        each_row(image_row, zero_row)
        h = e - 1
        if k < BASIS - 1:
            take_faces(e)
            img[first, :] += low_x[...] * (vec[first, :] - halo_x[h, 0])
            img[final, :] += high_x[...] * (vec[final, :] - halo_x[h, 1])
            for i, at in ((0, 0), (1, cols - 1)):
                edge[i] = take(img, at) + side_y[i] * (pack_y[h, i] - halo_y[h, i])
                put(img, at, edge[i])
            continue
        sums = each_row(dots_row, (jnp.zeros((8, layers), jnp.float32),) * count)
        message = jnp.zeros((1, 128), jnp.float32)
        for i, s in enumerate(sums):
            if i != last:
                message = into_lane(i, s, message)
        take_faces(e)
        s = fold(sums[last], low_x[...] * (vec[first, :] - halo_x[h, 0]) * vec[first, :])
        s = fold(s, high_x[...] * (vec[final, :] - halo_x[h, 1]) * vec[final, :])
        for i in range(2):
            s = fold(s, side_y[i] * (pack_y[h, i] - halo_y[h, i]) * pack_y[h, i])
        message = into_lane(last, s, message)

    own[5] = message
    sum_plane.start(own.at[5])
    own[6] = jnp.sum(sum_plane.take(own[5]), axis=0)
    sum_z.start(own.at[6])
    result = jnp.sum(sum_z.take(own[6]), axis=0)
    val = [result[:, i : i + 1] for i in range(count)]
    g00, g10, g11, g20, g21, g22, b0, b1, b2 = val

    def ratio(a, b):
        good = b > 0.0
        return jnp.where(good, a / jnp.where(good, b, 1.0), 0.0)

    l10, l20 = ratio(g10, g00), ratio(g20, g00)
    d1 = g11 - l10 * g10
    e21 = g21 - l20 * g10
    l21 = ratio(e21, d1)
    d2 = g22 - l20 * g20 - l21 * e21
    y1 = b1 - l10 * b0
    y2 = b2 - l20 * b0 - l21 * y1
    c2 = ratio(y2, d2)
    c1 = ratio(y1, d1) - l21 * c2
    c0 = ratio(b0, g00) - l10 * c1 - l20 * c2
    for k, c in enumerate((c0, c1, c2)):
        coef_out[k : k + 1, :] = jnp.broadcast_to(c, (1, layers))

    for group in groups:
        group.whole().wait_send()
    for d in range(4):
        pl.when(sends[d])(lambda: face_copy(EXCHANGES - 1, d).wait_send())
        pl.when(sends[d])(lambda: late_copy(d).wait_send())
    for store in stores:
        store.wait()


def solution(mesh):
    n_gx, n_gy = mesh.shape["gx"], mesh.shape["gy"]

    def per_device(
        rock_type,
        perm_table,
        poro_table,
        saturation,
        pressure_old,
        factor_inverse,
        inject_cells,
        inject_index,
        inject_rate,
        produce_cells,
        produce_index,
        produce_pressure,
    ):
        rows, cols, layers = saturation.shape
        cells = rows * cols
        blocks = cols // BLOCK
        f32, bf16 = jnp.float32, jnp.bfloat16
        flat = (cells, layers)
        field = pltpu.VMEM(flat, f32)
        smem = pl.BlockSpec(memory_space=pltpu.SMEM)
        vmem = pl.BlockSpec(memory_space=pltpu.VMEM)
        hbm = pl.BlockSpec(memory_space=pltpu.HBM)
        out = pl.BlockSpec(memory_space=pl.ANY)
        plane = n_gx * (n_gy // RING)
        dma = pltpu.SemaphoreType.DMA
        scratch = [
            pltpu.VMEM((4,) + flat, f32),
            pltpu.VMEM(flat, jnp.int32),
            pltpu.VMEM((blocks, layers, layers), f32),
            pltpu.VMEM((blocks, layers, layers), bf16),
            pltpu.VMEM((blocks, layers, layers), bf16),
            field,
            field,
            field,
            pltpu.VMEM((cells + 2 * cols + 2 * rows, 128), f32),
            pltpu.VMEM((layers, 128), bf16),
            field,
            field,
            field,
            pltpu.VMEM((cols, layers), f32),
            pltpu.VMEM((cols, layers), f32),
            pltpu.VMEM((2, rows, layers), f32),
            field,
            field,
            field,
            pltpu.VMEM(
                (inject_index.shape[0], cells + 2 * cols + 2 * rows, layers), f32
            ),
            field,
            field,
            field,
            field,
            pltpu.VMEM((BASIS,) + flat, f32),
            pltpu.VMEM((BASIS,) + flat, f32),
            pltpu.VMEM((2, 4, cols, layers), f32),
            pltpu.VMEM((2, 4, rows, layers), f32),
            pltpu.VMEM((2, 4, rows, layers), f32),
            pltpu.VMEM((EXCHANGES - 1, 2, cols, layers), f32),
            pltpu.VMEM((EXCHANGES - 1, 2, rows, layers), f32),
            pltpu.VMEM((BASIS, 2, cols, layers), f32),
            pltpu.VMEM((EXCHANGES - 1, 2, rows, layers), f32),
            pltpu.VMEM((7, 1, 128), f32),
            pltpu.VMEM((3 * (2 * REACH + 1), 1, 128), f32),
            pltpu.VMEM((n_gx, 1, 128), f32),
            pltpu.VMEM((n_gy // RING, 1, 128), f32),
            pltpu.VMEM((RING, 1, 128), f32),
            pltpu.VMEM((plane, 1, 128), f32),
            pltpu.VMEM((RING, 1, 128), f32),
            dma((4,)),
            dma((1 + BASIS,)),
            dma((4,)),
            dma((2, 4)),
            dma((4,)),
            dma((4,)),
            dma((6,)),
            dma((6,)),
        ]
        operands = (
            jnp.swapaxes(inject_cells, 1, 2),
            inject_rate,
            jnp.swapaxes(produce_cells, 1, 2),
            produce_pressure,
            perm_table,
            poro_table,
            inject_index,
            produce_index,
            rock_type.reshape(flat),
            saturation.reshape(flat),
            pressure_old.reshape(flat),
            factor_inverse.reshape(blocks, layers, layers),
        )
        satn, z0, z1, z2, coef = pl.pallas_call(
            functools.partial(kernel, (rows, cols, layers, n_gx, n_gy)),
            out_shape=[
                *[jax.ShapeDtypeStruct(flat, f32)] * (1 + BASIS),
                jax.ShapeDtypeStruct((BASIS, layers), f32),
            ],
            in_specs=[smem] * 6 + [vmem] * 2 + [hbm] * 4,
            out_specs=[out] * (1 + BASIS) + [vmem],
            scratch_shapes=scratch,
            compiler_params=pltpu.CompilerParams(
                collective_id=0, has_side_effects=True, vmem_limit_bytes=24 * 1024 * 1024
            ),
            name="reservoir_step",
        )(*(pltpu.with_memory_space_constraint(a, pltpu.HBM) for a in operands))
        change = coef[0:1] * z0 + coef[1:2] * z1 + coef[2:3] * z2
        pressure = pressure_old.reshape(flat) + change
        return satn.reshape(saturation.shape), pressure.reshape(saturation.shape)

    grid = P("gx", "gy", None)
    in_specs = (grid, P(), P(), grid, grid, P("gx", "gy", None, None)) + (P(),) * 6
    return jax.shard_map(
        per_device, mesh=mesh, in_specs=in_specs, out_specs=(grid, grid), check_vma=False
    )
```

```python
import functools

import jax
import jax.numpy as jnp
from jax import lax
from jax.experimental import pallas as pl
from jax.experimental.pallas import tpu as pltpu
from jax.sharding import PartitionSpec as P

MESH = pl.DeviceIdType.MESH
BLOCK = 16
BASIS = 3
UNROLL = 4
RING = 8
TIME_STEP = 0.002
SHIFT = 2.0**-14

INPUT, MOVED, BASE = 0, 1, 2
EXCHANGES = BASE + BASIS
SAT, PRS, PERM, DTP = 0, 1, 2, 3
LO_X, HI_X, LO_Y, HI_Y = 0, 1, 2, 3
FAR_X = (4, 3, 5, 2, 6, 1, 7)
FAR_Y = (2, 1, 3)
FAR_Z = (4, 3, 5, 2, 6, 1, 7)


def harmonic(former, latter):
    return 2.0 * former * latter / (former + latter)


def upwind(face, p_a, p_b, f_a, f_b):
    flow = face * (p_a - p_b)
    return flow * jnp.where(flow > 0.0, f_a, f_b)


def kernel(
    sizes,
    inj_cell,
    inj_rate,
    pro_cell,
    pro_pressure,
    perm_table,
    poro_table,
    inj_index,
    pro_index,
    rock_hbm,
    sat_hbm,
    prs_hbm,
    fac_hbm,
    satn_out,
    z0_out,
    z1_out,
    z2_out,
    coef_out,
    inp,
    rock,
    fac,
    prod_hi,
    prod_lo,
    poro,
    frac,
    mob,
    select,
    spots,
    face_x,
    face_y,
    face_z,
    low_x,
    high_x,
    side_y,
    moved,
    well_d,
    well_e,
    source,
    satn,
    total,
    diag,
    resid,
    base,
    image,
    input_x,
    input_y,
    input_pack,
    halo_x,
    halo_y,
    pack_x,
    pack_y,
    own,
    slot_w,
    slot_v,
    slot_x,
    slot_y,
    slot_s,
    slot_a,
    slot_b,
    load_sem,
    store_sem,
    face_send,
    face_recv,
    late_send,
    late_recv,
    group_send,
    group_recv,
):
    rows, cols, layers, n_gx, n_gy = sizes
    blocks = cols // BLOCK
    cells = rows * cols
    full_cols = cols * n_gy
    n_y = n_gy // RING
    plane = n_gx * n_y
    injectors = inj_index.shape[0]
    producers = pro_index.shape[0]
    perfs = inj_index.shape[1]
    sat, prs, perm, dtp = (inp.at[i] for i in range(4))

    gx = lax.axis_index("gx")
    gy = lax.axis_index("gy")
    yy = gy // RING
    zz = gy % RING
    spot_a = gx * n_y + yy

    def row(x):
        return pl.ds(pl.multiple_of(x * cols, cols), cols)

    def take(ref, c):
        parts = [ref[pl.ds(x * cols + c, 1), :] for x in range(rows)]
        return jnp.concatenate(parts, axis=0)

    def put(ref, c, value):
        for x in range(rows):
            ref[pl.ds(x * cols + c, 1), :] = value[x : x + 1]

    neighbours = (
        (lax.rem(gx + n_gx - 1, n_gx), gy),
        (lax.rem(gx + 1, n_gx), gy),
        (gx, lax.rem(gy + n_gy - 1, n_gy)),
        (gx, lax.rem(gy + 1, n_gy)),
    )
    sends = (gx > 0, gx < n_gx - 1, gy > 0, gy < n_gy - 1)
    hears = (gx < n_gx - 1, gx > 0, gy < n_gy - 1, gy > 0)

    def near(a, b, c=0):
        y = lax.rem(yy + b, n_y) if b else yy
        z = lax.rem(zz + c, RING) if c else zz
        return (lax.rem(gx + a, n_gx) if a else gx, y * RING + z)

    around_peers = [
        near(a, b) for a in (n_gx - 1, 1, 0) for b in (n_y - 1, 1, 0) if a or b
    ]
    x_peers = [near(a, 0) for a in FAR_X]
    y_peers = [near(0, b) for b in FAR_Y]
    z_peers = [near(0, 0, c) for c in FAR_Z]
    plane_peers = [near(a, b) for a in FAR_X + (0,) for b in FAR_Y + (0,) if a or b]

    def each_row(body, carry=None):
        def step(i, kept):
            for j in range(UNROLL):
                kept = body(i * UNROLL + j, kept)
            return kept

        if carry is None:
            pl.loop(0, rows // UNROLL)(lambda i: step(i, None) and None)
        else:
            carry = lax.fori_loop(0, rows // UNROLL, step, carry)
        return carry

    def split(v):
        high = v.astype(jnp.bfloat16)
        return high, (v - high.astype(jnp.float32)).astype(jnp.bfloat16)

    def product(a, b, dims):
        return lax.dot_general(a, b, (dims, ((), ())), preferred_element_type=jnp.float32)

    loads = [
        pltpu.make_async_copy(src, dst, load_sem.at[i])
        for i, (src, dst) in enumerate(
            ((sat_hbm, sat), (rock_hbm, rock), (prs_hbm, prs), (fac_hbm, fac))
        )
    ]
    for load in loads:
        load.start()

    barrier = pltpu.get_barrier_semaphore()

    def greet(peer):
        pl.semaphore_signal(barrier, inc=1, device_id=peer, device_id_type=MESH)

    for peer in neighbours[2:] + tuple(plane_peers[::-1]) + tuple(z_peers[::-1]):
        greet(peer)

    def clear_x(at):
        input_x[at] = jnp.zeros(input_x.shape[1:], jnp.float32)
        for e in range(EXCHANGES - 1):
            halo_x[e, at] = jnp.zeros(halo_x.shape[2:], jnp.float32)

    def clear_y(at):
        input_y[at] = jnp.zeros(input_y.shape[1:], jnp.float32)
        for e in range(EXCHANGES - 1):
            halo_y[e, at] = jnp.zeros(halo_y.shape[2:], jnp.float32)

    pl.when(gx == 0)(lambda: clear_x(0))
    pl.when(gx == n_gx - 1)(lambda: clear_x(1))
    pl.when(gy == 0)(lambda: clear_y(0))
    pl.when(gy == n_gy - 1)(lambda: clear_y(1))

    def lookup(kind, table):
        bit0 = (kind & 1) == 1
        bit1 = (kind & 2) == 2
        pairs = [jnp.where(bit0, table[2 * i + 1], table[2 * i]) for i in range(4)]
        high = jnp.where(bit1, pairs[3], pairs[2])
        return jnp.where(kind >= 4, high, jnp.where(bit1, pairs[1], pairs[0]))

    def fill_row(x, _=None):
        kind = rock[row(x), :]
        perm[row(x), :] = lookup(kind, perm_table)
        porosity = lookup(kind, poro_table)
        poro[row(x), :] = porosity
        dtp[row(x), :] = TIME_STEP / porosity

    loads[1].wait()
    for i, c in ((0, 0), (1, cols - 1)):
        kind = take(rock, c)
        input_pack[i, PERM] = lookup(kind, perm_table)
        input_pack[i, DTP] = TIME_STEP / lookup(kind, poro_table)
    fill_row(0)
    fill_row(rows - 1)
    loads[0].wait()
    loads[2].wait()
    for i, c in ((0, 0), (1, cols - 1)):
        input_pack[i, SAT] = take(sat, c)
        input_pack[i, PRS] = take(prs, c)

    def face_copy(e, d):
        if e == INPUT:
            soon = pl.ds(0, DTP)
            if d < 2:
                src = inp.at[soon, pl.ds(0 if d == LO_X else cells - cols, cols), :]
                dst = input_x.at[1 - d, soon]
            else:
                src, dst = input_pack.at[d - 2, soon], input_y.at[3 - d, soon]
        else:
            if d < 2:
                at = pl.ds(0 if d == LO_X else cells - cols, cols)
                src = moved.at[at, :] if e == MOVED else pack_x.at[e - BASE, d]
                dst = halo_x.at[e - 1, 1 - d]
            else:
                src, dst = pack_y.at[e - 1, d - 2], halo_y.at[e - 1, 3 - d]
        return pltpu.make_async_remote_copy(
            src_ref=src,
            dst_ref=dst,
            send_sem=face_send.at[d],
            recv_sem=face_recv.at[e % 2, d],
            device_id=neighbours[d],
            device_id_type=MESH,
        )

    def send_faces(e):
        for d in (LO_Y, HI_Y, LO_X, HI_X):

            @pl.when(sends[d])
            def _():
                if e > 0:
                    face_copy(e - 1, d).wait_send()
                face_copy(e, d).start()

    def take_faces(e):
        for d in range(4):
            pl.when(hears[d])(lambda: face_copy(e, d).wait_recv())

    def late_copy(d):
        if d < 2:
            src = dtp.at[pl.ds(0 if d == LO_X else cells - cols, cols), :]
            dst = input_x.at[1 - d, DTP]
        else:
            src, dst = input_pack.at[d - 2, DTP], input_y.at[3 - d, DTP]
        return pltpu.make_async_remote_copy(
            src_ref=src,
            dst_ref=dst,
            send_sem=late_send.at[d],
            recv_sem=late_recv.at[d],
            device_id=neighbours[d],
            device_id_type=MESH,
        )

    class Group:
        def __init__(self, k, peers, slots):
            self.k, self.peers, self.slots = k, peers, slots

        def copy(self, src, dst, peer):
            return pltpu.make_async_remote_copy(
                src_ref=src,
                dst_ref=dst,
                send_sem=group_send.at[self.k],
                recv_sem=group_recv.at[self.k],
                device_id=peer,
                device_id_type=MESH,
            )

        def start(self, src):
            for i, peer in enumerate(self.peers):
                self.copy(src, self.slots.at[i], peer).start()

        def whole(self):
            held = self.slots.at[pl.ds(0, len(self.peers))]
            return self.copy(held, held, self.peers[0])

        def take(self, mine):
            self.whole().wait_recv()
            self.slots[len(self.peers)] = mine
            return self.slots[...]

    well_z = Group(0, z_peers, slot_v)
    well_xy = Group(6, around_peers, slot_w)
    scale_x = Group(1, x_peers, slot_x)
    scale_y = Group(2, y_peers, slot_y)
    scale_z = Group(3, z_peers, slot_s)
    sum_plane = Group(4, plane_peers, slot_a)
    sum_z = Group(5, z_peers, slot_b)
    groups = (well_z, well_xy, scale_x, scale_y, scale_z, sum_plane, sum_z)

    pl.semaphore_wait(barrier, 2 + len(plane_peers) + len(z_peers))
    send_faces(INPUT)
    for d in range(4):
        pl.when(sends[d])(lambda: late_copy(d).start())

    lane = lax.broadcasted_iota(jnp.int32, (1, 128), 1)
    well_row = jnp.full((1, 128), -9, jnp.int32)
    well_layer = jnp.full((1, 128), -9, jnp.int32)
    pressure_row = jnp.zeros((1, 128), jnp.float32)
    rate_row = jnp.zeros((1, 128), jnp.float32)
    wide = cols + 16
    spread = lax.broadcasted_iota(jnp.int32, (wide, perfs), 0) - lax.broadcasted_iota(
        jnp.int32, (wide, perfs), 1
    )
    lane_wide = lax.broadcasted_iota(jnp.int32, (wide, 128), 1)
    column = jnp.zeros((wide, 128), jnp.float32)
    for w in range(producers + injectors):
        produces = w < producers
        cell_ref = pro_cell if produces else inj_cell
        index_ref = pro_index if produces else inj_index
        i = w if produces else w - producers
        cell = cell_ref[i, 0, 0]
        well_row = jnp.where(lane == w, cell // full_cols - gx * rows, well_row)
        well_layer = jnp.where(lane == w, cell_ref[i, 1, 0], well_layer)
        start = cell % full_cols
        offset = spread + (gy * cols - 8 - start)
        hit = jnp.where(
            (offset == 0) | (offset == full_cols) | (offset == -full_cols),
            index_ref[i : i + 1, :],
            0.0,
        )
        column = jnp.where(lane_wide == w, jnp.sum(hit, axis=1, keepdims=True), column)
        if produces:
            pressure_row = jnp.where(lane == w, pro_pressure[i], pressure_row)
        else:
            rate_row = jnp.where(lane == w, inj_rate[i], rate_row)
    is_producer = jnp.where(lane < producers, 1.0, 0.0)
    layer_pos = lax.broadcasted_iota(jnp.int32, (layers, 128), 0)
    spots[...] = jnp.where(layer_pos == well_layer, 1.0, 0.0).astype(jnp.bfloat16)
    own_column = column[8 : 8 + cols]
    for x in range(rows):
        select[x * cols : (x + 1) * cols, :] = jnp.where(well_row == x, own_column, 0.0)
    select[cells : cells + cols, :] = jnp.where(well_row == -1, own_column, 0.0)
    select[cells + cols : cells + 2 * cols, :] = jnp.where(well_row == rows, own_column, 0.0)
    row_pos = lax.broadcasted_iota(jnp.int32, (rows, 128), 0)
    rim_y = cells + 2 * cols
    select[rim_y : rim_y + rows, :] = jnp.where(row_pos == well_row, column[7:8], 0.0)
    select[rim_y + rows : rim_y + 2 * rows, :] = jnp.where(
        row_pos == well_row, column[8 + cols : 9 + cols], 0.0
    )


    def mobility(s):
        water = 2.0 * s * s
        rest = 1.0 - s
        return water, water + rest * rest

    def mobility_row(x, _):
        water, t = mobility(sat[row(x), :])
        mob[row(x), :] = t
        frac[row(x), :] = water / t

    each_row(mobility_row)
    spot = spots[...]
    lane_spot = lax.broadcasted_iota(jnp.int32, (layers, 128), 1)
    picked = sum(product(v, spot, ((1,), (0,))) for v in split(mob[...]))
    own[0] = jnp.sum(picked * select[pl.ds(0, cells), :], axis=0, keepdims=True)
    well_z.start(own.at[0])

    lane_z = lax.broadcasted_iota(jnp.int32, (cols, layers), 1)
    col_y = lax.broadcasted_iota(jnp.int32, (cols, layers), 0)
    inner_z = lane_z < layers - 1
    inner_y = col_y < cols - 1

    def next_y(v):
        return pltpu.roll(v, cols - 1, 0)

    def last_y(v):
        return pltpu.roll(v, 1, 0)

    def next_z(v):
        return pltpu.roll(v, layers - 1, 1)

    def last_z(v):
        return pltpu.roll(v, 1, 1)

    def place(chosen):
        return sum(product(v, spot, ((1,), (1,))) for v in split(chosen))

    loads[3].wait()
    largest = jnp.zeros((1, 128), jnp.float32)
    for b in range(blocks):
        lower = fac[b]
        high, low = split(lower)
        over = ((0,), (0,))
        gram = product(high, high, over) + product(high, low, over) + product(low, high, over)
        prod_hi[b], prod_lo[b] = split(gram)
        row_sum = jnp.sum(jnp.abs(gram), axis=0, keepdims=True)
        largest = jnp.maximum(largest, jnp.max(row_sum, axis=1, keepdims=True))
    own[1] = largest
    scale_x.start(own.at[1])

    for x in range(1, rows - 1):
        fill_row(x)
    chosen = select[pl.ds(0, cells), :]
    well_d[...] = place(chosen * is_producer)
    well_e[...] = place(chosen * pressure_row)

    zero_row = jnp.zeros((cols, layers), jnp.float32)

    def flux_row(x, flux_last):
        here, there = row(x), row(jnp.minimum(x + 1, rows - 1))
        k, p, f = perm[here, :], prs[here, :], frac[here, :]
        kx, px, fx = perm[there, :], prs[there, :], frac[there, :]
        tx = harmonic(k, kx)
        ty = jnp.where(inner_y, harmonic(k, next_y(k)), 0.0)
        tz = jnp.where(inner_z, 0.1 * harmonic(k, next_z(k)), 0.0)
        face_x[here, :] = tx
        face_y[here, :] = ty
        face_z[here, :] = tz
        wx = upwind(tx, p, px, f, fx)
        wy = upwind(ty, p, next_y(p), f, next_y(f))
        wz = upwind(tz, p, next_z(p), f, next_z(f))
        s = sat[here, :]
        made = 2.0 * s * s * (p * well_d[here, :] - well_e[here, :])
        moved[here, :] = s - dtp[here, :] * (
            made + (wx - flux_last) + (wy - last_y(wy)) + (wz - last_z(wz))
        )
        return wx

    each_row(flux_row, zero_row)

    def fraction(s):
        water, t = mobility(s)
        return water / t

    first, final = pl.ds(0, cols), pl.ds(cells - cols, cols)
    take_faces(INPUT)
    t = harmonic(input_x[0, PERM], perm[first, :])
    low_x[...] = t
    moved[first, :] += dtp[first, :] * upwind(
        t, input_x[0, PRS], prs[first, :], fraction(input_x[0, SAT]), frac[first, :]
    )
    t = harmonic(perm[final, :], input_x[1, PERM])
    high_x[...] = t
    moved[final, :] -= dtp[final, :] * upwind(
        t, prs[final, :], input_x[1, PRS], frac[final, :], fraction(input_x[1, SAT])
    )
    pack, rim = input_pack, input_y
    t = harmonic(rim[0, PERM], pack[0, PERM])
    side_y[0] = t
    flux = upwind(t, rim[0, PRS], pack[0, PRS], fraction(rim[0, SAT]), fraction(pack[0, SAT]))
    rims = [take(moved, 0) + pack[0, DTP] * flux]
    t = harmonic(pack[1, PERM], rim[1, PERM])
    side_y[1] = t
    flux = upwind(t, pack[1, PRS], rim[1, PRS], fraction(pack[1, SAT]), fraction(rim[1, SAT]))
    rims.append(take(moved, cols - 1) - pack[1, DTP] * flux)
    for i, c in ((0, 0), (1, cols - 1)):
        pack_y[MOVED - 1, i] = rims[i]
        put(moved, c, rims[i])
    send_faces(MOVED)
    own[3] = jnp.sum(well_z.take(own[0]), axis=0)
    well_xy.start(own.at[3])
    own[2] = jnp.max(scale_x.take(own[1]), axis=0)
    scale_y.start(own.at[2])

    chosen = split(select[...])
    for w in range(injectors):
        alone = jnp.where(lane_spot == producers + w, spot, jnp.zeros_like(spot))
        source[w] = sum(product(v, alone, ((1,), (1,))) for v in chosen)

    sums = jnp.sum(well_xy.take(own[3]), axis=0)
    scale = jnp.where(sums > 0.0, rate_row / jnp.where(sums > 0.0, sums, 1.0), 0.0)
    shares = [scale[:, producers + w : producers + w + 1] for w in range(injectors)]

    def weights(at):
        return sum(share * source[w, at, :] for w, share in enumerate(shares))


    def moved_row(x, _):
        here = row(x)
        made = mob[here, :] * weights(here)
        s = moved[here, :] + dtp[here, :] * made
        satn[here, :] = s
        resid[here, :] = made
        total[here, :] = mobility(s)[1]

    each_row(moved_row)

    store_satn = pltpu.make_async_copy(satn, satn_out, store_sem.at[0])
    store_satn.start()

    def residual_row(x, flux_last):
        here, there = row(x), row(jnp.minimum(x + 1, rows - 1))
        t, tx = total[here, :], total[there, :]
        p, px = prs[here, :], prs[there, :]
        cx = face_x[here, :] * (0.5 * (t + tx))
        cy = face_y[here, :] * (0.5 * (t + next_y(t)))
        cz = face_z[here, :] * (0.5 * (t + next_z(t)))
        face_x[here, :] = cx
        face_y[here, :] = cy
        face_z[here, :] = cz
        d, e = well_d[here, :], well_e[here, :]
        diag[here, :] = poro[here, :] + d * t
        fx = cx * (p - px)
        fy = cy * (p - next_y(p))
        fz = cz * (p - next_z(p))
        resid[here, :] = (
            resid[here, :]
            + t * (e - d * p)
            - ((fx - flux_last) + (fy - last_y(fy)) + (fz - last_z(fz)))
        )
        return fx

    each_row(residual_row, zero_row)

    own[4] = jnp.max(scale_y.take(own[2]), axis=0)
    scale_z.start(own.at[4])

    def rim_total(before, sat_rim, dtp_rim, weight):
        s = before + dtp_rim * (mobility(sat_rim)[1] * weight)
        return mobility(s)[1]

    pack_total = [take(total, 0), take(total, cols - 1)]
    edge = []
    take_faces(MOVED)
    for d in range(4):
        pl.when(hears[d])(lambda: late_copy(d).wait_recv())
    t = rim_total(
        halo_x[MOVED - 1, 0], input_x[0, SAT], input_x[0, DTP], weights(pl.ds(cells, cols))
    )
    c = low_x[...] * (0.5 * (total[first, :] + t))
    low_x[...] = c
    resid[first, :] -= c * (prs[first, :] - input_x[0, PRS])
    t = rim_total(
        halo_x[MOVED - 1, 1],
        input_x[1, SAT],
        input_x[1, DTP],
        weights(pl.ds(cells + cols, cols)),
    )
    c = high_x[...] * (0.5 * (total[final, :] + t))
    high_x[...] = c
    resid[final, :] -= c * (prs[final, :] - input_x[1, PRS])
    for i, at in ((0, 0), (1, cols - 1)):
        t = rim_total(
            halo_y[MOVED - 1, i],
            rim[i, SAT],
            rim[i, DTP],
            weights(pl.ds(rim_y + i * rows, rows)),
        )
        c = side_y[i] * (0.5 * (pack_total[i] + t))
        side_y[i] = c
        edge.append(take(resid, at) - c * (pack[i, PRS] - rim[i, PRS]))
        put(resid, at, edge[i])

    def apply(v, b, factor):
        high, low = split(v if factor is None else v * factor)
        z = jnp.dot(high, prod_hi[b], preferred_element_type=jnp.float32)
        z += jnp.dot(high, prod_lo[b], preferred_element_type=jnp.float32)
        return z + jnp.dot(low, prod_hi[b], preferred_element_type=jnp.float32)

    def precondition(src, dst, factor):
        for b in range(blocks):
            parts = [
                src[pl.ds(x * cols + b * BLOCK, BLOCK), :] for x in range(rows)
            ]
            z = apply(jnp.concatenate(parts, axis=0), b, factor)
            for x in range(rows):
                dst[pl.ds(x * cols + b * BLOCK, BLOCK), :] = z[x * BLOCK : (x + 1) * BLOCK]

    def precondition_rim(k, src, low_column, high_column, factor):
        for b in range(blocks):
            here = pl.ds(b * BLOCK, BLOCK)
            parts = [src[here, :], src[pl.ds(cells - cols + b * BLOCK, BLOCK), :]]
            if b == 0:
                parts.append(low_column)
            if b == blocks - 1:
                parts.append(high_column)
            z = apply(jnp.concatenate(parts, axis=0), b, factor)
            pack_x[k, 0, here, :] = z[:BLOCK]
            pack_x[k, 1, here, :] = z[BLOCK : 2 * BLOCK]
            if b == 0:
                pack_y[BASE - 1 + k, 0] = z[2 * BLOCK : 2 * BLOCK + rows]
            if b == blocks - 1:
                pack_y[BASE - 1 + k, 1] = z[-rows:]

    pairs = [(0, 0), (1, 0), (1, 1), (2, 0), (2, 1), (2, 2)]
    count = len(pairs) + BASIS
    last = len(pairs) - 1

    def fold(total_, term):
        for i in range(term.shape[0] // 8):
            total_ = total_ + term[8 * i : 8 * i + 8]
        return total_

    def dots_row(x, sums):
        here = row(x)
        v = [base[k, here, :] for k in range(BASIS)]
        u = [image[k, here, :] for k in range(BASIS)]
        r = resid[here, :]
        terms = [v[i] * u[j] for i, j in pairs] + [v[i] * r for i in range(BASIS)]
        return tuple(fold(s, term) for s, term in zip(sums, terms))

    def into_lane(i, s, message):
        s = jnp.sum(s, axis=0, keepdims=True)
        return jnp.where(lane == i, jnp.sum(s, axis=1, keepdims=True), message)

    stores = [store_satn]
    for k in range(BASIS):
        e = BASE + k
        vec, img = base.at[k], image.at[k]
        if k == 1:
            top = jnp.max(scale_z.take(own[4]), axis=0)
            norm = jnp.concatenate([1.0 / top] * (layers // 128), axis=1)
        factor = (lambda: None, lambda: (SHIFT * norm) * norm, lambda: SHIFT * norm)[k]()
        prior = resid if k == 0 else image.at[k - 1]
        precondition_rim(k, prior, edge[0], edge[1], factor)
        send_faces(e)
        precondition(prior, vec, factor)
        store = pltpu.make_async_copy(
            vec, (z0_out, z1_out, z2_out)[k], store_sem.at[1 + k]
        )
        store.start()
        stores.append(store)

        def image_row(x, flux_last, vec=vec, img=img):
            here, there = row(x), row(jnp.minimum(x + 1, rows - 1))
            v, vx = vec[here, :], vec[there, :]
            fx = face_x[here, :] * (v - vx)
            fy = face_y[here, :] * (v - next_y(v))
            fz = face_z[here, :] * (v - next_z(v))
            img[here, :] = (
                diag[here, :] * v
                + (fx - flux_last)
                + (fy - last_y(fy))
                + (fz - last_z(fz))
            )
            return fx

        each_row(image_row, zero_row)
        h = e - 1
        if k < BASIS - 1:
            take_faces(e)
            img[first, :] += low_x[...] * (vec[first, :] - halo_x[h, 0])
            img[final, :] += high_x[...] * (vec[final, :] - halo_x[h, 1])
            for i, at in ((0, 0), (1, cols - 1)):
                edge[i] = take(img, at) + side_y[i] * (pack_y[h, i] - halo_y[h, i])
                put(img, at, edge[i])
            continue
        sums = each_row(dots_row, (jnp.zeros((8, layers), jnp.float32),) * count)
        message = jnp.zeros((1, 128), jnp.float32)
        for i, s in enumerate(sums):
            if i != last:
                message = into_lane(i, s, message)
        take_faces(e)
        s = fold(sums[last], low_x[...] * (vec[first, :] - halo_x[h, 0]) * vec[first, :])
        s = fold(s, high_x[...] * (vec[final, :] - halo_x[h, 1]) * vec[final, :])
        for i in range(2):
            s = fold(s, side_y[i] * (pack_y[h, i] - halo_y[h, i]) * pack_y[h, i])
        message = into_lane(last, s, message)

    own[5] = message
    sum_plane.start(own.at[5])
    own[6] = jnp.sum(sum_plane.take(own[5]), axis=0)
    sum_z.start(own.at[6])
    result = jnp.sum(sum_z.take(own[6]), axis=0)
    val = [result[:, i : i + 1] for i in range(count)]
    g00, g10, g11, g20, g21, g22, b0, b1, b2 = val

    def ratio(a, b):
        good = b > 0.0
        return jnp.where(good, a / jnp.where(good, b, 1.0), 0.0)

    l10, l20 = ratio(g10, g00), ratio(g20, g00)
    d1 = g11 - l10 * g10
    e21 = g21 - l20 * g10
    l21 = ratio(e21, d1)
    d2 = g22 - l20 * g20 - l21 * e21
    y1 = b1 - l10 * b0
    y2 = b2 - l20 * b0 - l21 * y1
    c2 = ratio(y2, d2)
    c1 = ratio(y1, d1) - l21 * c2
    c0 = ratio(b0, g00) - l10 * c1 - l20 * c2
    for k, c in enumerate((c0, c1, c2)):
        coef_out[k : k + 1, :] = jnp.broadcast_to(c, (1, layers))

    for group in groups:
        group.whole().wait_send()
    for d in range(4):
        pl.when(sends[d])(lambda: face_copy(EXCHANGES - 1, d).wait_send())
        pl.when(sends[d])(lambda: late_copy(d).wait_send())
    for store in stores:
        store.wait()


def solution(mesh):
    n_gx, n_gy = mesh.shape["gx"], mesh.shape["gy"]

    def per_device(
        rock_type,
        perm_table,
        poro_table,
        saturation,
        pressure_old,
        factor_inverse,
        inject_cells,
        inject_index,
        inject_rate,
        produce_cells,
        produce_index,
        produce_pressure,
    ):
        rows, cols, layers = saturation.shape
        cells = rows * cols
        blocks = cols // BLOCK
        f32, bf16 = jnp.float32, jnp.bfloat16
        flat = (cells, layers)
        field = pltpu.VMEM(flat, f32)
        smem = pl.BlockSpec(memory_space=pltpu.SMEM)
        vmem = pl.BlockSpec(memory_space=pltpu.VMEM)
        hbm = pl.BlockSpec(memory_space=pltpu.HBM)
        out = pl.BlockSpec(memory_space=pl.ANY)
        plane = n_gx * (n_gy // RING)
        dma = pltpu.SemaphoreType.DMA
        scratch = [
            pltpu.VMEM((4,) + flat, f32),
            pltpu.VMEM(flat, jnp.int32),
            pltpu.VMEM((blocks, layers, layers), f32),
            pltpu.VMEM((blocks, layers, layers), bf16),
            pltpu.VMEM((blocks, layers, layers), bf16),
            field,
            field,
            field,
            pltpu.VMEM((cells + 2 * cols + 2 * rows, 128), f32),
            pltpu.VMEM((layers, 128), bf16),
            field,
            field,
            field,
            pltpu.VMEM((cols, layers), f32),
            pltpu.VMEM((cols, layers), f32),
            pltpu.VMEM((2, rows, layers), f32),
            field,
            field,
            field,
            pltpu.VMEM(
                (inject_index.shape[0], cells + 2 * cols + 2 * rows, layers), f32
            ),
            field,
            field,
            field,
            field,
            pltpu.VMEM((BASIS,) + flat, f32),
            pltpu.VMEM((BASIS,) + flat, f32),
            pltpu.VMEM((2, 4, cols, layers), f32),
            pltpu.VMEM((2, 4, rows, layers), f32),
            pltpu.VMEM((2, 4, rows, layers), f32),
            pltpu.VMEM((EXCHANGES - 1, 2, cols, layers), f32),
            pltpu.VMEM((EXCHANGES - 1, 2, rows, layers), f32),
            pltpu.VMEM((BASIS, 2, cols, layers), f32),
            pltpu.VMEM((EXCHANGES - 1, 2, rows, layers), f32),
            pltpu.VMEM((7, 1, 128), f32),
            pltpu.VMEM((9, 1, 128), f32),
            pltpu.VMEM((RING, 1, 128), f32),
            pltpu.VMEM((n_gx, 1, 128), f32),
            pltpu.VMEM((n_gy // RING, 1, 128), f32),
            pltpu.VMEM((RING, 1, 128), f32),
            pltpu.VMEM((plane, 1, 128), f32),
            pltpu.VMEM((RING, 1, 128), f32),
            dma((4,)),
            dma((1 + BASIS,)),
            dma((4,)),
            dma((2, 4)),
            dma((4,)),
            dma((4,)),
            dma((7,)),
            dma((7,)),
        ]
        operands = (
            jnp.swapaxes(inject_cells, 1, 2),
            inject_rate,
            jnp.swapaxes(produce_cells, 1, 2),
            produce_pressure,
            perm_table,
            poro_table,
            inject_index,
            produce_index,
            rock_type.reshape(flat),
            saturation.reshape(flat),
            pressure_old.reshape(flat),
            factor_inverse.reshape(blocks, layers, layers),
        )
        satn, z0, z1, z2, coef = pl.pallas_call(
            functools.partial(kernel, (rows, cols, layers, n_gx, n_gy)),
            out_shape=[
                *[jax.ShapeDtypeStruct(flat, f32)] * (1 + BASIS),
                jax.ShapeDtypeStruct((BASIS, layers), f32),
            ],
            in_specs=[smem] * 6 + [vmem] * 2 + [hbm] * 4,
            out_specs=[out] * (1 + BASIS) + [vmem],
            scratch_shapes=scratch,
            compiler_params=pltpu.CompilerParams(
                collective_id=0, has_side_effects=True, vmem_limit_bytes=24 * 1024 * 1024
            ),
            name="reservoir_step",
        )(*(pltpu.with_memory_space_constraint(a, pltpu.HBM) for a in operands))
        change = coef[0:1] * z0 + coef[1:2] * z1 + coef[2:3] * z2
        pressure = pressure_old.reshape(flat) + change
        return satn.reshape(saturation.shape), pressure.reshape(saturation.shape)

    grid = P("gx", "gy", None)
    in_specs = (grid, P(), P(), grid, grid, P("gx", "gy", None, None)) + (P(),) * 6
    return jax.shard_map(
        per_device, mesh=mesh, in_specs=in_specs, out_specs=(grid, grid), check_vma=False
    )
```

```python
import functools

import jax
import jax.numpy as jnp
from jax import lax
from jax.experimental import pallas as pl
from jax.experimental.pallas import tpu as pltpu
from jax.sharding import PartitionSpec as P

MESH = pl.DeviceIdType.MESH
BLOCK = 16
BASIS = 3
UNROLL = 4
CHUNKS = 4
RING = 8
TIME_STEP = 0.002
SHIFT = 2.0**-14

INPUT, MOVED, BASE = 0, 1, 2
EXCHANGES = BASE + BASIS
SAT, PRS, PERM, DTP = 0, 1, 2, 3
LO_X, HI_X, LO_Y, HI_Y = 0, 1, 2, 3
FAR_X = (4, 3, 5, 2, 6, 1, 7)
FAR_Y = (2, 1, 3)
FAR_Z = (4, 3, 5, 2, 6, 1, 7)


def harmonic(former, latter):
    return 2.0 * former * latter / (former + latter)


def upwind(face, p_a, p_b, f_a, f_b):
    flow = face * (p_a - p_b)
    return flow * jnp.where(flow > 0.0, f_a, f_b)


def kernel(
    sizes,
    inj_cell,
    inj_rate,
    pro_cell,
    pro_pressure,
    perm_table,
    poro_table,
    inj_index,
    pro_index,
    rock_hbm,
    sat_hbm,
    prs_hbm,
    fac_hbm,
    satn_out,
    z0_out,
    z1_out,
    z2_out,
    coef_out,
    inp,
    rock,
    fac,
    prod_hi,
    prod_lo,
    poro,
    frac,
    mob,
    select,
    spots,
    face_x,
    face_y,
    face_z,
    low_x,
    high_x,
    side_y,
    moved,
    well_d,
    well_e,
    source,
    satn,
    total,
    diag,
    resid,
    base,
    image,
    input_x,
    input_y,
    input_pack,
    halo_x,
    halo_y,
    pack_x,
    pack_y,
    own,
    slot_w,
    slot_v,
    slot_x,
    slot_y,
    slot_s,
    slot_a,
    slot_b,
    load_sem,
    store_sem,
    face_send,
    face_recv,
    late_send,
    late_recv,
    group_send,
    group_recv,
):
    rows, cols, layers, n_gx, n_gy = sizes
    blocks = cols // BLOCK
    cells = rows * cols
    full_cols = cols * n_gy
    n_y = n_gy // RING
    plane = n_gx * n_y
    injectors = inj_index.shape[0]
    producers = pro_index.shape[0]
    perfs = inj_index.shape[1]
    sat, prs, perm, dtp = (inp.at[i] for i in range(4))

    gx = lax.axis_index("gx")
    gy = lax.axis_index("gy")
    yy = gy // RING
    zz = gy % RING
    spot_a = gx * n_y + yy

    def row(x):
        return pl.ds(pl.multiple_of(x * cols, cols), cols)

    def take(ref, c):
        parts = [ref[pl.ds(x * cols + c, 1), :] for x in range(rows)]
        return jnp.concatenate(parts, axis=0)

    def put(ref, c, value):
        for x in range(rows):
            ref[pl.ds(x * cols + c, 1), :] = value[x : x + 1]

    neighbours = (
        (lax.rem(gx + n_gx - 1, n_gx), gy),
        (lax.rem(gx + 1, n_gx), gy),
        (gx, lax.rem(gy + n_gy - 1, n_gy)),
        (gx, lax.rem(gy + 1, n_gy)),
    )
    sends = (gx > 0, gx < n_gx - 1, gy > 0, gy < n_gy - 1)
    hears = (gx < n_gx - 1, gx > 0, gy < n_gy - 1, gy > 0)

    def near(a, b, c=0):
        y = lax.rem(yy + b, n_y) if b else yy
        z = lax.rem(zz + c, RING) if c else zz
        return (lax.rem(gx + a, n_gx) if a else gx, y * RING + z)

    around_peers = [
        near(a, b) for a in (n_gx - 1, 1, 0) for b in (n_y - 1, 1, 0) if a or b
    ]
    x_peers = [near(a, 0) for a in FAR_X]
    y_peers = [near(0, b) for b in FAR_Y]
    z_peers = [near(0, 0, c) for c in FAR_Z]
    plane_peers = [near(a, b) for a in FAR_X + (0,) for b in FAR_Y + (0,) if a or b]

    def each_row(body, carry=None):
        def step(i, kept):
            for j in range(UNROLL):
                kept = body(i * UNROLL + j, kept)
            return kept

        if carry is None:
            pl.loop(0, rows // UNROLL)(lambda i: step(i, None) and None)
        else:
            carry = lax.fori_loop(0, rows // UNROLL, step, carry)
        return carry

    def split(v):
        high = v.astype(jnp.bfloat16)
        return high, (v - high.astype(jnp.float32)).astype(jnp.bfloat16)

    def product(a, b, dims):
        return lax.dot_general(a, b, (dims, ((), ())), preferred_element_type=jnp.float32)

    loads = [
        pltpu.make_async_copy(src, dst, load_sem.at[i])
        for i, (src, dst) in enumerate(
            ((sat_hbm, sat), (rock_hbm, rock), (prs_hbm, prs), (fac_hbm, fac))
        )
    ]
    for load in loads:
        load.start()

    barrier = pltpu.get_barrier_semaphore()

    def greet(peer):
        pl.semaphore_signal(barrier, inc=1, device_id=peer, device_id_type=MESH)

    for peer in neighbours[2:] + tuple(plane_peers[::-1]) + tuple(z_peers[::-1]):
        greet(peer)

    def clear_x(at):
        input_x[at] = jnp.zeros(input_x.shape[1:], jnp.float32)
        for e in range(EXCHANGES - 1):
            halo_x[e, at] = jnp.zeros(halo_x.shape[2:], jnp.float32)

    def clear_y(at):
        input_y[at] = jnp.zeros(input_y.shape[1:], jnp.float32)
        for e in range(EXCHANGES - 1):
            halo_y[e, at] = jnp.zeros(halo_y.shape[2:], jnp.float32)

    pl.when(gx == 0)(lambda: clear_x(0))
    pl.when(gx == n_gx - 1)(lambda: clear_x(1))
    pl.when(gy == 0)(lambda: clear_y(0))
    pl.when(gy == n_gy - 1)(lambda: clear_y(1))

    def lookup(kind, table):
        bit0 = (kind & 1) == 1
        bit1 = (kind & 2) == 2
        pairs = [jnp.where(bit0, table[2 * i + 1], table[2 * i]) for i in range(4)]
        high = jnp.where(bit1, pairs[3], pairs[2])
        return jnp.where(kind >= 4, high, jnp.where(bit1, pairs[1], pairs[0]))

    def fill_row(x, _=None):
        kind = rock[row(x), :]
        perm[row(x), :] = lookup(kind, perm_table)
        porosity = lookup(kind, poro_table)
        poro[row(x), :] = porosity
        dtp[row(x), :] = TIME_STEP / porosity

    loads[1].wait()
    for i, c in ((0, 0), (1, cols - 1)):
        kind = take(rock, c)
        input_pack[i, PERM] = lookup(kind, perm_table)
        input_pack[i, DTP] = TIME_STEP / lookup(kind, poro_table)
    fill_row(0)
    fill_row(rows - 1)
    loads[0].wait()
    loads[2].wait()
    for i, c in ((0, 0), (1, cols - 1)):
        input_pack[i, SAT] = take(sat, c)
        input_pack[i, PRS] = take(prs, c)

    def face_copy(e, d):
        if e == INPUT:
            soon = pl.ds(0, DTP)
            if d < 2:
                src = inp.at[soon, pl.ds(0 if d == LO_X else cells - cols, cols), :]
                dst = input_x.at[1 - d, soon]
            else:
                src, dst = input_pack.at[d - 2, soon], input_y.at[3 - d, soon]
        else:
            if d < 2:
                at = pl.ds(0 if d == LO_X else cells - cols, cols)
                src = moved.at[at, :] if e == MOVED else pack_x.at[e - BASE, d]
                dst = halo_x.at[e - 1, 1 - d]
            else:
                src, dst = pack_y.at[e - 1, d - 2], halo_y.at[e - 1, 3 - d]
        return pltpu.make_async_remote_copy(
            src_ref=src,
            dst_ref=dst,
            send_sem=face_send.at[d],
            recv_sem=face_recv.at[e % 2, d],
            device_id=neighbours[d],
            device_id_type=MESH,
        )

    def send_faces(e):
        for d in (LO_Y, HI_Y, LO_X, HI_X):

            @pl.when(sends[d])
            def _():
                if e > 0:
                    face_copy(e - 1, d).wait_send()
                face_copy(e, d).start()

    def take_faces(e):
        for d in range(4):
            pl.when(hears[d])(lambda: face_copy(e, d).wait_recv())

    def late_copy(d):
        if d < 2:
            src = dtp.at[pl.ds(0 if d == LO_X else cells - cols, cols), :]
            dst = input_x.at[1 - d, DTP]
        else:
            src, dst = input_pack.at[d - 2, DTP], input_y.at[3 - d, DTP]
        return pltpu.make_async_remote_copy(
            src_ref=src,
            dst_ref=dst,
            send_sem=late_send.at[d],
            recv_sem=late_recv.at[d],
            device_id=neighbours[d],
            device_id_type=MESH,
        )

    class Group:
        def __init__(self, k, peers, slots):
            self.k, self.peers, self.slots = k, peers, slots

        def copy(self, src, dst, peer):
            return pltpu.make_async_remote_copy(
                src_ref=src,
                dst_ref=dst,
                send_sem=group_send.at[self.k],
                recv_sem=group_recv.at[self.k],
                device_id=peer,
                device_id_type=MESH,
            )

        def start(self, src):
            for i, peer in enumerate(self.peers):
                self.copy(src, self.slots.at[i], peer).start()

        def whole(self):
            held = self.slots.at[pl.ds(0, len(self.peers))]
            return self.copy(held, held, self.peers[0])

        def take(self, mine):
            self.whole().wait_recv()
            self.slots[len(self.peers)] = mine
            return self.slots[...]

    well_z = Group(0, z_peers, slot_v)
    well_xy = Group(6, around_peers, slot_w)
    scale_x = Group(1, x_peers, slot_x)
    scale_y = Group(2, y_peers, slot_y)
    scale_z = Group(3, z_peers, slot_s)
    sum_plane = Group(4, plane_peers, slot_a)
    sum_z = Group(5, z_peers, slot_b)
    groups = (well_z, well_xy, scale_x, scale_y, scale_z, sum_plane, sum_z)

    pl.semaphore_wait(barrier, 2 + len(plane_peers) + len(z_peers))
    send_faces(INPUT)
    for d in range(4):
        pl.when(sends[d])(lambda: late_copy(d).start())

    lane = lax.broadcasted_iota(jnp.int32, (1, 128), 1)
    well_row = jnp.full((1, 128), -9, jnp.int32)
    well_layer = jnp.full((1, 128), -9, jnp.int32)
    pressure_row = jnp.zeros((1, 128), jnp.float32)
    rate_row = jnp.zeros((1, 128), jnp.float32)
    wide = cols + 16
    spread = lax.broadcasted_iota(jnp.int32, (wide, perfs), 0) - lax.broadcasted_iota(
        jnp.int32, (wide, perfs), 1
    )
    lane_wide = lax.broadcasted_iota(jnp.int32, (wide, 128), 1)
    column = jnp.zeros((wide, 128), jnp.float32)
    for w in range(producers + injectors):
        produces = w < producers
        cell_ref = pro_cell if produces else inj_cell
        index_ref = pro_index if produces else inj_index
        i = w if produces else w - producers
        cell = cell_ref[i, 0, 0]
        well_row = jnp.where(lane == w, cell // full_cols - gx * rows, well_row)
        well_layer = jnp.where(lane == w, cell_ref[i, 1, 0], well_layer)
        start = cell % full_cols
        offset = spread + (gy * cols - 8 - start)
        hit = jnp.where(
            (offset == 0) | (offset == full_cols) | (offset == -full_cols),
            index_ref[i : i + 1, :],
            0.0,
        )
        column = jnp.where(lane_wide == w, jnp.sum(hit, axis=1, keepdims=True), column)
        if produces:
            pressure_row = jnp.where(lane == w, pro_pressure[i], pressure_row)
        else:
            rate_row = jnp.where(lane == w, inj_rate[i], rate_row)
    is_producer = jnp.where(lane < producers, 1.0, 0.0)
    layer_pos = lax.broadcasted_iota(jnp.int32, (layers, 128), 0)
    spots[...] = jnp.where(layer_pos == well_layer, 1.0, 0.0).astype(jnp.bfloat16)
    own_column = column[8 : 8 + cols]
    for x in range(rows):
        select[x * cols : (x + 1) * cols, :] = jnp.where(well_row == x, own_column, 0.0)
    select[cells : cells + cols, :] = jnp.where(well_row == -1, own_column, 0.0)
    select[cells + cols : cells + 2 * cols, :] = jnp.where(well_row == rows, own_column, 0.0)
    row_pos = lax.broadcasted_iota(jnp.int32, (rows, 128), 0)
    rim_y = cells + 2 * cols
    select[rim_y : rim_y + rows, :] = jnp.where(row_pos == well_row, column[7:8], 0.0)
    select[rim_y + rows : rim_y + 2 * rows, :] = jnp.where(
        row_pos == well_row, column[8 + cols : 9 + cols], 0.0
    )


    def mobility(s):
        water = 2.0 * s * s
        rest = 1.0 - s
        return water, water + rest * rest

    def mobility_row(x, _):
        water, t = mobility(sat[row(x), :])
        mob[row(x), :] = t
        frac[row(x), :] = water / t

    each_row(mobility_row)
    spot = spots[...]
    lane_spot = lax.broadcasted_iota(jnp.int32, (layers, 128), 1)
    picked = sum(product(v, spot, ((1,), (0,))) for v in split(mob[...]))
    own[0] = jnp.sum(picked * select[pl.ds(0, cells), :], axis=0, keepdims=True)
    well_z.start(own.at[0])

    lane_z = lax.broadcasted_iota(jnp.int32, (cols, layers), 1)
    col_y = lax.broadcasted_iota(jnp.int32, (cols, layers), 0)
    inner_z = lane_z < layers - 1
    inner_y = col_y < cols - 1

    def next_y(v):
        return pltpu.roll(v, cols - 1, 0)

    def last_y(v):
        return pltpu.roll(v, 1, 0)

    def next_z(v):
        return pltpu.roll(v, layers - 1, 1)

    def last_z(v):
        return pltpu.roll(v, 1, 1)

    def place(chosen):
        return sum(product(v, spot, ((1,), (1,))) for v in split(chosen))

    loads[3].wait()
    largest = jnp.zeros((1, 128), jnp.float32)
    for b in range(blocks):
        lower = fac[b]
        high, low = split(lower)
        over = ((0,), (0,))
        gram = product(high, high, over) + product(high, low, over) + product(low, high, over)
        prod_hi[b], prod_lo[b] = split(gram)
        row_sum = jnp.sum(jnp.abs(gram), axis=0, keepdims=True)
        largest = jnp.maximum(largest, jnp.max(row_sum, axis=1, keepdims=True))
    own[1] = largest
    scale_x.start(own.at[1])

    for x in range(1, rows - 1):
        fill_row(x)
    chosen = select[pl.ds(0, cells), :]
    well_d[...] = place(chosen * is_producer)
    well_e[...] = place(chosen * pressure_row)

    zero_row = jnp.zeros((cols, layers), jnp.float32)

    def flux_row(x, flux_last):
        here, there = row(x), row(jnp.minimum(x + 1, rows - 1))
        k, p, f = perm[here, :], prs[here, :], frac[here, :]
        kx, px, fx = perm[there, :], prs[there, :], frac[there, :]
        tx = harmonic(k, kx)
        ty = jnp.where(inner_y, harmonic(k, next_y(k)), 0.0)
        tz = jnp.where(inner_z, 0.1 * harmonic(k, next_z(k)), 0.0)
        face_x[here, :] = tx
        face_y[here, :] = ty
        face_z[here, :] = tz
        wx = upwind(tx, p, px, f, fx)
        wy = upwind(ty, p, next_y(p), f, next_y(f))
        wz = upwind(tz, p, next_z(p), f, next_z(f))
        s = sat[here, :]
        made = 2.0 * s * s * (p * well_d[here, :] - well_e[here, :])
        moved[here, :] = s - dtp[here, :] * (
            made + (wx - flux_last) + (wy - last_y(wy)) + (wz - last_z(wz))
        )
        return wx

    each_row(flux_row, zero_row)

    def fraction(s):
        water, t = mobility(s)
        return water / t

    first, final = pl.ds(0, cols), pl.ds(cells - cols, cols)
    take_faces(INPUT)
    t = harmonic(input_x[0, PERM], perm[first, :])
    low_x[...] = t
    moved[first, :] += dtp[first, :] * upwind(
        t, input_x[0, PRS], prs[first, :], fraction(input_x[0, SAT]), frac[first, :]
    )
    t = harmonic(perm[final, :], input_x[1, PERM])
    high_x[...] = t
    moved[final, :] -= dtp[final, :] * upwind(
        t, prs[final, :], input_x[1, PRS], frac[final, :], fraction(input_x[1, SAT])
    )
    pack, rim = input_pack, input_y
    t = harmonic(rim[0, PERM], pack[0, PERM])
    side_y[0] = t
    flux = upwind(t, rim[0, PRS], pack[0, PRS], fraction(rim[0, SAT]), fraction(pack[0, SAT]))
    rims = [take(moved, 0) + pack[0, DTP] * flux]
    t = harmonic(pack[1, PERM], rim[1, PERM])
    side_y[1] = t
    flux = upwind(t, pack[1, PRS], rim[1, PRS], fraction(pack[1, SAT]), fraction(rim[1, SAT]))
    rims.append(take(moved, cols - 1) - pack[1, DTP] * flux)
    for i, c in ((0, 0), (1, cols - 1)):
        pack_y[MOVED - 1, i] = rims[i]
        put(moved, c, rims[i])
    send_faces(MOVED)
    own[3] = jnp.sum(well_z.take(own[0]), axis=0)
    well_xy.start(own.at[3])
    own[2] = jnp.max(scale_x.take(own[1]), axis=0)
    scale_y.start(own.at[2])

    chosen = split(select[...])
    for w in range(injectors):
        alone = jnp.where(lane_spot == producers + w, spot, jnp.zeros_like(spot))
        source[w] = sum(product(v, alone, ((1,), (1,))) for v in chosen)

    sums = jnp.sum(well_xy.take(own[3]), axis=0)
    scale = jnp.where(sums > 0.0, rate_row / jnp.where(sums > 0.0, sums, 1.0), 0.0)
    shares = [scale[:, producers + w : producers + w + 1] for w in range(injectors)]

    def weights(at):
        return sum(share * source[w, at, :] for w, share in enumerate(shares))


    def moved_row(x, _):
        here = row(x)
        made = mob[here, :] * weights(here)
        s = moved[here, :] + dtp[here, :] * made
        satn[here, :] = s
        resid[here, :] = made
        total[here, :] = mobility(s)[1]

    each_row(moved_row)

    store_satn = pltpu.make_async_copy(satn, satn_out, store_sem.at[0])
    store_satn.start()

    def residual_row(x, flux_last):
        here, there = row(x), row(jnp.minimum(x + 1, rows - 1))
        t, tx = total[here, :], total[there, :]
        p, px = prs[here, :], prs[there, :]
        cx = face_x[here, :] * (0.5 * (t + tx))
        cy = face_y[here, :] * (0.5 * (t + next_y(t)))
        cz = face_z[here, :] * (0.5 * (t + next_z(t)))
        face_x[here, :] = cx
        face_y[here, :] = cy
        face_z[here, :] = cz
        d, e = well_d[here, :], well_e[here, :]
        diag[here, :] = poro[here, :] + d * t
        fx = cx * (p - px)
        fy = cy * (p - next_y(p))
        fz = cz * (p - next_z(p))
        resid[here, :] = (
            resid[here, :]
            + t * (e - d * p)
            - ((fx - flux_last) + (fy - last_y(fy)) + (fz - last_z(fz)))
        )
        return fx

    each_row(residual_row, zero_row)

    own[4] = jnp.max(scale_y.take(own[2]), axis=0)
    scale_z.start(own.at[4])

    def rim_total(before, sat_rim, dtp_rim, weight):
        s = before + dtp_rim * (mobility(sat_rim)[1] * weight)
        return mobility(s)[1]

    pack_total = [take(total, 0), take(total, cols - 1)]
    edge = []
    take_faces(MOVED)
    for d in range(4):
        pl.when(hears[d])(lambda: late_copy(d).wait_recv())
    t = rim_total(
        halo_x[MOVED - 1, 0], input_x[0, SAT], input_x[0, DTP], weights(pl.ds(cells, cols))
    )
    c = low_x[...] * (0.5 * (total[first, :] + t))
    low_x[...] = c
    resid[first, :] -= c * (prs[first, :] - input_x[0, PRS])
    t = rim_total(
        halo_x[MOVED - 1, 1],
        input_x[1, SAT],
        input_x[1, DTP],
        weights(pl.ds(cells + cols, cols)),
    )
    c = high_x[...] * (0.5 * (total[final, :] + t))
    high_x[...] = c
    resid[final, :] -= c * (prs[final, :] - input_x[1, PRS])
    for i, at in ((0, 0), (1, cols - 1)):
        t = rim_total(
            halo_y[MOVED - 1, i],
            rim[i, SAT],
            rim[i, DTP],
            weights(pl.ds(rim_y + i * rows, rows)),
        )
        c = side_y[i] * (0.5 * (pack_total[i] + t))
        side_y[i] = c
        edge.append(take(resid, at) - c * (pack[i, PRS] - rim[i, PRS]))
        put(resid, at, edge[i])

    def apply(v, b, factor):
        high, low = split(v if factor is None else v * factor)
        z = jnp.dot(high, prod_hi[b], preferred_element_type=jnp.float32)
        z += jnp.dot(high, prod_lo[b], preferred_element_type=jnp.float32)
        return z + jnp.dot(low, prod_hi[b], preferred_element_type=jnp.float32)

    def precondition(src, dst, factor):
        for b in range(blocks):
            parts = [
                src[pl.ds(x * cols + b * BLOCK, BLOCK), :] for x in range(rows)
            ]
            z = apply(jnp.concatenate(parts, axis=0), b, factor)
            for x in range(rows):
                dst[pl.ds(x * cols + b * BLOCK, BLOCK), :] = z[x * BLOCK : (x + 1) * BLOCK]

    def precondition_rim(k, src, low_column, high_column, factor):
        for b in range(blocks):
            here = pl.ds(b * BLOCK, BLOCK)
            parts = [src[here, :], src[pl.ds(cells - cols + b * BLOCK, BLOCK), :]]
            if b == 0:
                parts.append(low_column)
            if b == blocks - 1:
                parts.append(high_column)
            z = apply(jnp.concatenate(parts, axis=0), b, factor)
            pack_x[k, 0, here, :] = z[:BLOCK]
            pack_x[k, 1, here, :] = z[BLOCK : 2 * BLOCK]
            if b == 0:
                pack_y[BASE - 1 + k, 0] = z[2 * BLOCK : 2 * BLOCK + rows]
            if b == blocks - 1:
                pack_y[BASE - 1 + k, 1] = z[-rows:]

    pairs = [(0, 0), (1, 0), (1, 1), (2, 0), (2, 1), (2, 2)]
    count = len(pairs) + BASIS
    last = len(pairs) - 1

    def fold(total_, term):
        for i in range(term.shape[0] // 8):
            total_ = total_ + term[8 * i : 8 * i + 8]
        return total_

    def dots_row(x, sums):
        here = row(x)
        v = [base[k, here, :] for k in range(BASIS)]
        u = [image[k, here, :] for k in range(BASIS)]
        r = resid[here, :]
        terms = [v[i] * u[j] for i, j in pairs] + [v[i] * r for i in range(BASIS)]
        return tuple(fold(s, term) for s, term in zip(sums, terms))

    def into_lane(i, s, message):
        s = jnp.sum(s, axis=0, keepdims=True)
        return jnp.where(lane == i, jnp.sum(s, axis=1, keepdims=True), message)

    stores = [store_satn]
    for k in range(BASIS):
        e = BASE + k
        vec, img = base.at[k], image.at[k]
        if k == 1:
            top = jnp.max(scale_z.take(own[4]), axis=0)
            norm = jnp.concatenate([1.0 / top] * (layers // 128), axis=1)
        factor = (lambda: None, lambda: (SHIFT * norm) * norm, lambda: SHIFT * norm)[k]()
        prior = resid if k == 0 else image.at[k - 1]
        precondition_rim(k, prior, edge[0], edge[1], factor)
        send_faces(e)
        precondition(prior, vec, factor)
        store = pltpu.make_async_copy(
            vec, (z0_out, z1_out, z2_out)[k], store_sem.at[1 + k]
        )
        store.start()
        stores.append(store)

        def image_row(x, flux_last, vec=vec, img=img):
            here, there = row(x), row(jnp.minimum(x + 1, rows - 1))
            v, vx = vec[here, :], vec[there, :]
            fx = face_x[here, :] * (v - vx)
            fy = face_y[here, :] * (v - next_y(v))
            fz = face_z[here, :] * (v - next_z(v))
            img[here, :] = (
                diag[here, :] * v
                + (fx - flux_last)
                + (fy - last_y(fy))
                + (fz - last_z(fz))
            )
            return fx

        each_row(image_row, zero_row)
        h = e - 1
        if k < BASIS - 1:
            take_faces(e)
            img[first, :] += low_x[...] * (vec[first, :] - halo_x[h, 0])
            img[final, :] += high_x[...] * (vec[final, :] - halo_x[h, 1])
            for i, at in ((0, 0), (1, cols - 1)):
                edge[i] = take(img, at) + side_y[i] * (pack_y[h, i] - halo_y[h, i])
                put(img, at, edge[i])
            continue
        sums = each_row(dots_row, (jnp.zeros((8, layers), jnp.float32),) * count)
        message = jnp.zeros((1, 128), jnp.float32)
        for i, s in enumerate(sums):
            if i != last:
                message = into_lane(i, s, message)
        take_faces(e)
        s = fold(sums[last], low_x[...] * (vec[first, :] - halo_x[h, 0]) * vec[first, :])
        s = fold(s, high_x[...] * (vec[final, :] - halo_x[h, 1]) * vec[final, :])
        for i in range(2):
            s = fold(s, side_y[i] * (pack_y[h, i] - halo_y[h, i]) * pack_y[h, i])
        message = into_lane(last, s, message)

    own[5] = message
    sum_plane.start(own.at[5])
    own[6] = jnp.sum(sum_plane.take(own[5]), axis=0)
    sum_z.start(own.at[6])
    result = jnp.sum(sum_z.take(own[6]), axis=0)
    val = [result[:, i : i + 1] for i in range(count)]
    g00, g10, g11, g20, g21, g22, b0, b1, b2 = val

    def ratio(a, b):
        good = b > 0.0
        return jnp.where(good, a / jnp.where(good, b, 1.0), 0.0)

    l10, l20 = ratio(g10, g00), ratio(g20, g00)
    d1 = g11 - l10 * g10
    e21 = g21 - l20 * g10
    l21 = ratio(e21, d1)
    d2 = g22 - l20 * g20 - l21 * e21
    y1 = b1 - l10 * b0
    y2 = b2 - l20 * b0 - l21 * y1
    c2 = ratio(y2, d2)
    c1 = ratio(y1, d1) - l21 * c2
    c0 = ratio(b0, g00) - l10 * c1 - l20 * c2
    for k, c in enumerate((c0, c1, c2)):
        coef_out[k : k + 1, :] = jnp.broadcast_to(c, (1, layers))

    for group in groups:
        group.whole().wait_send()
    for d in range(4):
        pl.when(sends[d])(lambda: face_copy(EXCHANGES - 1, d).wait_send())
        pl.when(sends[d])(lambda: late_copy(d).wait_send())
    for store in stores:
        store.wait()


def closing(coef, prs, z0, z1, z2, satn, satn_out, out, result, sems):
    stores = [pltpu.make_async_copy(satn, satn_out, sems.at[CHUNKS])]
    stores[0].start()
    size = prs.shape[0] // CHUNKS
    for i in range(CHUNKS):
        at = pl.ds(i * size, size)
        result[at, :] = prs[at, :] + (
            coef[0:1, :] * z0[at, :] + coef[1:2, :] * z1[at, :] + coef[2:3, :] * z2[at, :]
        )
        store = pltpu.make_async_copy(result.at[at], out.at[at], sems.at[i])
        store.start()
        stores.append(store)
    for store in stores:
        store.wait()


def solution(mesh):
    n_gx, n_gy = mesh.shape["gx"], mesh.shape["gy"]

    def per_device(
        rock_type,
        perm_table,
        poro_table,
        saturation,
        pressure_old,
        factor_inverse,
        inject_cells,
        inject_index,
        inject_rate,
        produce_cells,
        produce_index,
        produce_pressure,
    ):
        rows, cols, layers = saturation.shape
        cells = rows * cols
        blocks = cols // BLOCK
        f32, bf16 = jnp.float32, jnp.bfloat16
        flat = (cells, layers)
        field = pltpu.VMEM(flat, f32)
        smem = pl.BlockSpec(memory_space=pltpu.SMEM)
        vmem = pl.BlockSpec(memory_space=pltpu.VMEM)
        hbm = pl.BlockSpec(memory_space=pltpu.HBM)
        out = pl.BlockSpec(memory_space=pl.ANY)
        plane = n_gx * (n_gy // RING)
        dma = pltpu.SemaphoreType.DMA
        scratch = [
            pltpu.VMEM((4,) + flat, f32),
            pltpu.VMEM(flat, jnp.int32),
            pltpu.VMEM((blocks, layers, layers), f32),
            pltpu.VMEM((blocks, layers, layers), bf16),
            pltpu.VMEM((blocks, layers, layers), bf16),
            field,
            field,
            field,
            pltpu.VMEM((cells + 2 * cols + 2 * rows, 128), f32),
            pltpu.VMEM((layers, 128), bf16),
            field,
            field,
            field,
            pltpu.VMEM((cols, layers), f32),
            pltpu.VMEM((cols, layers), f32),
            pltpu.VMEM((2, rows, layers), f32),
            field,
            field,
            field,
            pltpu.VMEM(
                (inject_index.shape[0], cells + 2 * cols + 2 * rows, layers), f32
            ),
            field,
            field,
            field,
            field,
            pltpu.VMEM((BASIS,) + flat, f32),
            pltpu.VMEM((BASIS,) + flat, f32),
            pltpu.VMEM((2, 4, cols, layers), f32),
            pltpu.VMEM((2, 4, rows, layers), f32),
            pltpu.VMEM((2, 4, rows, layers), f32),
            pltpu.VMEM((EXCHANGES - 1, 2, cols, layers), f32),
            pltpu.VMEM((EXCHANGES - 1, 2, rows, layers), f32),
            pltpu.VMEM((BASIS, 2, cols, layers), f32),
            pltpu.VMEM((EXCHANGES - 1, 2, rows, layers), f32),
            pltpu.VMEM((7, 1, 128), f32),
            pltpu.VMEM((9, 1, 128), f32),
            pltpu.VMEM((RING, 1, 128), f32),
            pltpu.VMEM((n_gx, 1, 128), f32),
            pltpu.VMEM((n_gy // RING, 1, 128), f32),
            pltpu.VMEM((RING, 1, 128), f32),
            pltpu.VMEM((plane, 1, 128), f32),
            pltpu.VMEM((RING, 1, 128), f32),
            dma((4,)),
            dma((1 + BASIS,)),
            dma((4,)),
            dma((2, 4)),
            dma((4,)),
            dma((4,)),
            dma((7,)),
            dma((7,)),
        ]
        operands = (
            jnp.swapaxes(inject_cells, 1, 2),
            inject_rate,
            jnp.swapaxes(produce_cells, 1, 2),
            produce_pressure,
            perm_table,
            poro_table,
            inject_index,
            produce_index,
            rock_type.reshape(flat),
            saturation.reshape(flat),
            pressure_old.reshape(flat),
            factor_inverse.reshape(blocks, layers, layers),
        )
        satn, z0, z1, z2, coef = pl.pallas_call(
            functools.partial(kernel, (rows, cols, layers, n_gx, n_gy)),
            out_shape=[
                *[jax.ShapeDtypeStruct(flat, f32)] * (1 + BASIS),
                jax.ShapeDtypeStruct((BASIS, layers), f32),
            ],
            in_specs=[smem] * 6 + [vmem] * 2 + [hbm] * 4,
            out_specs=[out] * (1 + BASIS) + [vmem],
            scratch_shapes=scratch,
            compiler_params=pltpu.CompilerParams(
                collective_id=0, has_side_effects=True, vmem_limit_bytes=24 * 1024 * 1024
            ),
            name="reservoir_step",
        )(*(pltpu.with_memory_space_constraint(a, pltpu.HBM) for a in operands))
        satn, pressure = pl.pallas_call(
            closing,
            out_shape=[jax.ShapeDtypeStruct(flat, f32)] * 2,
            in_specs=[vmem] * 5 + [out],
            out_specs=[hbm] * 2,
            scratch_shapes=[field, dma((CHUNKS + 1,))],
            compiler_params=pltpu.CompilerParams(vmem_limit_bytes=8 * 1024 * 1024),
            name="reservoir_close",
        )(coef, pressure_old.reshape(flat), z0, z1, z2, satn)
        return satn.reshape(saturation.shape), pressure.reshape(saturation.shape)

    grid = P("gx", "gy", None)
    in_specs = (grid, P(), P(), grid, grid, P("gx", "gy", None, None)) + (P(),) * 6
    return jax.shard_map(
        per_device, mesh=mesh, in_specs=in_specs, out_specs=(grid, grid), check_vma=False
    )
```

```python
import functools

import jax
import jax.numpy as jnp
from jax import lax
from jax.experimental import pallas as pl
from jax.experimental.pallas import tpu as pltpu
from jax.sharding import PartitionSpec as P

MESH = pl.DeviceIdType.MESH
BLOCK = 16
BASIS = 3
UNROLL = 8
CHUNKS = 4
RING = 8
TIME_STEP = 0.002
SHIFT = 2.0**-14

INPUT, MOVED, BASE = 0, 1, 2
EXCHANGES = BASE + BASIS
SAT, PRS, PERM, DTP = 0, 1, 2, 3
LO_X, HI_X, LO_Y, HI_Y = 0, 1, 2, 3
FAR_X = (4, 3, 5, 2, 6, 1, 7)
FAR_Y = (2, 1, 3)
FAR_Z = (4, 3, 5, 2, 6, 1, 7)


def harmonic(former, latter):
    return 2.0 * former * latter / (former + latter)


def upwind(face, p_a, p_b, f_a, f_b):
    flow = face * (p_a - p_b)
    return flow * jnp.where(flow > 0.0, f_a, f_b)


def kernel(
    sizes,
    inj_cell,
    inj_rate,
    pro_cell,
    pro_pressure,
    perm_table,
    poro_table,
    inj_index,
    pro_index,
    rock_hbm,
    sat_hbm,
    prs_hbm,
    fac_hbm,
    satn_out,
    z0_out,
    z1_out,
    z2_out,
    coef_out,
    inp,
    rock,
    fac,
    prod_hi,
    prod_lo,
    poro,
    frac,
    mob,
    select,
    spots,
    face_x,
    face_y,
    face_z,
    low_x,
    high_x,
    side_y,
    moved,
    well_d,
    well_e,
    source,
    satn,
    total,
    diag,
    resid,
    base,
    image,
    input_x,
    input_y,
    input_pack,
    halo_x,
    halo_y,
    pack_x,
    pack_y,
    own,
    slot_w,
    slot_v,
    slot_x,
    slot_y,
    slot_s,
    slot_a,
    slot_b,
    load_sem,
    store_sem,
    face_send,
    face_recv,
    late_send,
    late_recv,
    group_send,
    group_recv,
):
    rows, cols, layers, n_gx, n_gy = sizes
    blocks = cols // BLOCK
    cells = rows * cols
    full_cols = cols * n_gy
    n_y = n_gy // RING
    plane = n_gx * n_y
    injectors = inj_index.shape[0]
    producers = pro_index.shape[0]
    perfs = inj_index.shape[1]
    sat, prs, perm, dtp = (inp.at[i] for i in range(4))

    gx = lax.axis_index("gx")
    gy = lax.axis_index("gy")
    yy = gy // RING
    zz = gy % RING
    spot_a = gx * n_y + yy

    def row(x):
        return pl.ds(pl.multiple_of(x * cols, cols), cols)

    def take(ref, c):
        parts = [ref[pl.ds(x * cols + c, 1), :] for x in range(rows)]
        return jnp.concatenate(parts, axis=0)

    def put(ref, c, value):
        for x in range(rows):
            ref[pl.ds(x * cols + c, 1), :] = value[x : x + 1]

    neighbours = (
        (lax.rem(gx + n_gx - 1, n_gx), gy),
        (lax.rem(gx + 1, n_gx), gy),
        (gx, lax.rem(gy + n_gy - 1, n_gy)),
        (gx, lax.rem(gy + 1, n_gy)),
    )
    sends = (gx > 0, gx < n_gx - 1, gy > 0, gy < n_gy - 1)
    hears = (gx < n_gx - 1, gx > 0, gy < n_gy - 1, gy > 0)

    def near(a, b, c=0):
        y = lax.rem(yy + b, n_y) if b else yy
        z = lax.rem(zz + c, RING) if c else zz
        return (lax.rem(gx + a, n_gx) if a else gx, y * RING + z)

    around_peers = [
        near(a, b) for a in (n_gx - 1, 1, 0) for b in (n_y - 1, 1, 0) if a or b
    ]
    x_peers = [near(a, 0) for a in FAR_X]
    y_peers = [near(0, b) for b in FAR_Y]
    z_peers = [near(0, 0, c) for c in FAR_Z]
    plane_peers = [near(a, b) for a in FAR_X + (0,) for b in FAR_Y + (0,) if a or b]

    def each_row(body, carry=None):
        def step(i, kept):
            for j in range(UNROLL):
                kept = body(i * UNROLL + j, kept)
            return kept

        if carry is None:
            pl.loop(0, rows // UNROLL)(lambda i: step(i, None) and None)
        else:
            carry = lax.fori_loop(0, rows // UNROLL, step, carry)
        return carry

    def split(v):
        high = v.astype(jnp.bfloat16)
        return high, (v - high.astype(jnp.float32)).astype(jnp.bfloat16)

    def product(a, b, dims):
        return lax.dot_general(a, b, (dims, ((), ())), preferred_element_type=jnp.float32)

    loads = [
        pltpu.make_async_copy(src, dst, load_sem.at[i])
        for i, (src, dst) in enumerate(
            ((sat_hbm, sat), (rock_hbm, rock), (prs_hbm, prs), (fac_hbm, fac))
        )
    ]
    for load in loads:
        load.start()

    barrier = pltpu.get_barrier_semaphore()

    def greet(peer):
        pl.semaphore_signal(barrier, inc=1, device_id=peer, device_id_type=MESH)

    for peer in neighbours[2:] + tuple(plane_peers[::-1]) + tuple(z_peers[::-1]):
        greet(peer)

    def clear_x(at):
        input_x[at] = jnp.zeros(input_x.shape[1:], jnp.float32)
        for e in range(EXCHANGES - 1):
            halo_x[e, at] = jnp.zeros(halo_x.shape[2:], jnp.float32)

    def clear_y(at):
        input_y[at] = jnp.zeros(input_y.shape[1:], jnp.float32)
        for e in range(EXCHANGES - 1):
            halo_y[e, at] = jnp.zeros(halo_y.shape[2:], jnp.float32)

    pl.when(gx == 0)(lambda: clear_x(0))
    pl.when(gx == n_gx - 1)(lambda: clear_x(1))
    pl.when(gy == 0)(lambda: clear_y(0))
    pl.when(gy == n_gy - 1)(lambda: clear_y(1))

    def lookup(kind, table):
        bit0 = (kind & 1) == 1
        bit1 = (kind & 2) == 2
        pairs = [jnp.where(bit0, table[2 * i + 1], table[2 * i]) for i in range(4)]
        high = jnp.where(bit1, pairs[3], pairs[2])
        return jnp.where(kind >= 4, high, jnp.where(bit1, pairs[1], pairs[0]))

    def fill_row(x, _=None):
        kind = rock[row(x), :]
        perm[row(x), :] = lookup(kind, perm_table)
        porosity = lookup(kind, poro_table)
        poro[row(x), :] = porosity
        dtp[row(x), :] = TIME_STEP / porosity

    loads[1].wait()
    for i, c in ((0, 0), (1, cols - 1)):
        kind = take(rock, c)
        input_pack[i, PERM] = lookup(kind, perm_table)
        input_pack[i, DTP] = TIME_STEP / lookup(kind, poro_table)
    fill_row(0)
    fill_row(rows - 1)
    loads[0].wait()
    loads[2].wait()
    for i, c in ((0, 0), (1, cols - 1)):
        input_pack[i, SAT] = take(sat, c)
        input_pack[i, PRS] = take(prs, c)

    def face_copy(e, d):
        if e == INPUT:
            soon = pl.ds(0, DTP)
            if d < 2:
                src = inp.at[soon, pl.ds(0 if d == LO_X else cells - cols, cols), :]
                dst = input_x.at[1 - d, soon]
            else:
                src, dst = input_pack.at[d - 2, soon], input_y.at[3 - d, soon]
        else:
            if d < 2:
                at = pl.ds(0 if d == LO_X else cells - cols, cols)
                src = moved.at[at, :] if e == MOVED else pack_x.at[e - BASE, d]
                dst = halo_x.at[e - 1, 1 - d]
            else:
                src, dst = pack_y.at[e - 1, d - 2], halo_y.at[e - 1, 3 - d]
        return pltpu.make_async_remote_copy(
            src_ref=src,
            dst_ref=dst,
            send_sem=face_send.at[d],
            recv_sem=face_recv.at[e % 2, d],
            device_id=neighbours[d],
            device_id_type=MESH,
        )

    def send_faces(e):
        for d in (LO_Y, HI_Y, LO_X, HI_X):

            @pl.when(sends[d])
            def _():
                if e > 0:
                    face_copy(e - 1, d).wait_send()
                face_copy(e, d).start()

    def take_faces(e):
        for d in range(4):
            pl.when(hears[d])(lambda: face_copy(e, d).wait_recv())

    def late_copy(d):
        if d < 2:
            src = dtp.at[pl.ds(0 if d == LO_X else cells - cols, cols), :]
            dst = input_x.at[1 - d, DTP]
        else:
            src, dst = input_pack.at[d - 2, DTP], input_y.at[3 - d, DTP]
        return pltpu.make_async_remote_copy(
            src_ref=src,
            dst_ref=dst,
            send_sem=late_send.at[d],
            recv_sem=late_recv.at[d],
            device_id=neighbours[d],
            device_id_type=MESH,
        )

    class Group:
        def __init__(self, k, peers, slots):
            self.k, self.peers, self.slots = k, peers, slots

        def copy(self, src, dst, peer):
            return pltpu.make_async_remote_copy(
                src_ref=src,
                dst_ref=dst,
                send_sem=group_send.at[self.k],
                recv_sem=group_recv.at[self.k],
                device_id=peer,
                device_id_type=MESH,
            )

        def start(self, src):
            for i, peer in enumerate(self.peers):
                self.copy(src, self.slots.at[i], peer).start()

        def whole(self):
            held = self.slots.at[pl.ds(0, len(self.peers))]
            return self.copy(held, held, self.peers[0])

        def take(self, mine):
            self.whole().wait_recv()
            self.slots[len(self.peers)] = mine
            return self.slots[...]

    well_z = Group(0, z_peers, slot_v)
    well_xy = Group(6, around_peers, slot_w)
    scale_x = Group(1, x_peers, slot_x)
    scale_y = Group(2, y_peers, slot_y)
    scale_z = Group(3, z_peers, slot_s)
    sum_plane = Group(4, plane_peers, slot_a)
    sum_z = Group(5, z_peers, slot_b)
    groups = (well_z, well_xy, scale_x, scale_y, scale_z, sum_plane, sum_z)

    pl.semaphore_wait(barrier, 2 + len(plane_peers) + len(z_peers))
    send_faces(INPUT)
    for d in range(4):
        pl.when(sends[d])(lambda: late_copy(d).start())

    lane = lax.broadcasted_iota(jnp.int32, (1, 128), 1)
    well_row = jnp.full((1, 128), -9, jnp.int32)
    well_layer = jnp.full((1, 128), -9, jnp.int32)
    pressure_row = jnp.zeros((1, 128), jnp.float32)
    rate_row = jnp.zeros((1, 128), jnp.float32)
    wide = cols + 16
    spread = lax.broadcasted_iota(jnp.int32, (wide, perfs), 0) - lax.broadcasted_iota(
        jnp.int32, (wide, perfs), 1
    )
    lane_wide = lax.broadcasted_iota(jnp.int32, (wide, 128), 1)
    column = jnp.zeros((wide, 128), jnp.float32)
    for w in range(producers + injectors):
        produces = w < producers
        cell_ref = pro_cell if produces else inj_cell
        index_ref = pro_index if produces else inj_index
        i = w if produces else w - producers
        cell = cell_ref[i, 0, 0]
        well_row = jnp.where(lane == w, cell // full_cols - gx * rows, well_row)
        well_layer = jnp.where(lane == w, cell_ref[i, 1, 0], well_layer)
        start = cell % full_cols
        offset = spread + (gy * cols - 8 - start)
        hit = jnp.where(
            (offset == 0) | (offset == full_cols) | (offset == -full_cols),
            index_ref[i : i + 1, :],
            0.0,
        )
        column = jnp.where(lane_wide == w, jnp.sum(hit, axis=1, keepdims=True), column)
        if produces:
            pressure_row = jnp.where(lane == w, pro_pressure[i], pressure_row)
        else:
            rate_row = jnp.where(lane == w, inj_rate[i], rate_row)
    is_producer = jnp.where(lane < producers, 1.0, 0.0)
    layer_pos = lax.broadcasted_iota(jnp.int32, (layers, 128), 0)
    spots[...] = jnp.where(layer_pos == well_layer, 1.0, 0.0).astype(jnp.bfloat16)
    own_column = column[8 : 8 + cols]
    for x in range(rows):
        select[x * cols : (x + 1) * cols, :] = jnp.where(well_row == x, own_column, 0.0)
    select[cells : cells + cols, :] = jnp.where(well_row == -1, own_column, 0.0)
    select[cells + cols : cells + 2 * cols, :] = jnp.where(well_row == rows, own_column, 0.0)
    row_pos = lax.broadcasted_iota(jnp.int32, (rows, 128), 0)
    rim_y = cells + 2 * cols
    select[rim_y : rim_y + rows, :] = jnp.where(row_pos == well_row, column[7:8], 0.0)
    select[rim_y + rows : rim_y + 2 * rows, :] = jnp.where(
        row_pos == well_row, column[8 + cols : 9 + cols], 0.0
    )


    def mobility(s):
        water = 2.0 * s * s
        rest = 1.0 - s
        return water, water + rest * rest

    def mobility_row(x, _):
        water, t = mobility(sat[row(x), :])
        mob[row(x), :] = t
        frac[row(x), :] = water / t

    each_row(mobility_row)
    spot = spots[...]
    lane_spot = lax.broadcasted_iota(jnp.int32, (layers, 128), 1)
    picked = sum(product(v, spot, ((1,), (0,))) for v in split(mob[...]))
    own[0] = jnp.sum(picked * select[pl.ds(0, cells), :], axis=0, keepdims=True)
    well_z.start(own.at[0])

    lane_z = lax.broadcasted_iota(jnp.int32, (cols, layers), 1)
    col_y = lax.broadcasted_iota(jnp.int32, (cols, layers), 0)
    inner_z = lane_z < layers - 1
    inner_y = col_y < cols - 1

    def next_y(v):
        return pltpu.roll(v, cols - 1, 0)

    def last_y(v):
        return pltpu.roll(v, 1, 0)

    def next_z(v):
        return pltpu.roll(v, layers - 1, 1)

    def last_z(v):
        return pltpu.roll(v, 1, 1)

    def place(chosen):
        return sum(product(v, spot, ((1,), (1,))) for v in split(chosen))

    loads[3].wait()
    largest = jnp.zeros((1, 128), jnp.float32)
    for b in range(blocks):
        lower = fac[b]
        high, low = split(lower)
        over = ((0,), (0,))
        gram = product(high, high, over) + product(high, low, over) + product(low, high, over)
        prod_hi[b], prod_lo[b] = split(gram)
        row_sum = jnp.sum(jnp.abs(gram), axis=0, keepdims=True)
        largest = jnp.maximum(largest, jnp.max(row_sum, axis=1, keepdims=True))
    own[1] = largest
    scale_x.start(own.at[1])

    for x in range(1, rows - 1):
        fill_row(x)
    chosen = select[pl.ds(0, cells), :]
    well_d[...] = place(chosen * is_producer)
    well_e[...] = place(chosen * pressure_row)

    zero_row = jnp.zeros((cols, layers), jnp.float32)

    def flux_row(x, flux_last):
        here, there = row(x), row(jnp.minimum(x + 1, rows - 1))
        k, p, f = perm[here, :], prs[here, :], frac[here, :]
        kx, px, fx = perm[there, :], prs[there, :], frac[there, :]
        tx = harmonic(k, kx)
        ty = jnp.where(inner_y, harmonic(k, next_y(k)), 0.0)
        tz = jnp.where(inner_z, 0.1 * harmonic(k, next_z(k)), 0.0)
        face_x[here, :] = tx
        face_y[here, :] = ty
        face_z[here, :] = tz
        wx = upwind(tx, p, px, f, fx)
        wy = upwind(ty, p, next_y(p), f, next_y(f))
        wz = upwind(tz, p, next_z(p), f, next_z(f))
        s = sat[here, :]
        made = 2.0 * s * s * (p * well_d[here, :] - well_e[here, :])
        moved[here, :] = s - dtp[here, :] * (
            made + (wx - flux_last) + (wy - last_y(wy)) + (wz - last_z(wz))
        )
        return wx

    each_row(flux_row, zero_row)

    def fraction(s):
        water, t = mobility(s)
        return water / t

    first, final = pl.ds(0, cols), pl.ds(cells - cols, cols)
    take_faces(INPUT)
    t = harmonic(input_x[0, PERM], perm[first, :])
    low_x[...] = t
    moved[first, :] += dtp[first, :] * upwind(
        t, input_x[0, PRS], prs[first, :], fraction(input_x[0, SAT]), frac[first, :]
    )
    t = harmonic(perm[final, :], input_x[1, PERM])
    high_x[...] = t
    moved[final, :] -= dtp[final, :] * upwind(
        t, prs[final, :], input_x[1, PRS], frac[final, :], fraction(input_x[1, SAT])
    )
    pack, rim = input_pack, input_y
    t = harmonic(rim[0, PERM], pack[0, PERM])
    side_y[0] = t
    flux = upwind(t, rim[0, PRS], pack[0, PRS], fraction(rim[0, SAT]), fraction(pack[0, SAT]))
    rims = [take(moved, 0) + pack[0, DTP] * flux]
    t = harmonic(pack[1, PERM], rim[1, PERM])
    side_y[1] = t
    flux = upwind(t, pack[1, PRS], rim[1, PRS], fraction(pack[1, SAT]), fraction(rim[1, SAT]))
    rims.append(take(moved, cols - 1) - pack[1, DTP] * flux)
    for i, c in ((0, 0), (1, cols - 1)):
        pack_y[MOVED - 1, i] = rims[i]
        put(moved, c, rims[i])
    send_faces(MOVED)
    own[3] = jnp.sum(well_z.take(own[0]), axis=0)
    well_xy.start(own.at[3])
    own[2] = jnp.max(scale_x.take(own[1]), axis=0)
    scale_y.start(own.at[2])

    chosen = split(select[...])
    for w in range(injectors):
        alone = jnp.where(lane_spot == producers + w, spot, jnp.zeros_like(spot))
        source[w] = sum(product(v, alone, ((1,), (1,))) for v in chosen)

    sums = jnp.sum(well_xy.take(own[3]), axis=0)
    scale = jnp.where(sums > 0.0, rate_row / jnp.where(sums > 0.0, sums, 1.0), 0.0)
    shares = [scale[:, producers + w : producers + w + 1] for w in range(injectors)]

    def weights(at):
        return sum(share * source[w, at, :] for w, share in enumerate(shares))


    def moved_row(x, _):
        here = row(x)
        made = mob[here, :] * weights(here)
        s = moved[here, :] + dtp[here, :] * made
        satn[here, :] = s
        resid[here, :] = made
        total[here, :] = mobility(s)[1]

    each_row(moved_row)

    store_satn = pltpu.make_async_copy(satn, satn_out, store_sem.at[0])
    store_satn.start()

    def residual_row(x, flux_last):
        here, there = row(x), row(jnp.minimum(x + 1, rows - 1))
        t, tx = total[here, :], total[there, :]
        p, px = prs[here, :], prs[there, :]
        cx = face_x[here, :] * (0.5 * (t + tx))
        cy = face_y[here, :] * (0.5 * (t + next_y(t)))
        cz = face_z[here, :] * (0.5 * (t + next_z(t)))
        face_x[here, :] = cx
        face_y[here, :] = cy
        face_z[here, :] = cz
        d, e = well_d[here, :], well_e[here, :]
        diag[here, :] = poro[here, :] + d * t
        fx = cx * (p - px)
        fy = cy * (p - next_y(p))
        fz = cz * (p - next_z(p))
        resid[here, :] = (
            resid[here, :]
            + t * (e - d * p)
            - ((fx - flux_last) + (fy - last_y(fy)) + (fz - last_z(fz)))
        )
        return fx

    each_row(residual_row, zero_row)

    own[4] = jnp.max(scale_y.take(own[2]), axis=0)
    scale_z.start(own.at[4])

    def rim_total(before, sat_rim, dtp_rim, weight):
        s = before + dtp_rim * (mobility(sat_rim)[1] * weight)
        return mobility(s)[1]

    pack_total = [take(total, 0), take(total, cols - 1)]
    edge = []
    take_faces(MOVED)
    for d in range(4):
        pl.when(hears[d])(lambda: late_copy(d).wait_recv())
    t = rim_total(
        halo_x[MOVED - 1, 0], input_x[0, SAT], input_x[0, DTP], weights(pl.ds(cells, cols))
    )
    c = low_x[...] * (0.5 * (total[first, :] + t))
    low_x[...] = c
    resid[first, :] -= c * (prs[first, :] - input_x[0, PRS])
    t = rim_total(
        halo_x[MOVED - 1, 1],
        input_x[1, SAT],
        input_x[1, DTP],
        weights(pl.ds(cells + cols, cols)),
    )
    c = high_x[...] * (0.5 * (total[final, :] + t))
    high_x[...] = c
    resid[final, :] -= c * (prs[final, :] - input_x[1, PRS])
    for i, at in ((0, 0), (1, cols - 1)):
        t = rim_total(
            halo_y[MOVED - 1, i],
            rim[i, SAT],
            rim[i, DTP],
            weights(pl.ds(rim_y + i * rows, rows)),
        )
        c = side_y[i] * (0.5 * (pack_total[i] + t))
        side_y[i] = c
        edge.append(take(resid, at) - c * (pack[i, PRS] - rim[i, PRS]))
        put(resid, at, edge[i])

    def apply(v, b, factor):
        high, low = split(v if factor is None else v * factor)
        z = jnp.dot(high, prod_hi[b], preferred_element_type=jnp.float32)
        z += jnp.dot(high, prod_lo[b], preferred_element_type=jnp.float32)
        return z + jnp.dot(low, prod_hi[b], preferred_element_type=jnp.float32)

    def precondition(src, dst, factor):
        for b in range(blocks):
            parts = [
                src[pl.ds(x * cols + b * BLOCK, BLOCK), :] for x in range(rows)
            ]
            z = apply(jnp.concatenate(parts, axis=0), b, factor)
            for x in range(rows):
                dst[pl.ds(x * cols + b * BLOCK, BLOCK), :] = z[x * BLOCK : (x + 1) * BLOCK]

    def precondition_rim(k, src, low_column, high_column, factor):
        for b in range(blocks):
            here = pl.ds(b * BLOCK, BLOCK)
            parts = [src[here, :], src[pl.ds(cells - cols + b * BLOCK, BLOCK), :]]
            if b == 0:
                parts.append(low_column)
            if b == blocks - 1:
                parts.append(high_column)
            z = apply(jnp.concatenate(parts, axis=0), b, factor)
            pack_x[k, 0, here, :] = z[:BLOCK]
            pack_x[k, 1, here, :] = z[BLOCK : 2 * BLOCK]
            if b == 0:
                pack_y[BASE - 1 + k, 0] = z[2 * BLOCK : 2 * BLOCK + rows]
            if b == blocks - 1:
                pack_y[BASE - 1 + k, 1] = z[-rows:]

    pairs = [(0, 0), (1, 0), (1, 1), (2, 0), (2, 1), (2, 2)]
    count = len(pairs) + BASIS
    last = len(pairs) - 1

    def fold(total_, term):
        for i in range(term.shape[0] // 8):
            total_ = total_ + term[8 * i : 8 * i + 8]
        return total_

    def dots_row(x, sums):
        here = row(x)
        v = [base[k, here, :] for k in range(BASIS)]
        u = [image[k, here, :] for k in range(BASIS)]
        r = resid[here, :]
        terms = [v[i] * u[j] for i, j in pairs] + [v[i] * r for i in range(BASIS)]
        return tuple(fold(s, term) for s, term in zip(sums, terms))

    def into_lane(i, s, message):
        s = jnp.sum(s, axis=0, keepdims=True)
        return jnp.where(lane == i, jnp.sum(s, axis=1, keepdims=True), message)

    stores = [store_satn]
    for k in range(BASIS):
        e = BASE + k
        vec, img = base.at[k], image.at[k]
        if k == 1:
            top = jnp.max(scale_z.take(own[4]), axis=0)
            norm = jnp.concatenate([1.0 / top] * (layers // 128), axis=1)
        factor = (lambda: None, lambda: (SHIFT * norm) * norm, lambda: SHIFT * norm)[k]()
        prior = resid if k == 0 else image.at[k - 1]
        precondition_rim(k, prior, edge[0], edge[1], factor)
        send_faces(e)
        precondition(prior, vec, factor)
        store = pltpu.make_async_copy(
            vec, (z0_out, z1_out, z2_out)[k], store_sem.at[1 + k]
        )
        store.start()
        stores.append(store)

        def image_row(x, flux_last, vec=vec, img=img):
            here, there = row(x), row(jnp.minimum(x + 1, rows - 1))
            v, vx = vec[here, :], vec[there, :]
            fx = face_x[here, :] * (v - vx)
            fy = face_y[here, :] * (v - next_y(v))
            fz = face_z[here, :] * (v - next_z(v))
            img[here, :] = (
                diag[here, :] * v
                + (fx - flux_last)
                + (fy - last_y(fy))
                + (fz - last_z(fz))
            )
            return fx

        each_row(image_row, zero_row)
        h = e - 1
        if k < BASIS - 1:
            take_faces(e)
            img[first, :] += low_x[...] * (vec[first, :] - halo_x[h, 0])
            img[final, :] += high_x[...] * (vec[final, :] - halo_x[h, 1])
            for i, at in ((0, 0), (1, cols - 1)):
                edge[i] = take(img, at) + side_y[i] * (pack_y[h, i] - halo_y[h, i])
                put(img, at, edge[i])
            continue
        sums = each_row(dots_row, (jnp.zeros((8, layers), jnp.float32),) * count)
        message = jnp.zeros((1, 128), jnp.float32)
        for i, s in enumerate(sums):
            if i != last:
                message = into_lane(i, s, message)
        take_faces(e)
        s = fold(sums[last], low_x[...] * (vec[first, :] - halo_x[h, 0]) * vec[first, :])
        s = fold(s, high_x[...] * (vec[final, :] - halo_x[h, 1]) * vec[final, :])
        for i in range(2):
            s = fold(s, side_y[i] * (pack_y[h, i] - halo_y[h, i]) * pack_y[h, i])
        message = into_lane(last, s, message)

    own[5] = message
    sum_plane.start(own.at[5])
    own[6] = jnp.sum(sum_plane.take(own[5]), axis=0)
    sum_z.start(own.at[6])
    result = jnp.sum(sum_z.take(own[6]), axis=0)
    val = [result[:, i : i + 1] for i in range(count)]
    g00, g10, g11, g20, g21, g22, b0, b1, b2 = val

    def ratio(a, b):
        good = b > 0.0
        return jnp.where(good, a / jnp.where(good, b, 1.0), 0.0)

    l10, l20 = ratio(g10, g00), ratio(g20, g00)
    d1 = g11 - l10 * g10
    e21 = g21 - l20 * g10
    l21 = ratio(e21, d1)
    d2 = g22 - l20 * g20 - l21 * e21
    y1 = b1 - l10 * b0
    y2 = b2 - l20 * b0 - l21 * y1
    c2 = ratio(y2, d2)
    c1 = ratio(y1, d1) - l21 * c2
    c0 = ratio(b0, g00) - l10 * c1 - l20 * c2
    for k, c in enumerate((c0, c1, c2)):
        coef_out[k : k + 1, :] = jnp.broadcast_to(c, (1, layers))

    for group in groups:
        group.whole().wait_send()
    for d in range(4):
        pl.when(sends[d])(lambda: face_copy(EXCHANGES - 1, d).wait_send())
        pl.when(sends[d])(lambda: late_copy(d).wait_send())
    for store in stores:
        store.wait()


def closing(coef, prs, z0, z1, z2, satn, satn_out, out, result, sems):
    stores = [pltpu.make_async_copy(satn, satn_out, sems.at[CHUNKS])]
    stores[0].start()
    size = prs.shape[0] // CHUNKS
    for i in range(CHUNKS):
        at = pl.ds(i * size, size)
        result[at, :] = prs[at, :] + (
            coef[0:1, :] * z0[at, :] + coef[1:2, :] * z1[at, :] + coef[2:3, :] * z2[at, :]
        )
        store = pltpu.make_async_copy(result.at[at], out.at[at], sems.at[i])
        store.start()
        stores.append(store)
    for store in stores:
        store.wait()


def solution(mesh):
    n_gx, n_gy = mesh.shape["gx"], mesh.shape["gy"]

    def per_device(
        rock_type,
        perm_table,
        poro_table,
        saturation,
        pressure_old,
        factor_inverse,
        inject_cells,
        inject_index,
        inject_rate,
        produce_cells,
        produce_index,
        produce_pressure,
    ):
        rows, cols, layers = saturation.shape
        cells = rows * cols
        blocks = cols // BLOCK
        f32, bf16 = jnp.float32, jnp.bfloat16
        flat = (cells, layers)
        field = pltpu.VMEM(flat, f32)
        smem = pl.BlockSpec(memory_space=pltpu.SMEM)
        vmem = pl.BlockSpec(memory_space=pltpu.VMEM)
        hbm = pl.BlockSpec(memory_space=pltpu.HBM)
        out = pl.BlockSpec(memory_space=pl.ANY)
        plane = n_gx * (n_gy // RING)
        dma = pltpu.SemaphoreType.DMA
        scratch = [
            pltpu.VMEM((4,) + flat, f32),
            pltpu.VMEM(flat, jnp.int32),
            pltpu.VMEM((blocks, layers, layers), f32),
            pltpu.VMEM((blocks, layers, layers), bf16),
            pltpu.VMEM((blocks, layers, layers), bf16),
            field,
            field,
            field,
            pltpu.VMEM((cells + 2 * cols + 2 * rows, 128), f32),
            pltpu.VMEM((layers, 128), bf16),
            field,
            field,
            field,
            pltpu.VMEM((cols, layers), f32),
            pltpu.VMEM((cols, layers), f32),
            pltpu.VMEM((2, rows, layers), f32),
            field,
            field,
            field,
            pltpu.VMEM(
                (inject_index.shape[0], cells + 2 * cols + 2 * rows, layers), f32
            ),
            field,
            field,
            field,
            field,
            pltpu.VMEM((BASIS,) + flat, f32),
            pltpu.VMEM((BASIS,) + flat, f32),
            pltpu.VMEM((2, 4, cols, layers), f32),
            pltpu.VMEM((2, 4, rows, layers), f32),
            pltpu.VMEM((2, 4, rows, layers), f32),
            pltpu.VMEM((EXCHANGES - 1, 2, cols, layers), f32),
            pltpu.VMEM((EXCHANGES - 1, 2, rows, layers), f32),
            pltpu.VMEM((BASIS, 2, cols, layers), f32),
            pltpu.VMEM((EXCHANGES - 1, 2, rows, layers), f32),
            pltpu.VMEM((7, 1, 128), f32),
            pltpu.VMEM((9, 1, 128), f32),
            pltpu.VMEM((RING, 1, 128), f32),
            pltpu.VMEM((n_gx, 1, 128), f32),
            pltpu.VMEM((n_gy // RING, 1, 128), f32),
            pltpu.VMEM((RING, 1, 128), f32),
            pltpu.VMEM((plane, 1, 128), f32),
            pltpu.VMEM((RING, 1, 128), f32),
            dma((4,)),
            dma((1 + BASIS,)),
            dma((4,)),
            dma((2, 4)),
            dma((4,)),
            dma((4,)),
            dma((7,)),
            dma((7,)),
        ]
        operands = (
            jnp.swapaxes(inject_cells, 1, 2),
            inject_rate,
            jnp.swapaxes(produce_cells, 1, 2),
            produce_pressure,
            perm_table,
            poro_table,
            inject_index,
            produce_index,
            rock_type.reshape(flat),
            saturation.reshape(flat),
            pressure_old.reshape(flat),
            factor_inverse.reshape(blocks, layers, layers),
        )
        satn, z0, z1, z2, coef = pl.pallas_call(
            functools.partial(kernel, (rows, cols, layers, n_gx, n_gy)),
            out_shape=[
                *[jax.ShapeDtypeStruct(flat, f32)] * (1 + BASIS),
                jax.ShapeDtypeStruct((BASIS, layers), f32),
            ],
            in_specs=[smem] * 6 + [vmem] * 2 + [hbm] * 4,
            out_specs=[out] * (1 + BASIS) + [vmem],
            scratch_shapes=scratch,
            compiler_params=pltpu.CompilerParams(
                collective_id=0, has_side_effects=True, vmem_limit_bytes=24 * 1024 * 1024
            ),
            name="reservoir_step",
        )(*(pltpu.with_memory_space_constraint(a, pltpu.HBM) for a in operands))
        satn, pressure = pl.pallas_call(
            closing,
            out_shape=[jax.ShapeDtypeStruct(flat, f32)] * 2,
            in_specs=[vmem] * 5 + [out],
            out_specs=[hbm] * 2,
            scratch_shapes=[field, dma((CHUNKS + 1,))],
            compiler_params=pltpu.CompilerParams(vmem_limit_bytes=8 * 1024 * 1024),
            name="reservoir_close",
        )(coef, pressure_old.reshape(flat), z0, z1, z2, satn)
        return satn.reshape(saturation.shape), pressure.reshape(saturation.shape)

    grid = P("gx", "gy", None)
    in_specs = (grid, P(), P(), grid, grid, P("gx", "gy", None, None)) + (P(),) * 6
    return jax.shard_map(
        per_device, mesh=mesh, in_specs=in_specs, out_specs=(grid, grid), check_vma=False
    )
```
